768 devices in a mesh: group: 3 (over z_hi), cuts: 32 (over y, x), sub: 8 (over z_lo, core).
Axes of the slice: x: 4, y: 8, z: 12 (z_hi: 3, z_lo: 4; z = z_hi * 4 + z_lo), core: 2. Of those that a mesh axis runs over, the one named last changes fastest.
Arguments:
- disp_now: float32 [3, 3, 2048, 1089], P('group', None, ('cuts', 'sub')), may hold values from -6 to 6
- disp_prev: float32 [3, 3, 2048, 1089], P('group', None, ('cuts', 'sub')), may hold values from -6 to 6
- memory_init: float32 [3, 3, 5, 125, 32768], P('group', None, None, None, ('cuts', 'sub')), may hold values from -6 to 6
- density: float32 [2048, 1089], P(('cuts', 'sub')), may hold values from 0.8 to 1.6
- lame_lambda: float32 [125, 32768], P(None, ('cuts', 'sub')), may hold values from 0.4 to 1.6
- shear_mu: float32 [125, 32768], P(None, ('cuts', 'sub')), may hold values from 0.4 to 1.2
- sls_decay: float32 [3, 32768], P(None, ('cuts', 'sub')), may hold values from 0.3 to 0.98
- owner_map: int32 [512, 64, 1], P(('cuts', 'sub')), may hold values from 0 to 7; in each aligned block of 64 rows (0 to 63, 64 to 127, ..., all dimensions but the last counted through in order) at most 16 rows name the same one
Outputs:
- disp_final: float32 [3, 3, 2048, 1089], P('group', None, ('cuts', 'sub'))
- kernels: float32 [3, 65536, 250], P('group', ('cuts', 'sub'))
The draws below stay inside these ranges and needn't reach their ends.
Inputs may be any that keep to these rules, and one draw needn't show every extreme that they name: `owner_map`: among the 64 elements of one slab, no sub-slice owns more than 16; in some slab one owns exactly 16.
All inputs are finite; a program needn't handle non-finite values.
Results may differ from the reference program's by a relative error of at most 0.0004.
The reference program's roundings to bfloat16 on the way (of `kernel_part`) count: a program that leaves them out, or rounds other values in their place, can miss the bound.
Values may be sent and summed in bfloat16 or wider, within the bound.
A program may use at most 64 MiB of HBM per device.

```python
import math
import jax
import jax.numpy as jnp
import numpy as np
from jax import lax

EX = 2
EY = 8
EZ = 8
NODES = 125
N_SLS = 3
STEPS = 3
EYZ = 64
YZ = 1089
ELX = 512
ELEMS = 32768
NXG = 2048
MOST = 16
KROWS = 65536
FIELDS = 3
N_GROUP = 3
N_CUTS = 32
N_SUB = 8


def block_levels(rng, dims, split, smallest, top_value):
    loudness = 1.0
    for axis_at, blocks in split:
        draws = jax.random.uniform(jax.random.fold_in(jax.random.fold_in(rng, 6), axis_at), (blocks,), jnp.float32, smallest / len(split), top_value / len(split))
        loudness = loudness * jnp.repeat(jnp.exp(draws), dims[axis_at] // blocks).reshape((-1,) + (1,) * (len(dims) - 1 - axis_at))
    return loudness


def shared_out(stream_key, own, number, rows, amount, top, reach, slope):
    ranking = jax.random.permutation(stream_key, amount)
    crowded, ordinary = shares(amount, rows * top, reach, slope, True), shares(amount, rows * top, reach, slope, False)
    places = jnp.arange(amount)

    def named(sizes, offset_by):
        used = int((sizes > 0).sum())
        fixed = max(1, used // 4)
        moved = fixed + (places - fixed + offset_by * (used - fixed)) % max(1, amount - fixed)
        return jnp.zeros((amount,), jnp.int32).at[ranking[jnp.where(places < fixed, places, moved)]].set(jnp.asarray(sizes, jnp.int32))

    sizes = jnp.where(number % 4 == 0, named(crowded, number // 4), named(ordinary, number - number // 4 - 1))
    mixed = jax.random.permutation(jax.random.fold_in(own, 3), amount)
    donor, sink = mixed[0:amount // 2 * 2:2], mixed[1:amount // 2 * 2:2]
    slack = jnp.minimum(sizes[donor] - 1, reach - sizes[sink]) // 2
    slack = jnp.where((donor == ranking[0]) | (sink == ranking[0]) | (sizes[sink] == 0), 0, jnp.maximum(slack, 0))
    moved = jax.random.randint(jax.random.fold_in(own, 4), (amount // 2,), 0, 1 << 20) % (slack + 1)
    sizes = sizes.at[donor].add(-moved).at[sink].add(moved)
    items = jnp.searchsorted(jnp.cumsum(sizes), jnp.arange(rows * top), side="right").astype(jnp.int32)
    listing = items.reshape(top, rows).T
    listing = listing[jax.random.permutation(jax.random.fold_in(own, 1), rows)]
    offset_by = jax.random.randint(jax.random.fold_in(own, 2), (rows, 1), 0, top)
    return jnp.take_along_axis(listing, (jnp.arange(top)[None, :] + offset_by) % top, axis=1)


def shares(count, total, reach, slope, full):
    loads = [(1 << 20) // math.isqrt(rank ** slope) + 1 for rank in range(1, count + 1)]
    largest = reach if full else min(reach, max(-(-total // count), total * loads[0] // sum(loads)))
    least = 1 if total - largest >= count - 1 else 0
    counts, spare = [largest] + [least] * (count - 1), total - largest - least * (count - 1)
    while spare > 0:
        free = [i for i in range(1, count) if counts[i] < largest] or [i for i in range(1, count) if counts[i] < reach]
        pool, budget = sum([loads[i] for i in free]), spare
        for i in free:
            more = min(reach - counts[i], max(1, budget * loads[i] // pool), spare)
            counts[i] = counts[i] + more
            spare = spare - more
    return np.array(counts)


def bell_draw(stream_key, dims, spread, reach, shards=(), kind=jnp.bfloat16):
    entries = jax.random.normal(stream_key, dims, jnp.float32) * spread
    if len(shards) > 0:
        entries = block_levels(stream_key, dims, shards, -0.22, 0.18) * entries
    return jnp.clip(entries, min=-reach, max=reach).astype(kind)


def setup_inputs(seed: int = 0) -> dict:
    seeds = jax.random.split(jax.random.key(seed), 9)
    disp_now = bell_draw(seeds[0], (FIELDS, 3, NXG, YZ), 1.0, 6.0, ((0, 3), (2, 256)), jnp.float32)
    disp_prev = bell_draw(seeds[1], (FIELDS, 3, NXG, YZ), 1.0, 6.0, ((0, 3), (2, 256)), jnp.float32)
    memory_init = bell_draw(seeds[2], (FIELDS, N_SLS, 5, NODES, ELEMS), 1.0, 6.0, ((0, 3), (4, 256)), jnp.float32)
    density = jnp.clip(jnp.exp(math.log(1.6) - 0.6931472 * jax.random.uniform(seeds[3], (NXG, YZ), jnp.float32) ** block_levels(seeds[3], (NXG, YZ), ((0, 256),), -0.2, 0.2)), 0.8, 1.6)
    lame_lambda = jnp.clip(jnp.exp(math.log(1.6) - 1.3862944 * jax.random.uniform(seeds[4], (NODES, ELEMS), jnp.float32) ** block_levels(seeds[4], (NODES, ELEMS), ((1, 256),), -0.2, 0.2)), 0.4, 1.6)
    shear_mu = jnp.clip(jnp.exp(math.log(1.2) - 1.0986123 * jax.random.uniform(seeds[5], (NODES, ELEMS), jnp.float32) ** block_levels(seeds[5], (NODES, ELEMS), ((1, 256),), -0.2, 0.2)), 0.4, 1.2)
    sls_decay = jnp.clip(jnp.exp(math.log(0.98) - 1.1837701 * jax.random.uniform(seeds[6], (N_SLS, ELEMS), jnp.float32) ** block_levels(seeds[6], (N_SLS, ELEMS), ((1, 256),), -0.2, 0.2)), 0.3, 0.98)
    owner_map_keys = jax.random.split(jax.random.fold_in(seeds[7], 1), ELX * EYZ // EYZ)
    owner_map_turns = jax.random.permutation(jax.random.fold_in(seeds[7], 3), ELX * EYZ // EYZ)
    owner_map = jax.vmap(lambda own, number: shared_out(jax.random.fold_in(seeds[7], 2), own, number, EYZ, N_SUB, 1, MOST, 2))(owner_map_keys, owner_map_turns).reshape((ELX, EYZ, 1))
    return dict(disp_now=disp_now, disp_prev=disp_prev, memory_init=memory_init, density=density, lame_lambda=lame_lambda, shear_mu=shear_mu, sls_decay=sls_decay, owner_map=owner_map)


time_step = 0.03
step_square = 0.0009
relax_strength = (0.12, 0.08, 0.05)

def gll_tables():
    root_value = math.sqrt(3.0 / 7.0)
    points = [-1.0, -root_value, 0.0, root_value, 1.0]
    weights = [0.1, 49.0 / 90.0, 32.0 / 45.0, 49.0 / 90.0, 0.1]
    derivative = np.zeros((5, 5))
    for p in range(5):
        for a in range(5):
            accum = 0.0
            for m in range(5):
                if m != a:
                    factor = 1.0 / (points[a] - points[m])
                    for k in range(5):
                        if k != a and k != m:
                            factor = factor * (points[p] - points[k]) / (points[a] - points[k])
                    accum = accum + factor
            derivative[p, a] = accum
    return (jnp.asarray(derivative, jnp.float32), jnp.asarray(np.array(weights), jnp.float32))

def split_line(values, elem_count):
    leading = values[..., :4 * elem_count].reshape(values.shape[:-1] + (elem_count, 4))
    trailing = values[..., 4::4]
    return jnp.concatenate([leading, trailing[..., None]], axis=-1)

def join_line(values):
    elem_count = values.shape[-2]
    leading = values[..., :4].reshape(values.shape[:-2] + (4 * elem_count,))
    padding = jnp.zeros(values.shape[:-1] + (3,), values.dtype)
    trailing = jnp.concatenate([padding, values[..., 4:]], axis=-1).reshape(values.shape[:-2] + (4 * elem_count,))
    border = jnp.zeros(values.shape[:-2] + (1,), values.dtype)
    return jnp.concatenate([leading, border], axis=-1) + jnp.concatenate([border, trailing], axis=-1)

def to_elements(extended, count_y, count_z):
    components, layers = (extended.shape[0], extended.shape[1])
    node_grid = extended.reshape(components, layers, 5, 4 * count_y + 1, 4 * count_z + 1)
    along_z = split_line(node_grid, count_z)
    reordered = jnp.transpose(along_z, (0, 1, 2, 4, 5, 3))
    along_y = split_line(reordered, count_y)
    ordered = jnp.transpose(along_y, (0, 2, 6, 4, 1, 5, 3))
    return ordered.reshape(components, 5, 5, 5, layers * count_y * count_z)

def to_nodes(elem_force, layers, count_y, count_z):
    components = elem_force.shape[0]
    shaped = elem_force.reshape(components, 5, 5, 5, layers, count_y, count_z)
    ordered = jnp.transpose(shaped, (0, 4, 1, 6, 3, 5, 2))
    along_y = join_line(ordered)
    reordered = jnp.transpose(along_y, (0, 1, 2, 5, 3, 4))
    along_z = join_line(reordered)
    return along_z.reshape(components, layers, 5, -1)

def strain_parts(elem_disp, derivative):
    highest = lax.Precision.HIGHEST
    grad_x = jnp.einsum('pa,cabde->cpbde', derivative, elem_disp, precision=highest)
    grad_y = jnp.einsum('qb,cabde->caqde', derivative, elem_disp, precision=highest)
    grad_z = jnp.einsum('rd,cabde->cabre', derivative, elem_disp, precision=highest)
    parts = jnp.stack([grad_x[0], grad_y[1], grad_z[2], 0.5 * (grad_y[0] + grad_x[1]), 0.5 * (grad_z[0] + grad_x[2]), 0.5 * (grad_z[1] + grad_y[2])])
    return parts.reshape(6, 125, -1)

def node_weights(count_y, count_z):
    derivative, weights = gll_tables()
    line_y = join_line(jnp.broadcast_to(weights, (count_y, 5)))
    line_z = join_line(jnp.broadcast_to(weights, (count_z, 5)))
    face_weight = (line_y[:, None] * line_z[None, :]).reshape(-1)
    layer_weight = jnp.stack([weights[0] + weights[4], weights[1], weights[2], weights[3]])
    return layer_weight[:, None] * face_weight[None, :]

def element_pass(extended, forward, memory, lame_lambda, shear_mu, sls_decay, count_y, count_z):
    highest = lax.Precision.HIGHEST
    derivative, weights = gll_tables()
    layers = extended.shape[1]
    own_strain = strain_parts(to_elements(extended, count_y, count_z), derivative)
    far_strain = strain_parts(to_elements(forward, count_y, count_z), derivative)
    trace_own = own_strain[0] + own_strain[1] + own_strain[2]
    trace_far = far_strain[0] + far_strain[1] + far_strain[2]
    deviator = jnp.stack([own_strain[0] - trace_own / 3.0, own_strain[1] - trace_own / 3.0, own_strain[3], own_strain[4], own_strain[5]])
    twice_mu = 2.0 * shear_mu
    strengths = jnp.asarray(relax_strength, jnp.float32)[:, None, None, None]
    decay_full = sls_decay[:, None, None, :]
    memory_new = decay_full * memory + (1.0 - decay_full) * strengths * (twice_mu * deviator)[None]
    relax_sum = lax.optimization_barrier(jnp.sum(memory_new, axis=0))
    bulk_part = lame_lambda * trace_own
    sigma_xx = bulk_part + twice_mu * own_strain[0] - relax_sum[0]
    sigma_yy = bulk_part + twice_mu * own_strain[1] - relax_sum[1]
    sigma_zz = bulk_part + twice_mu * own_strain[2] + relax_sum[0] + relax_sum[1]
    sigma_xy = twice_mu * own_strain[3] - relax_sum[2]
    sigma_xz = twice_mu * own_strain[4] - relax_sum[3]
    sigma_yz = twice_mu * own_strain[5] - relax_sum[4]
    weight_cube = (weights[:, None, None] * weights[None, :, None] * weights[None, None, :]).reshape(5, 5, 5, 1)
    stack_x = jnp.stack([sigma_xx, sigma_xy, sigma_xz]).reshape(3, 5, 5, 5, -1) * weight_cube
    stack_y = jnp.stack([sigma_xy, sigma_yy, sigma_yz]).reshape(3, 5, 5, 5, -1) * weight_cube
    stack_z = jnp.stack([sigma_xz, sigma_yz, sigma_zz]).reshape(3, 5, 5, 5, -1) * weight_cube
    elem_force = -(jnp.einsum('pa,cpbde->cabde', derivative, stack_x, precision=highest) + jnp.einsum('qb,caqde->cabde', derivative, stack_y, precision=highest) + jnp.einsum('rd,cabre->cabde', derivative, stack_z, precision=highest))
    kappa = lame_lambda + twice_mu / 3.0
    bulk_kernel = time_step * kappa * trace_far * trace_own
    shear_product = (own_strain[0] - trace_own / 3.0) * (far_strain[0] - trace_far / 3.0) + (own_strain[1] - trace_own / 3.0) * (far_strain[1] - trace_far / 3.0) + (own_strain[2] - trace_own / 3.0) * (far_strain[2] - trace_far / 3.0) + 2.0 * (own_strain[3] * far_strain[3] + own_strain[4] * far_strain[4] + own_strain[5] * far_strain[5])
    shear_kernel = time_step * twice_mu * shear_product
    kernel_part = jnp.stack([bulk_kernel, shear_kernel]).astype(jnp.bfloat16)
    node_force = to_nodes(elem_force.reshape(3, 125, -1), layers, count_y, count_z)
    return (node_force, memory_new, kernel_part)

def reference(disp_now, disp_prev, memory_init, density, lame_lambda, shear_mu, sls_decay, owner_map):
    slab_total = N_CUTS * N_SUB * EX
    block_size = math.gcd(slab_total, 16)
    block_count = slab_total // block_size
    elem_slab = EY * EZ
    lambda_blocks = lame_lambda.reshape(125, block_count, -1).transpose(1, 0, 2)
    mu_blocks = shear_mu.reshape(125, block_count, -1).transpose(1, 0, 2)
    decay_blocks = sls_decay.reshape(N_SLS, block_count, -1).transpose(1, 0, 2)
    node_mass = density.reshape(slab_total, 4, -1) * node_weights(EY, EZ)[None]

    def one_block(items):
        return element_pass(items[0], items[1], items[2], items[3], items[4], items[5], EY, EZ)

    def run_field(field_index, forward_list):
        current = disp_now[field_index].reshape(3, slab_total, 4, -1)
        previous = disp_prev[field_index].reshape(3, slab_total, 4, -1)
        memory = memory_init[field_index].reshape(N_SLS, 5, 125, block_count, -1).transpose(3, 0, 1, 2, 4)
        kernel_sum = jnp.zeros((block_count, 2, 125, block_size * elem_slab), jnp.float32)
        collected = []
        for step_index in range(STEPS):
            extended = jnp.concatenate([current, jnp.roll(current[:, :, 0:1], -1, axis=1)], axis=2)
            if forward_list is None:
                forward_low = lax.optimization_barrier(extended.astype(jnp.bfloat16))
                collected.append(forward_low)
            else:
                forward_low = forward_list[step_index]
            forward = forward_low.astype(jnp.float32)
            ext_blocks = extended.reshape(3, block_count, block_size, 5, -1).transpose(1, 0, 2, 3, 4)
            far_blocks = forward.reshape(3, block_count, block_size, 5, -1).transpose(1, 0, 2, 3, 4)
            force_blocks, memory, kernel_part = lax.map(one_block, (ext_blocks, far_blocks, memory, lambda_blocks, mu_blocks, decay_blocks))
            force_ext = force_blocks.transpose(1, 0, 2, 3, 4).reshape(3, slab_total, 5, -1)
            passed = jnp.roll(force_ext[:, :, 4:5], 1, axis=1)
            zeros_rest = jnp.zeros((3, slab_total, 3, force_ext.shape[-1]), jnp.float32)
            node_force = force_ext[:, :, 0:4] + jnp.concatenate([passed, zeros_rest], axis=2)
            updated = 2.0 * current - previous + step_square * node_force / node_mass
            previous = current
            current = updated
            kernel_sum = kernel_sum + kernel_part.astype(jnp.float32)
        return (current, kernel_sum, collected)
    owners = owner_map[:, :, 0]
    onehot = (owners[:, :, None] == jnp.arange(N_SUB, dtype=jnp.int32)[None, None, :]).astype(jnp.int32)
    rank = lax.optimization_barrier(jnp.sum((jnp.cumsum(onehot, axis=1) - onehot) * onehot, axis=2))
    slab_index = jnp.arange(slab_total, dtype=jnp.int32)[:, None]
    device_slab = slab_index // EX
    local_slab = slab_index % EX
    rows = (device_slab // N_SUB * N_SUB + owners) * (N_SUB * EX * MOST) + device_slab % N_SUB * (EX * MOST) + local_slab * MOST + rank
    rows = rows.reshape(-1).astype(jnp.int32)
    finals = []
    placed_all = []
    forward_list = None
    for field_index in range(N_GROUP):
        final_disp, kernel_sum, collected = run_field(field_index, forward_list)
        if field_index == 0:
            forward_list = collected
        payload = kernel_sum.reshape(block_count, 2, 125, block_size, elem_slab).transpose(0, 3, 4, 1, 2)
        payload = payload.reshape(-1, 250)
        placed = jnp.zeros((KROWS, 250), jnp.float32).at[rows].set(payload)
        finals.append(final_disp.reshape(3, NXG, -1))
        placed_all.append(placed)
    return (jnp.stack(finals), jnp.stack(placed_all))
```

```python
import functools
import math

import jax
import jax.numpy as jnp
import numpy as np
from jax import lax
from jax.experimental import pallas as pl
from jax.experimental.pallas import tpu as pltpu
from jax.sharding import PartitionSpec as P

STEPS = 3
TIME_STEP = 0.03
STEP_SQUARE = 0.0009
RELAX = (0.12, 0.08, 0.05)
F32 = jnp.float32
BF16 = jnp.bfloat16
MESH = pl.DeviceIdType.MESH

BLOCKS = [(b, d) for d in range(5) for b in range(5)]
UROWS = 208
GK = 1280
FROWS = 160


def gll():
    root = math.sqrt(3.0 / 7.0)
    x = [-1.0, -root, 0.0, root, 1.0]
    w = np.array([0.1, 49.0 / 90.0, 32.0 / 45.0, 49.0 / 90.0, 0.1])
    der = np.zeros((5, 5))
    for p in range(5):
        for a in range(5):
            acc = 0.0
            for m in range(5):
                if m != a:
                    fac = 1.0 / (x[a] - x[m])
                    for k in range(5):
                        if k != a and k != m:
                            fac = fac * (x[p] - x[k]) / (x[a] - x[k])
                    acc = acc + fac
            der[p, a] = acc
    return der.astype(np.float32).astype(np.float64), w.astype(np.float32).astype(np.float64)


def pieces(mat, count):
    out = []
    rest = mat.astype(np.float64)
    for _ in range(count):
        part = rest.astype(jnp.bfloat16)
        out.append(part)
        rest = rest - part.astype(np.float64)
    return out


def tables():
    der, w = gll()
    grad = np.zeros((384, UROWS))
    grad_far = np.zeros((384, FROWS))
    force = np.zeros((UROWS, 384))

    def row(a, b, d):
        return (d * 5 + b) * 8 + a

    def row_far(a, b, d):
        return a * 32 + d * 5 + b

    for a in range(5):
        for b in range(5):
            for d in range(5):
                r, rf = row(a, b, d), row_far(a, b, d)
                for p in range(5):
                    for j, q in enumerate(((p, b, d), (a, p, d), (a, b, p))):
                        n = j * 128 + q[0] * 25 + q[1] * 5 + q[2]
                        at = (a, b, d)[j]
                        grad[n, r] = der[p, at]
                        grad_far[n, rf] = der[p, at]
                        force[r, n] = -der[p, at] * w[q[0]] * w[q[1]] * w[q[2]]
    g = pieces(grad, 3)
    gm = np.zeros((384, GK), jnp.bfloat16)
    for i, k in enumerate((0, 0, 0, 1, 1, 2)):
        gm[:, i * UROWS : (i + 1) * UROWS] = g[k]
    gf = np.concatenate(pieces(grad_far, 3), axis=1)
    f = pieces(force, 3)
    fm = np.concatenate([f[k] for k in (0, 0, 0, 1, 1, 2)], axis=1)
    weight = np.ones((UROWS, 128))
    for a in range(5):
        for b in range(5):
            for d in range(5):
                for e in range(128):
                    ey, ez = (e // 8) % 8, e % 8
                    wx = w[0] + w[4] if a in (0, 4) else w[a]
                    wy = w[b] + (w[0] if (b == 4 and ey < 7) or (b == 0 and ey > 0) else 0.0)
                    wz = w[d] + (w[0] if (d == 4 and ez < 7) or (d == 0 and ez > 0) else 0.0)
                    weight[row(a, b, d), e] = wx * wy * wz
    return gm, gf, fm, (weight / STEP_SQUARE).astype(np.float32)


def split3(x):
    x1 = x.astype(BF16)
    r1 = x - x1.astype(F32)
    x2 = r1.astype(BF16)
    x3 = (r1 - x2.astype(F32)).astype(BF16)
    return x1, x2, x3


def kernel(
    gm_ref, gf_ref, fm_ref, wt_ref,
    now_ref, prev_ref, mem_ref, dens_ref, lam_ref, mu_ref, dec_ref, own_ref,
    disp_ref, ker_ref,
    raw, tee, cur, pre, inv, urhs, grad, srhs, force, mem, far, frhs, fgrad, kb, ks, sel,
    halo_out, halo_in, face_out, face_left, face_right, parts_out, parts_in,
    halo_sem, face_send, face_recv, far_send, far_recv, part_send, part_recv,
):
    group = lax.axis_index("group")
    cuts = lax.axis_index("cuts")
    sub = lax.axis_index("sub")
    flat = cuts * 8 + sub
    ring = lax.axis_size("cuts") * 8
    nxt = lax.rem(flat + 1, ring)
    prv = lax.rem(flat + ring - 1, ring)
    right = (group, lax.div(nxt, 8), lax.rem(nxt, 8))
    left = (group, lax.div(prv, 8), lax.rem(prv, 8))

    barrier = pltpu.get_barrier_semaphore()
    for dev in (left, right):
        pl.semaphore_signal(barrier, inc=1, device_id=dev, device_id_type=MESH)
    for k in range(1, 3):
        pl.semaphore_signal(
            barrier, inc=1, device_id=(lax.rem(group + k, 3), cuts, sub), device_id_type=MESH
        )
    for k in range(1, 8):
        pl.semaphore_signal(
            barrier, inc=1, device_id=(group, cuts, lax.rem(sub + k, 8)), device_id_type=MESH
        )

    lane = lax.broadcasted_iota(jnp.int32, (8, 128), 1)
    subl = lax.broadcasted_iota(jnp.int32, (8, 128), 0)
    low = lane < 64
    ez = lax.rem(lane, 8)
    ey = lax.rem(lax.div(lane, 8), 8)

    raw[:, 1024:1152] = jnp.zeros((56, 128), F32)
    for c in range(3):
        raw[c * 8 : c * 8 + 8, 0:1089] = now_ref[0, c]
        raw[24 + c * 8 : 32 + c * 8, 0:1089] = prev_ref[0, c]
    raw[48:56, 0:1089] = dens_ref[...]
    rest = jnp.zeros((72, 128), F32)
    for i in range(9):
        block = jnp.concatenate([raw[:, i * 128 : i * 128 + 128], rest], axis=0)
        tee[i * 128 : i * 128 + 128, :] = block.T
    for i in range(0, 25, 2):
        pair = BLOCKS[i : i + 2]
        rows = []
        for b, d in (pair + pair)[:2]:
            for y in range(8):
                rows.append(tee[pl.ds(132 * y + 33 * b + d, 8, stride=4), :])
        turned = jnp.concatenate(rows, axis=0).T
        for h, (b, d) in enumerate(pair):
            at = (d * 5 + b) * 8
            for q in range(7):
                v = turned[q * 8 : q * 8 + 8, :]
                swapped = pltpu.roll(v, 64, 1)
                if h == 0:
                    val = jnp.where(low, v, pltpu.roll(swapped, 4, 0))
                else:
                    val = jnp.where(low, swapped, pltpu.roll(v, 4, 0))
                if q < 3:
                    cur[q, at : at + 8, :] = val
                elif q < 6:
                    pre[q - 3, at : at + 8, :] = val
                else:
                    inv[at : at + 8, :] = val
    cur[:, 200:208, :] = jnp.zeros((3, 8, 128), F32)
    pre[:, 200:208, :] = jnp.zeros((3, 8, 128), F32)
    inv[200:208, :] = jnp.ones((8, 128), F32)

    low25 = lax.broadcasted_iota(jnp.int32, (25, 128), 1) < 64
    face0, face4 = pl.ds(0, 25, stride=8), pl.ds(4, 25, stride=8)
    for c in range(3):
        halo_out[c] = jnp.where(
            low25, cur[c, face0, :], pltpu.roll(pre[c, face0, :], 64, 1)
        )
    halo_out[3] = inv[face0, :]
    pl.semaphore_wait(barrier, 11)
    halo = pltpu.make_async_remote_copy(
        src_ref=halo_out, dst_ref=halo_in, send_sem=halo_sem.at[0], recv_sem=halo_sem.at[1],
        device_id=left, device_id_type=MESH,
    )
    halo.start()

    slot = lax.broadcasted_iota(jnp.int32, (64, 256), 1)
    here = lax.broadcasted_iota(jnp.int32, (64, 64), 0)
    there = lax.broadcasted_iota(jnp.int32, (64, 64), 1)
    earlier = jnp.where(there < here, 1.0, 0.0).astype(BF16)
    for h in range(2):
        owner = jnp.broadcast_to(own_ref[h], (64, 256))
        hit = owner == lax.div(slot, 32)
        onehot = jnp.where(hit, 1.0, 0.0)
        count = jnp.dot(earlier, onehot.astype(BF16), preferred_element_type=F32)
        want = (lax.rem(slot, 16)).astype(F32)
        mine = lax.rem(lax.div(slot, 16), 2) == h
        rank_hit = jnp.where(count == want, onehot, 0.0)
        fgrad[h * 64 : h * 64 + 64, 0:256] = jnp.where(mine, rank_hit, 0.0)
    for i in range(2):
        sel[i * 128 : i * 128 + 128, :] = (
            fgrad[0:128, i * 128 : i * 128 + 128].T.astype(BF16)
        )
    urhs[1248:1280, :] = jnp.zeros((32, 384), BF16)
    zeros16 = jnp.zeros((16, 384), BF16)
    for i in range(18):
        srhs[i * 128 + 112 : i * 128 + 128, :] = zeros16
    zeros_tail = jnp.zeros((16, 128), F32)
    kb[112:128, :] = zeros_tail
    ks[112:128, :] = zeros_tail

    halo.wait()
    for c in range(3):
        got = halo_in[c]
        cur[c, face4, :] = jnp.where(low25, cur[c, face4, :], pltpu.roll(got, 64, 1))
        pre[c, face4, :] = jnp.where(low25, pre[c, face4, :], got)
    inv[face4, :] = jnp.where(low25, inv[face4, :], pltpu.roll(halo_in[3], 64, 1))
    inv[...] = 1.0 / (inv[...] * wt_ref[...])

    far_copies = []
    for s in range(STEPS):
        far_copies.append(
            [
                pltpu.make_async_remote_copy(
                    src_ref=far.at[s], dst_ref=far.at[s],
                    send_sem=far_send.at[s, k - 1], recv_sem=far_recv.at[s],
                    device_id=(k, cuts, sub), device_id_type=MESH,
                )
                for k in (1, 2)
            ]
        )

    def send_far(s):
        @pl.when(group == 0)
        def _():
            for a in range(5):
                far[s, a * 32 + 16 : a * 32 + 32, :] = zeros16
                for c in range(3):
                    far[s, a * 32 : a * 32 + 25, c * 128 : c * 128 + 128] = cur[
                        c, pl.ds(a, 25, stride=8), :
                    ].astype(BF16)
            for copy in far_copies[s]:
                copy.start()

    def gradient(s):
        def body(i, carry):
            r = pl.multiple_of(i * 16, 16)
            for c in range(3):
                u1, u2, u3 = split3(cur[c, pl.ds(r, 16), :])
                for k, part in enumerate((u1, u2, u3, u1, u2, u1)):
                    at = pl.multiple_of(k * UROWS + r, 16)
                    urhs[pl.ds(at, 16), c * 128 : c * 128 + 128] = part
            return carry

        lax.fori_loop(0, UROWS // 16, body, 0)
        grad[s] = jnp.dot(gm_ref[...], urhs[...], preferred_element_type=F32)

    def stress(s):
        def rows(r, n):
            at = pl.ds(r, n)
            g = [
                [grad[s, pl.ds(j * 128 + r, n), c * 128 : c * 128 + 128] for j in range(3)]
                for c in range(3)
            ]
            exx, eyy, ezz = g[0][0], g[1][1], g[2][2]
            exy = 0.5 * (g[0][1] + g[1][0])
            exz = 0.5 * (g[0][2] + g[2][0])
            eyz = 0.5 * (g[1][2] + g[2][1])
            tr = exx + eyy + ezz
            third = tr * (1.0 / 3.0)
            m2 = 2.0 * mu_ref[at, :]
            dev = [m2 * (exx - third), m2 * (eyy - third), m2 * exy, m2 * exz, m2 * eyz]
            total = [None] * 5
            for l in range(3):
                dec = dec_ref[l : l + 1, :]
                gain = (1.0 - dec) * RELAX[l]
                for k in range(5):
                    old = mem_ref[0, l, k, at, :] if s == 0 else mem[l, k, at, :]
                    new = dec * old + gain * dev[k]
                    if s < STEPS - 1:
                        mem[l, k, at, :] = new
                    total[k] = new if total[k] is None else total[k] + new
            bulk = lam_ref[at, :] * tr
            sxx = bulk + m2 * exx - total[0]
            syy = bulk + m2 * eyy - total[1]
            szz = bulk + m2 * ezz + (total[0] + total[1])
            sxy = m2 * exy - total[2]
            sxz = m2 * exz - total[3]
            syz = m2 * eyz - total[4]
            places = (
                (sxx, ((0, 0),)), (syy, ((1, 1),)), (szz, ((2, 2),)),
                (sxy, ((0, 1), (1, 0))), (sxz, ((0, 2), (2, 0))), (syz, ((1, 2), (2, 1))),
            )
            for val, where in places:
                p1, p2, p3 = split3(val)
                for k, part in enumerate((p1, p2, p3, p1, p2, p1)):
                    for c, j in where:
                        srhs[pl.ds(k * 384 + j * 128 + r, n), c * 128 : c * 128 + 128] = part

        def body(i, carry):
            rows(pl.multiple_of(i * 16, 16), 16)
            return carry

        lax.fori_loop(0, 7, body, 0)
        rows(112, 13)
        out = jnp.dot(fm_ref[...], srhs[...], preferred_element_type=F32)
        for c in range(3):
            force[c] = out[:, c * 128 : c * 128 + 128]

    def assemble():
        for c in range(3):
            for b in range(5):
                f0 = force[c, b * 8 : b * 8 + 8, :]
                f4 = force[c, 160 + b * 8 : 168 + b * 8, :]
                n0 = f0 + jnp.where(ez > 0, pltpu.roll(f4, 1, 1), 0.0)
                n4 = f4 + jnp.where(ez < 7, pltpu.roll(f0, 127, 1), 0.0)
                force[c, b * 8 : b * 8 + 8, :] = n0
                force[c, 160 + b * 8 : 168 + b * 8, :] = n4
            for d in range(5):
                f0 = force[c, d * 40 : d * 40 + 8, :]
                f4 = force[c, d * 40 + 32 : d * 40 + 40, :]
                n0 = f0 + jnp.where(ey > 0, pltpu.roll(f4, 8, 1), 0.0)
                n4 = f4 + jnp.where(ey < 7, pltpu.roll(f0, 120, 1), 0.0)
                force[c, d * 40 : d * 40 + 8, :] = n0
                force[c, d * 40 + 32 : d * 40 + 40, :] = n4

    def face_copies(s):
        to_right = pltpu.make_async_remote_copy(
            src_ref=face_out.at[s], dst_ref=face_left.at[s],
            send_sem=face_send.at[s, 0], recv_sem=face_recv.at[s, 0],
            device_id=right, device_id_type=MESH,
        )
        if s == STEPS - 1:
            return [to_right]
        to_left = pltpu.make_async_remote_copy(
            src_ref=face_out.at[s], dst_ref=face_right.at[s],
            send_sem=face_send.at[s, 1], recv_sem=face_recv.at[s, 1],
            device_id=left, device_id_type=MESH,
        )
        return [to_right, to_left]

    def update(s):
        for c in range(3):
            f0, f4 = force[c, face0, :], force[c, face4, :]
            force[c, face0, :] = f0 + pltpu.roll(jnp.where(low25, f4, face_left[s, c]), 64, 1)
            if s < STEPS - 1:
                force[c, face4, :] = f4 + pltpu.roll(
                    jnp.where(low25, face_right[s, c], f0), 64, 1
                )
            else:
                force[c, face4, :] = f4 + pltpu.roll(f0, 64, 1)

        def body(i, carry):
            at = pl.ds(pl.multiple_of(i * 8, 8), 8)
            scale = inv[at, :]
            for c in range(3):
                u = cur[c, at, :]
                cur[c, at, :] = 2.0 * u - pre[c, at, :] + force[c, at, :] * scale
                pre[c, at, :] = u
            return carry

        lax.fori_loop(0, 25, body, 0)

    part_copies = []
    for s in range(STEPS):
        line = []
        for k in range(1, 8):
            to = lax.rem(sub + k, 8)
            line.append(
                pltpu.make_async_remote_copy(
                    src_ref=parts_out.at[s, to], dst_ref=parts_in.at[s, sub],
                    send_sem=part_send.at[s, k - 1], recv_sem=part_recv.at[s, k - 1],
                    device_id=(group, cuts, to), device_id_type=MESH,
                )
            )
        part_copies.append(line)

    def kernel_part(s):
        @pl.when(group != 0)
        def _():
            far_copies[s][0].wait_recv()

        for k in range(3):
            frhs[k * FROWS : (k + 1) * FROWS, :] = far[s]
        fgrad[...] = jnp.dot(gf_ref[...], frhs[...], preferred_element_type=F32)

        def rows(r, n):
            at = pl.ds(r, n)

            def strain(get):
                g = [[get(c, j) for j in range(3)] for c in range(3)]
                diag = [g[0][0], g[1][1], g[2][2]]
                tr = diag[0] + diag[1] + diag[2]
                third = tr * (1.0 / 3.0)
                dev = [x - third for x in diag]
                shear = [g[0][1] + g[1][0], g[0][2] + g[2][0], g[1][2] + g[2][1]]
                return tr, dev, shear

            tr, dev, off = strain(
                lambda c, j: grad[s, pl.ds(j * 128 + r, n), c * 128 : c * 128 + 128]
            )
            trf, devf, offf = strain(
                lambda c, j: fgrad[pl.ds(j * 128 + r, n), c * 128 : c * 128 + 128]
            )
            m2 = 2.0 * mu_ref[at, :]
            kappa = lam_ref[at, :] + m2 * (1.0 / 3.0)
            kb[at, :] = TIME_STEP * kappa * trf * tr
            prod = dev[0] * devf[0] + dev[1] * devf[1] + dev[2] * devf[2]
            cross = off[0] * offf[0] + off[1] * offf[1] + off[2] * offf[2]
            ks[at, :] = TIME_STEP * m2 * (prod + 0.5 * cross)

        def body(i, carry):
            rows(pl.multiple_of(i * 8, 8), 8)
            return carry

        lax.fori_loop(0, 15, body, 0)
        rows(120, 5)
        for i, ref in enumerate((kb, ks)):
            placed = lax.dot_general(
                sel[...], ref[...].astype(BF16), (((1,), (1,)), ((), ())),
                preferred_element_type=F32,
            ).astype(BF16)
            for t in range(8):
                parts_out[s, t, :, i * 128 : i * 128 + 128] = placed[t * 32 : t * 32 + 32, :]
        parts_in[s, sub] = parts_out[s, sub]
        for copy in part_copies[s]:
            copy.start()

    for s in range(STEPS):
        send_far(s)
        gradient(s)
        stress(s)
        assemble()
        for c in range(3):
            face_out[s, c] = jnp.where(low25, force[c, face0, :], force[c, face4, :])
        copies = face_copies(s)
        for copy in copies:
            copy.start()
        if s == STEPS - 1:
            kernel_part(0)
        for copy in copies:
            copy.wait()
        update(s)

    kernel_part(1)
    rest = jnp.zeros((104, 128), F32)
    for i in range(0, 25, 2):
        pair = BLOCKS[i : i + 2]
        blocks = []
        for c in range(3):
            both = []
            for b, d in pair:
                at = (d * 5 + b) * 8
                v = cur[c, at : at + 8, :]
                both.append(jnp.where(subl < 4, v, pltpu.roll(pltpu.roll(v, 64, 1), 4, 0)))
            second = both[-1]
            blocks.append(jnp.where(low, both[0], pltpu.roll(second, 64, 1)))
        turned = jnp.concatenate(blocks + [rest], axis=0).T
        for h, (b, d) in enumerate(pair):
            for y in range(8):
                tee[pl.ds(132 * y + 33 * b + d, 8, stride=4), :] = turned[
                    h * 64 + y * 8 : h * 64 + y * 8 + 8, :
                ]
    for i in range(9):
        block = tee[i * 128 : i * 128 + 128, :].T
        width = min(128, 1089 - i * 128)
        for c in range(3):
            disp_ref[0, c, :, i * 128 : i * 128 + width] = block[c * 8 : c * 8 + 8, 0:width]

    kernel_part(2)
    for s in range(STEPS):
        @pl.when(group == 0)
        def _():
            for copy in far_copies[s]:
                copy.wait_send()

        for copy in part_copies[s]:
            copy.wait()
    for t in range(8):
        total = parts_in[0, t].astype(F32)
        for s in range(1, STEPS):
            total = total + parts_in[s, t].astype(F32)
        ker_ref[0, t * 32 : t * 32 + 32, 0:125] = total[:, 0:125]
        ker_ref[0, t * 32 : t * 32 + 32, 125:250] = total[:, 128:253]


def per_device(consts, now, prev, mem, dens, lam, mu, dec, own):
    vmem = pl.BlockSpec(memory_space=pltpu.VMEM)
    dma = pltpu.SemaphoreType.DMA
    return pl.pallas_call(
        kernel,
        out_shape=(
            jax.ShapeDtypeStruct((1, 3, 8, 1089), F32),
            jax.ShapeDtypeStruct((1, 256, 250), F32),
        ),
        in_specs=[vmem] * 12,
        out_specs=(vmem, vmem),
        scratch_shapes=[
            pltpu.VMEM((56, 1152), F32),
            pltpu.VMEM((1152, 128), F32),
            pltpu.VMEM((3, UROWS, 128), F32),
            pltpu.VMEM((3, UROWS, 128), F32),
            pltpu.VMEM((UROWS, 128), F32),
            pltpu.VMEM((GK, 384), BF16),
            pltpu.VMEM((STEPS, 384, 384), F32),
            pltpu.VMEM((2304, 384), BF16),
            pltpu.VMEM((3, UROWS, 128), F32),
            pltpu.VMEM((3, 5, 125, 128), F32),
            pltpu.VMEM((STEPS, FROWS, 384), BF16),
            pltpu.VMEM((3 * FROWS, 384), BF16),
            pltpu.VMEM((384, 384), F32),
            pltpu.VMEM((128, 128), F32),
            pltpu.VMEM((128, 128), F32),
            pltpu.VMEM((256, 128), BF16),
            pltpu.VMEM((4, 25, 128), F32),
            pltpu.VMEM((4, 25, 128), F32),
            pltpu.VMEM((STEPS, 3, 25, 128), F32),
            pltpu.VMEM((STEPS, 3, 25, 128), F32),
            pltpu.VMEM((STEPS, 3, 25, 128), F32),
            pltpu.VMEM((STEPS, 8, 32, 256), BF16),
            pltpu.VMEM((STEPS, 8, 32, 256), BF16),
            dma((2,)),
            dma((STEPS, 2)),
            dma((STEPS, 2)),
            dma((STEPS, 2)),
            dma((STEPS,)),
            dma((STEPS, 7)),
            dma((STEPS, 7)),
        ],
        compiler_params=pltpu.CompilerParams(
            collective_id=0, has_side_effects=True, vmem_limit_bytes=48 * 1024 * 1024
        ),
        name="wavefields",
    )(*consts, now, prev, mem, dens, lam, mu, dec, own)


def solution(mesh):
    consts = tuple(jnp.asarray(t) for t in tables())
    in_specs = (
        P("group", None, ("cuts", "sub"), None),
        P("group", None, ("cuts", "sub"), None),
        P("group", None, None, None, ("cuts", "sub")),
        P(("cuts", "sub"), None),
        P(None, ("cuts", "sub")),
        P(None, ("cuts", "sub")),
        P(None, ("cuts", "sub")),
        P(("cuts", "sub"), None, None),
    )
    out_specs = (P("group", None, ("cuts", "sub"), None), P("group", ("cuts", "sub"), None))
    return jax.shard_map(
        functools.partial(per_device, consts),
        mesh=mesh, in_specs=in_specs, out_specs=out_specs, check_vma=False,
    )
```

```python
import functools
import math

import jax
import jax.numpy as jnp
import numpy as np
from jax import lax
from jax.experimental import pallas as pl
from jax.experimental.pallas import tpu as pltpu
from jax.sharding import PartitionSpec as P

STEPS = 3
TIME_STEP = 0.03
STEP_SQUARE = 0.0009
RELAX = (0.12, 0.08, 0.05)
F32 = jnp.float32
BF16 = jnp.bfloat16
MESH = pl.DeviceIdType.MESH

BLOCKS = [(b, d) for d in range(5) for b in range(5)]
UROWS = 208
GK = 1280
NBR = 18


def gll():
    root = math.sqrt(3.0 / 7.0)
    x = [-1.0, -root, 0.0, root, 1.0]
    w = np.array([0.1, 49.0 / 90.0, 32.0 / 45.0, 49.0 / 90.0, 0.1])
    der = np.zeros((5, 5))
    for p in range(5):
        for a in range(5):
            acc = 0.0
            for m in range(5):
                if m != a:
                    fac = 1.0 / (x[a] - x[m])
                    for k in range(5):
                        if k != a and k != m:
                            fac = fac * (x[p] - x[k]) / (x[a] - x[k])
                    acc = acc + fac
            der[p, a] = acc
    return der.astype(np.float32).astype(np.float64), w.astype(np.float32).astype(np.float64)


def pieces(mat, count):
    out = []
    rest = mat.astype(np.float64)
    for _ in range(count):
        part = rest.astype(jnp.bfloat16)
        out.append(part)
        rest = rest - part.astype(np.float64)
    return out


def tables():
    der, w = gll()
    grad = np.zeros((384, UROWS))
    force = np.zeros((UROWS, 384))

    def row(a, b, d):
        return (d * 5 + b) * 8 + a

    for a in range(5):
        for b in range(5):
            for d in range(5):
                r = row(a, b, d)
                for p in range(5):
                    for j, q in enumerate(((p, b, d), (a, p, d), (a, b, p))):
                        n = j * 128 + q[0] * 25 + q[1] * 5 + q[2]
                        at = (a, b, d)[j]
                        grad[n, r] = der[p, at]
                        force[r, n] = -der[p, at] * w[q[0]] * w[q[1]] * w[q[2]]
    g = pieces(grad, 3)
    gm = np.zeros((384, GK), jnp.bfloat16)
    for i, k in enumerate((0, 0, 0, 1, 1, 2)):
        gm[:, i * UROWS : (i + 1) * UROWS] = g[k]
    gf = np.concatenate(g, axis=1)
    f = pieces(force, 2)
    fm = np.concatenate([f[k] for k in (0, 0, 1)], axis=1)
    weight = np.ones((UROWS, 128))
    for a in range(5):
        for b in range(5):
            for d in range(5):
                for e in range(128):
                    ey, ez = (e // 8) % 8, e % 8
                    wx = w[0] + w[4] if a in (0, 4) else w[a]
                    wy = w[b] + (w[0] if (b == 4 and ey < 7) or (b == 0 and ey > 0) else 0.0)
                    wz = w[d] + (w[0] if (d == 4 and ez < 7) or (d == 0 and ez > 0) else 0.0)
                    weight[row(a, b, d), e] = wx * wy * wz
    return gm, gf, fm, (weight / STEP_SQUARE).astype(np.float32)


def split3(x):
    x1 = x.astype(BF16)
    r1 = x - x1.astype(F32)
    x2 = r1.astype(BF16)
    x3 = (r1 - x2.astype(F32)).astype(BF16)
    return x1, x2, x3


def kernel(
    gm_hbm, gf_hbm, fm_hbm, wt_hbm,
    now_hbm, prev_hbm, mem_hbm, dens_hbm, lam_hbm, mu_hbm, dec_hbm, own_hbm,
    disp_ref, ker_ref,
    gm_ref, gf_ref, fm_ref, wt_ref, now_ref, prev_ref, mem, dens_ref, lam_ref, mu_ref,
    dec_ref, own_ref, own_row, load_sem,
    last, tee, cur, pre, inv, urhs, grad, srhs, force, base, finv, xs, yi, yb, fint, fbnd,
    frhs, fgrad, kb, ks, sel,
    halo_out, halo_in, face_out, face_left, face_right, parts_out, parts_in,
    halo_sem, face_send, face_recv, far_send, far_recv, part_send, part_recv,
):
    loads = [
        pltpu.make_async_copy(src, dst, load_sem.at[i])
        for i, (src, dst) in enumerate(
            (
                (now_hbm, now_ref), (prev_hbm, prev_ref), (dens_hbm, dens_ref),
                (wt_hbm, wt_ref), (own_hbm, own_ref), (gm_hbm, gm_ref),
                (dec_hbm, dec_ref), (lam_hbm, lam_ref), (mu_hbm, mu_ref),
                (fm_hbm, fm_ref), (gf_hbm, gf_ref),
            )
        )
    ]
    for l in range(3):
        for k in range(5):
            loads.append(
                pltpu.make_async_copy(
                    mem_hbm.at[l, k, :, 0, :], mem.at[l, k], load_sem.at[len(loads)]
                )
            )
    for load in loads:
        load.start()

    group = lax.axis_index("group")
    cuts = lax.axis_index("cuts")
    sub = lax.axis_index("sub")
    flat = cuts * 8 + sub
    ring = lax.axis_size("cuts") * 8
    nxt = lax.rem(flat + 1, ring)
    prv = lax.rem(flat + ring - 1, ring)
    right = (group, lax.div(nxt, 8), lax.rem(nxt, 8))
    left = (group, lax.div(prv, 8), lax.rem(prv, 8))

    barrier = pltpu.get_barrier_semaphore()
    for dev in (left, right):
        pl.semaphore_signal(barrier, inc=1, device_id=dev, device_id_type=MESH)
    for k in range(1, 3):
        pl.semaphore_signal(
            barrier, inc=1, device_id=(lax.rem(group + k, 3), cuts, sub), device_id_type=MESH
        )
    for k in range(1, 8):
        pl.semaphore_signal(
            barrier, inc=1, device_id=(group, cuts, lax.rem(sub + k, 8)), device_id_type=MESH
        )

    lane = lax.broadcasted_iota(jnp.int32, (8, 128), 1)
    subl = lax.broadcasted_iota(jnp.int32, (8, 128), 0)
    low = lane < 64
    ez = lax.rem(lane, 8)
    ey = lax.rem(lax.div(lane, 8), 8)
    low25 = lax.broadcasted_iota(jnp.int32, (25, 128), 1) < 64
    low18 = lax.broadcasted_iota(jnp.int32, (NBR, 128), 1) < 64
    face0, face4 = pl.ds(0, 25, stride=8), pl.ds(4, 25, stride=8)

    for i in range(3):
        loads[i].wait()
    last[...] = jnp.zeros((56, 128), F32)
    for c in range(3):
        last[c * 8 : c * 8 + 8, 0:65] = now_ref[0, c, :, 1024:1089]
        last[24 + c * 8 : 32 + c * 8, 0:65] = prev_ref[0, c, :, 1024:1089]
    last[48:56, 0:65] = dens_ref[:, 1024:1089]
    rest = jnp.zeros((72, 128), F32)
    for i in range(9):
        if i < 8:
            at = slice(i * 128, i * 128 + 128)
            stack = [now_ref[0, c, :, at] for c in range(3)]
            stack += [prev_ref[0, c, :, at] for c in range(3)] + [dens_ref[:, at], rest]
        else:
            stack = [last[...], rest]
        tee[i * 128 : i * 128 + 128, :] = jnp.concatenate(stack, axis=0).T
    for i in range(0, 25, 2):
        pair = BLOCKS[i : i + 2]
        rows = []
        for b, d in (pair + pair)[:2]:
            for y in range(8):
                rows.append(tee[pl.ds(132 * y + 33 * b + d, 8, stride=4), :])
        turned = jnp.concatenate(rows, axis=0).T
        for h, (b, d) in enumerate(pair):
            at = (d * 5 + b) * 8
            for q in range(7):
                v = turned[q * 8 : q * 8 + 8, :]
                swapped = pltpu.roll(v, 64, 1)
                if h == 0:
                    val = jnp.where(low, v, pltpu.roll(swapped, 4, 0))
                else:
                    val = jnp.where(low, swapped, pltpu.roll(v, 4, 0))
                if q < 3:
                    cur[q, at : at + 8, :] = val
                elif q < 6:
                    pre[q - 3, at : at + 8, :] = val
                else:
                    inv[at : at + 8, :] = val
    cur[:, 200:208, :] = jnp.zeros((3, 8, 128), F32)
    pre[:, 200:208, :] = jnp.zeros((3, 8, 128), F32)
    inv[200:208, :] = jnp.ones((8, 128), F32)
    for c in range(3):
        halo_out[c] = jnp.where(
            low25, cur[c, face0, :], pltpu.roll(pre[c, face0, :], 64, 1)
        )
    halo_out[3] = inv[face0, :]
    pl.semaphore_wait(barrier, 11)
    halo = pltpu.make_async_remote_copy(
        src_ref=halo_out, dst_ref=halo_in, send_sem=halo_sem.at[0], recv_sem=halo_sem.at[1],
        device_id=left, device_id_type=MESH,
    )
    halo.start()

    def far_copy(s, part, k):
        buf = fint if part == 0 else fbnd
        return pltpu.make_async_remote_copy(
            src_ref=buf.at[s], dst_ref=buf.at[s],
            send_sem=far_send.at[s, part, k - 1], recv_sem=far_recv.at[s, part],
            device_id=(k, cuts, sub), device_id_type=MESH,
        )

    def pack_far(s, part):
        @pl.when(group == 0)
        def _():
            for c in range(3):
                for d in range(4):
                    for b in range(4):
                        to = (d * 4 + b) * 8
                        xs[c, to : to + 8, :] = cur[c, (d * 5 + b) * 8 : (d * 5 + b) * 8 + 8, :]
                ends = cur[c, 192:200, :]
                for b in range(4):
                    moved = pltpu.roll(cur[c, 160 + b * 8 : 168 + b * 8, :], 121 + b, 1)
                    ends = jnp.where(ez == b, moved, ends) if b else jnp.where(
                        ez == b, moved, pltpu.roll(ends, 125, 1)
                    )
                xs[c, 128:136, :] = ends
                ends = pltpu.roll(cur[c, 32:40, :], 72, 1)
                for d in range(1, 4):
                    moved = pltpu.roll(cur[c, d * 40 + 32 : d * 40 + 40, :], 72 + 8 * d, 1)
                    ends = jnp.where(ey == d, moved, ends)
                xs[c, 136:144, :] = ends
                if part == 0:
                    for a in range(1, 5):
                        yi[pl.ds(72 * c + a - 1, NBR, stride=4), :] = xs[
                            c, pl.ds(a, NBR, stride=8), :
                        ]
                else:
                    yb[pl.ds(c, NBR, stride=3), :] = jnp.where(
                        low18, xs[c, pl.ds(0, NBR, stride=8), :], xs[c, pl.ds(4, NBR, stride=8), :]
                    )
            if part == 0:
                fint[s] = yi[...].astype(BF16)
            else:
                fbnd[s] = yb[...].astype(BF16)
            for k in (1, 2):
                far_copy(s, part, k).start()

    yi[216:224, :] = jnp.zeros((8, 128), F32)
    yb[48:64, :] = jnp.zeros((16, 128), F32)
    pack_far(0, 0)

    for i in range(3, 5):
        loads[i].wait()
    own_row[0:1, 0:64] = own_ref[0]
    own_row[0:1, 64:128] = own_ref[1]
    slot = lax.broadcasted_iota(jnp.int32, (256, 128), 0)
    elem = lax.broadcasted_iota(jnp.int32, (256, 128), 1)
    onehot = jnp.where(own_row[0:1, :] == lax.div(slot, 32), 1.0, 0.0)
    one = lax.broadcasted_iota(jnp.int32, (128, 128), 0)
    two = lax.broadcasted_iota(jnp.int32, (128, 128), 1)
    one_low, two_low = one < 64, two < 64
    earlier = jnp.where(one < two, jnp.where(two_low, 1.0, jnp.where(one_low, 0.0, 1.0)), 0.0)
    count = jnp.dot(onehot.astype(BF16), earlier.astype(BF16), preferred_element_type=F32)
    rank_hit = jnp.where(count == lax.rem(slot, 16).astype(F32), onehot, 0.0)
    mine = lax.rem(lax.div(slot, 16), 2) == lax.div(elem, 64)
    sel[...] = jnp.where(mine, rank_hit, 0.0).astype(BF16)
    urhs[1248:1280, :] = jnp.zeros((32, 384), BF16)
    zeros16 = jnp.zeros((16, 384), BF16)
    for i in range(9):
        srhs[i * 128 + 112 : i * 128 + 128, :] = zeros16
    kb[112:128, :] = jnp.zeros((16, 128), BF16)
    ks[112:128, :] = jnp.zeros((16, 128), BF16)

    halo.wait()
    for c in range(3):
        got = halo_in[c]
        cur[c, face4, :] = jnp.where(low25, cur[c, face4, :], pltpu.roll(got, 64, 1))
        pre[c, face4, :] = jnp.where(low25, pre[c, face4, :], got)
    inv[face4, :] = jnp.where(low25, inv[face4, :], pltpu.roll(halo_in[3], 64, 1))
    pack_far(0, 1)
    inv[...] = 1.0 / (inv[...] * wt_ref[...])
    finv[...] = jnp.where(low25, inv[face0, :], inv[face4, :])

    def gradient(s):
        for i in range(UROWS // 16):
            for c in range(3):
                u1, u2, u3 = split3(cur[c, i * 16 : i * 16 + 16, :])
                for k, part in enumerate((u1, u2, u3, u1, u2, u1)):
                    at = k * UROWS + i * 16
                    urhs[at : at + 16, c * 128 : c * 128 + 128] = part
        grad[s] = jnp.dot(gm_ref[...], urhs[...], preferred_element_type=F32)

    def stress(s):
        def rows(r, n):
            at = slice(r, r + n)
            g = [
                [
                    grad[s, j * 128 + r : j * 128 + r + n, c * 128 : c * 128 + 128]
                    for j in range(3)
                ]
                for c in range(3)
            ]
            exx, eyy, ezz = g[0][0], g[1][1], g[2][2]
            exy = 0.5 * (g[0][1] + g[1][0])
            exz = 0.5 * (g[0][2] + g[2][0])
            eyz = 0.5 * (g[1][2] + g[2][1])
            tr = exx + eyy + ezz
            third = tr * (1.0 / 3.0)
            m2 = 2.0 * mu_ref[at, :]
            sxy, sxz, syz = m2 * exy, m2 * exz, m2 * eyz
            dev = [m2 * (exx - third), m2 * (eyy - third), sxy, sxz, syz]
            total = [None] * 5
            for k in range(5):
                for l in range(3):
                    new = dec_ref[l : l + 1, :] * mem[l, k, at, :] + gains[l] * dev[k]
                    if s < STEPS - 1:
                        mem[l, k, at, :] = new
                    total[k] = new if total[k] is None else total[k] + new
            bulk = lam_ref[at, :] * tr
            sxx = bulk + m2 * exx - total[0]
            syy = bulk + m2 * eyy - total[1]
            szz = bulk + m2 * ezz + (total[0] + total[1])
            places = (
                (sxx, ((0, 0),)), (syy, ((1, 1),)), (szz, ((2, 2),)),
                (sxy - total[2], ((0, 1), (1, 0))), (sxz - total[3], ((0, 2), (2, 0))),
                (syz - total[4], ((1, 2), (2, 1))),
            )
            for val, where in places:
                p1 = val.astype(BF16)
                p2 = (val - p1.astype(F32)).astype(BF16)
                for k, part in enumerate((p1, p2, p1)):
                    for c, j in where:
                        to = k * 384 + j * 128 + r
                        srhs[to : to + n, c * 128 : c * 128 + 128] = part

        gains = [(1.0 - dec_ref[l : l + 1, :]) * RELAX[l] for l in range(3)]
        for i in range(7):
            rows(i * 16, 16)
        rows(112, 13)
        out = jnp.dot(fm_ref[...], srhs[...], preferred_element_type=F32)
        for c in range(3):
            force[c] = out[:, c * 128 : c * 128 + 128]

    def assemble(s):
        for c in range(3):
            for b in range(5):
                f0 = force[c, b * 8 : b * 8 + 8, :]
                f4 = force[c, 160 + b * 8 : 168 + b * 8, :]
                n0 = f0 + jnp.where(ez > 0, pltpu.roll(f4, 1, 1), 0.0)
                n4 = f4 + jnp.where(ez < 7, pltpu.roll(f0, 127, 1), 0.0)
                force[c, b * 8 : b * 8 + 8, :] = n0
                force[c, 160 + b * 8 : 168 + b * 8, :] = n4
            for d in range(5):
                f0 = force[c, d * 40 : d * 40 + 8, :]
                f4 = force[c, d * 40 + 32 : d * 40 + 40, :]
                n0 = f0 + jnp.where(ey > 0, pltpu.roll(f4, 8, 1), 0.0)
                n4 = f4 + jnp.where(ey < 7, pltpu.roll(f0, 120, 1), 0.0)
                force[c, d * 40 : d * 40 + 8, :] = n0
                force[c, d * 40 + 32 : d * 40 + 40, :] = n4
            face_out[s, c] = jnp.where(low25, force[c, face0, :], force[c, face4, :])

    def face_copies(s):
        to_right = pltpu.make_async_remote_copy(
            src_ref=face_out.at[s], dst_ref=face_left.at[s],
            send_sem=face_send.at[s, 0], recv_sem=face_recv.at[s, 0],
            device_id=right, device_id_type=MESH,
        )
        if s == STEPS - 1:
            return [to_right]
        to_left = pltpu.make_async_remote_copy(
            src_ref=face_out.at[s], dst_ref=face_right.at[s],
            send_sem=face_send.at[s, 1], recv_sem=face_recv.at[s, 1],
            device_id=left, device_id_type=MESH,
        )
        return [to_right, to_left]

    def update_inside():
        for c in range(3):
            f0, f4 = force[c, face0, :], force[c, face4, :]
            force[c, face0, :] = f0 + jnp.where(low25, 0.0, pltpu.roll(f4, 64, 1))
            force[c, face4, :] = f4 + jnp.where(low25, pltpu.roll(f0, 64, 1), 0.0)
            base[c] = jnp.where(
                low25,
                2.0 * cur[c, face0, :] - pre[c, face0, :],
                2.0 * cur[c, face4, :] - pre[c, face4, :],
            )
        for i in range(UROWS // 16):
            at = slice(i * 16, i * 16 + 16)
            scale = inv[at, :]
            for c in range(3):
                u = cur[c, at, :]
                cur[c, at, :] = 2.0 * u - pre[c, at, :] + force[c, at, :] * scale
                pre[c, at, :] = u

    def update_ends(s):
        for c in range(3):
            if s < STEPS - 1:
                got = jnp.where(low25, face_right[s, c], face_left[s, c])
            else:
                got = face_left[s, c]
            new = base[c] + (face_out[s, c] + pltpu.roll(got, 64, 1)) * finv[...]
            cur[c, face0, :] = jnp.where(low25, new, cur[c, face0, :])
            if s < STEPS - 1:
                cur[c, face4, :] = jnp.where(low25, cur[c, face4, :], new)

    part_copies = []
    for s in range(STEPS):
        line = []
        for k in range(1, 8):
            to = lax.rem(sub + k, 8)
            line.append(
                pltpu.make_async_remote_copy(
                    src_ref=parts_out.at[s, to], dst_ref=parts_in.at[s, sub],
                    send_sem=part_send.at[s, k - 1], recv_sem=part_recv.at[s, k - 1],
                    device_id=(group, cuts, to), device_id_type=MESH,
                )
            )
        part_copies.append(line)

    def kernel_part(s):
        @pl.when(group != 0)
        def _():
            for part in range(2):
                far_copy(s, part, 1).wait_recv()

        yi[...] = fint[s].astype(F32)
        yb[...] = fbnd[s].astype(F32)
        for c in range(3):
            for a in range(1, 4):
                xs[c, pl.ds(a, NBR, stride=8), :] = yi[pl.ds(72 * c + a - 1, NBR, stride=4), :]
            mid = yi[pl.ds(72 * c + 3, NBR, stride=4), :]
            ends = yb[pl.ds(c, NBR, stride=3), :]
            xs[c, pl.ds(0, NBR, stride=8), :] = jnp.where(low18, ends, pltpu.roll(mid, 64, 1))
            xs[c, pl.ds(4, NBR, stride=8), :] = jnp.where(low18, mid, ends)
        for c in range(3):
            block = {}
            for d in range(4):
                for b in range(4):
                    at = (d * 4 + b) * 8
                    block[b, d] = xs[c, at : at + 8, :]
            zend, yend = xs[c, 128:136, :], xs[c, 136:144, :]
            for d in range(4):
                block[4, d] = jnp.where(
                    ey < 7, pltpu.roll(block[0, d], 120, 1), pltpu.roll(yend, 8 * (7 - d), 1)
                )
            for b in range(5):
                block[b, 4] = jnp.where(
                    ez < 7, pltpu.roll(block[b, 0], 127, 1), pltpu.roll(zend, 7 - b, 1)
                )
            line = [block[bd] for bd in BLOCKS] + [jnp.zeros((8, 128), F32)]
            for i in range(0, 26, 2):
                tile = jnp.concatenate(line[i : i + 2], axis=0).astype(BF16)
                for k in range(3):
                    at = k * UROWS + i * 8
                    frhs[at : at + 16, c * 128 : c * 128 + 128] = tile
        fgrad[...] = jnp.dot(gf_ref[...], frhs[...], preferred_element_type=F32)

        def rows(r, n):
            at = slice(r, r + n)

            def strain(get):
                g = [[get(c, j) for j in range(3)] for c in range(3)]
                diag = [g[0][0], g[1][1], g[2][2]]
                tr = diag[0] + diag[1] + diag[2]
                third = tr * (1.0 / 3.0)
                dev = [x - third for x in diag]
                shear = [g[0][1] + g[1][0], g[0][2] + g[2][0], g[1][2] + g[2][1]]
                return tr, dev, shear

            tr, dev, off = strain(
                lambda c, j: grad[s, j * 128 + r : j * 128 + r + n, c * 128 : c * 128 + 128]
            )
            trf, devf, offf = strain(
                lambda c, j: fgrad[j * 128 + r : j * 128 + r + n, c * 128 : c * 128 + 128]
            )
            m2 = 2.0 * mu_ref[at, :]
            kappa = lam_ref[at, :] + m2 * (1.0 / 3.0)
            kb[at, :] = (TIME_STEP * kappa * trf * tr).astype(BF16)
            prod = dev[0] * devf[0] + dev[1] * devf[1] + dev[2] * devf[2]
            cross = off[0] * offf[0] + off[1] * offf[1] + off[2] * offf[2]
            ks[at, :] = (TIME_STEP * m2 * (prod + 0.5 * cross)).astype(BF16)

        for i in range(7):
            rows(i * 16, 16)
        rows(112, 13)
        for i, ref in enumerate((kb, ks)):
            placed = lax.dot_general(
                sel[...], ref[...], (((1,), (1,)), ((), ())), preferred_element_type=F32
            ).astype(BF16)
            for t in range(8):
                parts_out[s, t, :, i * 128 : i * 128 + 128] = placed[t * 32 : t * 32 + 32, :]
        parts_in[s, sub] = parts_out[s, sub]
        for copy in part_copies[s]:
            copy.start()

    for i in range(5, 6):
        loads[i].wait()
    for s in range(STEPS):
        gradient(s)
        if s == 0:
            for load in loads[6:]:
                load.wait()
        stress(s)
        assemble(s)
        copies = face_copies(s)
        for copy in copies:
            copy.start()
        update_inside()
        if s < STEPS - 1:
            pack_far(s + 1, 0)
            if s == 1:
                kernel_part(0)
        else:
            kernel_part(1)
            kernel_part(2)
        for copy in copies:
            copy.wait()
        update_ends(s)
        if s < STEPS - 1:
            pack_far(s + 1, 1)

    rest = jnp.zeros((104, 128), F32)
    for i in range(0, 25, 2):
        pair = BLOCKS[i : i + 2]
        blocks = []
        for c in range(3):
            both = []
            for b, d in pair:
                at = (d * 5 + b) * 8
                v = cur[c, at : at + 8, :]
                both.append(jnp.where(subl < 4, v, pltpu.roll(pltpu.roll(v, 64, 1), 4, 0)))
            second = both[-1]
            blocks.append(jnp.where(low, both[0], pltpu.roll(second, 64, 1)))
        turned = jnp.concatenate(blocks + [rest], axis=0).T
        for h, (b, d) in enumerate(pair):
            for y in range(8):
                tee[pl.ds(132 * y + 33 * b + d, 8, stride=4), :] = turned[
                    h * 64 + y * 8 : h * 64 + y * 8 + 8, :
                ]
    for i in range(9):
        block = tee[i * 128 : i * 128 + 128, :].T
        width = min(128, 1089 - i * 128)
        for c in range(3):
            disp_ref[0, c, :, i * 128 : i * 128 + width] = block[c * 8 : c * 8 + 8, 0:width]

    @pl.when(group == 0)
    def _():
        for s in range(STEPS):
            for part in range(2):
                for k in (1, 2):
                    far_copy(s, part, k).wait_send()

    for s in range(STEPS):
        for copy in part_copies[s]:
            copy.wait()
    for t in range(8):
        total = parts_in[0, t].astype(F32)
        for s in range(1, STEPS):
            total = total + parts_in[s, t].astype(F32)
        ker_ref[0, t * 32 : t * 32 + 32, 0:125] = total[:, 0:125]
        ker_ref[0, t * 32 : t * 32 + 32, 125:250] = total[:, 128:253]


def per_device(consts, now, prev, mem, dens, lam, mu, dec, own):
    vmem = pl.BlockSpec(memory_space=pltpu.VMEM)
    hbm = pl.BlockSpec(memory_space=pl.ANY)
    dma = pltpu.SemaphoreType.DMA
    mem = jnp.transpose(mem, (1, 2, 3, 0, 4))
    own = jnp.transpose(own, (0, 2, 1))
    return pl.pallas_call(
        kernel,
        out_shape=(
            jax.ShapeDtypeStruct((1, 3, 8, 1089), F32),
            jax.ShapeDtypeStruct((1, 256, 250), F32),
        ),
        in_specs=[hbm] * 12,
        out_specs=(vmem, vmem),
        scratch_shapes=[
            pltpu.VMEM((384, GK), BF16),
            pltpu.VMEM((384, 3 * UROWS), BF16),
            pltpu.VMEM((UROWS, 1152), BF16),
            pltpu.VMEM((UROWS, 128), F32),
            pltpu.VMEM((1, 3, 8, 1089), F32),
            pltpu.VMEM((1, 3, 8, 1089), F32),
            pltpu.VMEM((3, 5, 125, 128), F32),
            pltpu.VMEM((8, 1089), F32),
            pltpu.VMEM((125, 128), F32),
            pltpu.VMEM((125, 128), F32),
            pltpu.VMEM((3, 128), F32),
            pltpu.VMEM((2, 1, 64), jnp.int32),
            pltpu.VMEM((8, 128), jnp.int32),
            dma((26,)),
            pltpu.VMEM((56, 128), F32),
            pltpu.VMEM((1152, 128), F32),
            pltpu.VMEM((3, UROWS, 128), F32),
            pltpu.VMEM((3, UROWS, 128), F32),
            pltpu.VMEM((UROWS, 128), F32),
            pltpu.VMEM((GK, 384), BF16),
            pltpu.VMEM((STEPS, 384, 384), F32),
            pltpu.VMEM((1152, 384), BF16),
            pltpu.VMEM((3, UROWS, 128), F32),
            pltpu.VMEM((3, 25, 128), F32),
            pltpu.VMEM((25, 128), F32),
            pltpu.VMEM((3, 8 * NBR, 128), F32),
            pltpu.VMEM((224, 128), F32),
            pltpu.VMEM((64, 128), F32),
            pltpu.VMEM((STEPS, 224, 128), BF16),
            pltpu.VMEM((STEPS, 64, 128), BF16),
            pltpu.VMEM((3 * UROWS, 384), BF16),
            pltpu.VMEM((384, 384), F32),
            pltpu.VMEM((128, 128), BF16),
            pltpu.VMEM((128, 128), BF16),
            pltpu.VMEM((256, 128), BF16),
            pltpu.VMEM((4, 25, 128), F32),
            pltpu.VMEM((4, 25, 128), F32),
            pltpu.VMEM((STEPS, 3, 25, 128), F32),
            pltpu.VMEM((STEPS, 3, 25, 128), F32),
            pltpu.VMEM((STEPS, 3, 25, 128), F32),
            pltpu.VMEM((STEPS, 8, 32, 256), BF16),
            pltpu.VMEM((STEPS, 8, 32, 256), BF16),
            dma((2,)),
            dma((STEPS, 2)),
            dma((STEPS, 2)),
            dma((STEPS, 2, 2)),
            dma((STEPS, 2)),
            dma((STEPS, 7)),
            dma((STEPS, 7)),
        ],
        compiler_params=pltpu.CompilerParams(collective_id=0, has_side_effects=True),
        name="wavefields",
    )(*consts, now, prev, mem, dens, lam, mu, dec, own)


def solution(mesh):
    consts = tuple(jnp.asarray(t) for t in tables())
    in_specs = (
        P("group", None, ("cuts", "sub"), None),
        P("group", None, ("cuts", "sub"), None),
        P("group", None, None, None, ("cuts", "sub")),
        P(("cuts", "sub"), None),
        P(None, ("cuts", "sub")),
        P(None, ("cuts", "sub")),
        P(None, ("cuts", "sub")),
        P(("cuts", "sub"), None, None),
    )
    out_specs = (P("group", None, ("cuts", "sub"), None), P("group", ("cuts", "sub"), None))
    return jax.shard_map(
        functools.partial(per_device, consts),
        mesh=mesh, in_specs=in_specs, out_specs=out_specs, check_vma=False,
    )
```

```python
import functools
import math

import jax
import jax.numpy as jnp
import numpy as np
from jax import lax
from jax.experimental import pallas as pl
from jax.experimental.pallas import tpu as pltpu
from jax.sharding import PartitionSpec as P

STEPS = 3
TIME_STEP = 0.03
STEP_SQUARE = 0.0009
RELAX = (0.12, 0.08, 0.05)
F32 = jnp.float32
BF16 = jnp.bfloat16
MESH = pl.DeviceIdType.MESH

BLOCKS = [(b, d) for d in range(5) for b in range(5)]
UROWS = 208
GK = 1280
NBR = 18


def gll():
    root = math.sqrt(3.0 / 7.0)
    x = [-1.0, -root, 0.0, root, 1.0]
    w = np.array([0.1, 49.0 / 90.0, 32.0 / 45.0, 49.0 / 90.0, 0.1])
    der = np.zeros((5, 5))
    for p in range(5):
        for a in range(5):
            acc = 0.0
            for m in range(5):
                if m != a:
                    fac = 1.0 / (x[a] - x[m])
                    for k in range(5):
                        if k != a and k != m:
                            fac = fac * (x[p] - x[k]) / (x[a] - x[k])
                    acc = acc + fac
            der[p, a] = acc
    return der.astype(np.float32).astype(np.float64), w.astype(np.float32).astype(np.float64)


def pieces(mat, count):
    out = []
    rest = mat.astype(np.float64)
    for _ in range(count):
        part = rest.astype(jnp.bfloat16)
        out.append(part)
        rest = rest - part.astype(np.float64)
    return out


def tables():
    der, w = gll()
    grad = np.zeros((384, UROWS))
    force = np.zeros((UROWS, 384))

    def row(a, b, d):
        return (d * 5 + b) * 8 + a

    for a in range(5):
        for b in range(5):
            for d in range(5):
                r = row(a, b, d)
                for p in range(5):
                    for j, q in enumerate(((p, b, d), (a, p, d), (a, b, p))):
                        n = j * 128 + q[0] * 25 + q[1] * 5 + q[2]
                        at = (a, b, d)[j]
                        grad[n, r] = der[p, at]
                        force[r, n] = -der[p, at] * w[q[0]] * w[q[1]] * w[q[2]]
    g = pieces(grad, 3)
    gm = np.zeros((384, GK), jnp.bfloat16)
    for i, k in enumerate((0, 0, 0, 1, 1, 2)):
        gm[:, i * UROWS : (i + 1) * UROWS] = g[k]
    gf = np.concatenate(g, axis=1)
    f = pieces(force, 2)
    fm = np.concatenate([f[k] for k in (0, 0, 1)], axis=1)
    weight = np.ones((UROWS, 128))
    for a in range(5):
        for b in range(5):
            for d in range(5):
                for e in range(128):
                    ey, ez = (e // 8) % 8, e % 8
                    wx = w[0] + w[4] if a in (0, 4) else w[a]
                    wy = w[b] + (w[0] if (b == 4 and ey < 7) or (b == 0 and ey > 0) else 0.0)
                    wz = w[d] + (w[0] if (d == 4 and ez < 7) or (d == 0 and ez > 0) else 0.0)
                    weight[row(a, b, d), e] = wx * wy * wz
    return gm, gf, fm, (weight / STEP_SQUARE).astype(np.float32)


def split3(x):
    x1 = x.astype(BF16)
    r1 = x - x1.astype(F32)
    x2 = r1.astype(BF16)
    x3 = (r1 - x2.astype(F32)).astype(BF16)
    return x1, x2, x3


def kernel(
    gm_hbm, gf_hbm, fm_hbm, wt_hbm,
    now_hbm, prev_hbm, mem_hbm, dens_hbm, lam_hbm, mu_hbm, dec_hbm, own_hbm,
    disp_ref, ker_ref,
    gm_ref, gf_ref, fm_ref, wt_ref, now_ref, prev_ref, mem, dens_ref, lam_ref, mu_ref,
    dec_ref, own_ref, own_row, load_sem,
    last, tee, cur, pre, inv, urhs, grad, srhs, force, base, finv, xs, yi, yb, fint, fbnd,
    frhs, fgrad, kb, ks, sel,
    halo_out, halo_in, own_face, face_out, face_left, face_right, parts_out, parts_in,
    halo_sem, face_send, face_recv, far_send, far_recv, part_send, part_recv,
):
    loads = [
        pltpu.make_async_copy(src, dst, load_sem.at[i])
        for i, (src, dst) in enumerate(
            (
                (now_hbm, now_ref), (prev_hbm, prev_ref), (dens_hbm, dens_ref),
                (wt_hbm, wt_ref), (own_hbm, own_ref), (gm_hbm, gm_ref),
                (dec_hbm, dec_ref), (lam_hbm, lam_ref), (mu_hbm, mu_ref),
                (fm_hbm, fm_ref), (gf_hbm, gf_ref),
            )
        )
    ]
    for l in range(3):
        for k in range(5):
            loads.append(
                pltpu.make_async_copy(
                    mem_hbm.at[l, k, :, 0, :], mem.at[l, k], load_sem.at[len(loads)]
                )
            )
    for load in loads:
        load.start()

    group = lax.axis_index("group")
    cuts = lax.axis_index("cuts")
    sub = lax.axis_index("sub")
    flat = cuts * 8 + sub
    ring = lax.axis_size("cuts") * 8
    nxt = lax.rem(flat + 1, ring)
    prv = lax.rem(flat + ring - 1, ring)
    right = (group, lax.div(nxt, 8), lax.rem(nxt, 8))
    left = (group, lax.div(prv, 8), lax.rem(prv, 8))

    barrier = pltpu.get_barrier_semaphore()
    for dev in (left, right):
        pl.semaphore_signal(barrier, inc=1, device_id=dev, device_id_type=MESH)
    for k in range(1, 3):
        pl.semaphore_signal(
            barrier, inc=1, device_id=(lax.rem(group + k, 3), cuts, sub), device_id_type=MESH
        )
    for k in range(1, 8):
        pl.semaphore_signal(
            barrier, inc=1, device_id=(group, cuts, lax.rem(sub + k, 8)), device_id_type=MESH
        )

    lane = lax.broadcasted_iota(jnp.int32, (8, 128), 1)
    subl = lax.broadcasted_iota(jnp.int32, (8, 128), 0)
    low = lane < 64
    ez = lax.rem(lane, 8)
    ey = lax.rem(lax.div(lane, 8), 8)
    low25 = lax.broadcasted_iota(jnp.int32, (25, 128), 1) < 64
    low18 = lax.broadcasted_iota(jnp.int32, (NBR, 128), 1) < 64
    face0, face4 = pl.ds(0, 25, stride=8), pl.ds(4, 25, stride=8)

    for i in range(3):
        loads[i].wait()
    last[...] = jnp.zeros((56, 128), F32)
    for c in range(3):
        last[c * 8 : c * 8 + 8, 0:65] = now_ref[0, c, :, 1024:1089]
        last[24 + c * 8 : 32 + c * 8, 0:65] = prev_ref[0, c, :, 1024:1089]
    last[48:56, 0:65] = dens_ref[:, 1024:1089]
    rest = jnp.zeros((72, 128), F32)
    for i in range(9):
        if i < 8:
            at = slice(i * 128, i * 128 + 128)
            stack = [now_ref[0, c, :, at] for c in range(3)]
            stack += [prev_ref[0, c, :, at] for c in range(3)] + [dens_ref[:, at], rest]
        else:
            stack = [last[...], rest]
        tee[i * 128 : i * 128 + 128, :] = jnp.concatenate(stack, axis=0).T
    for i in range(0, 25, 2):
        pair = BLOCKS[i : i + 2]
        rows = []
        for b, d in (pair + pair)[:2]:
            for y in range(8):
                rows.append(tee[pl.ds(132 * y + 33 * b + d, 8, stride=4), :])
        turned = jnp.concatenate(rows, axis=0).T
        for h, (b, d) in enumerate(pair):
            at = (d * 5 + b) * 8
            for q in range(7):
                v = turned[q * 8 : q * 8 + 8, :]
                swapped = pltpu.roll(v, 64, 1)
                if h == 0:
                    val = jnp.where(low, v, pltpu.roll(swapped, 4, 0))
                else:
                    val = jnp.where(low, swapped, pltpu.roll(v, 4, 0))
                if q < 3:
                    cur[q, at : at + 8, :] = val
                elif q < 6:
                    pre[q - 3, at : at + 8, :] = val
                else:
                    inv[at : at + 8, :] = val
    cur[:, 200:208, :] = jnp.zeros((3, 8, 128), F32)
    pre[:, 200:208, :] = jnp.zeros((3, 8, 128), F32)
    inv[200:208, :] = jnp.ones((8, 128), F32)
    for c in range(3):
        halo_out[c] = jnp.where(
            low25, cur[c, face0, :], pltpu.roll(pre[c, face0, :], 64, 1)
        )
    halo_out[3] = inv[face0, :]
    pl.semaphore_wait(barrier, 11)
    halo = pltpu.make_async_remote_copy(
        src_ref=halo_out, dst_ref=halo_in, send_sem=halo_sem.at[0], recv_sem=halo_sem.at[1],
        device_id=left, device_id_type=MESH,
    )
    halo.start()

    def far_copy(s, part, k):
        buf = fbnd.at[s] if part == 2 else fint.at[s, part]
        return pltpu.make_async_remote_copy(
            src_ref=buf, dst_ref=buf,
            send_sem=far_send.at[s, part, k - 1], recv_sem=far_recv.at[s, part],
            device_id=(k, cuts, sub), device_id_type=MESH,
        )

    def direct(s, parts):
        return [
            (part, k)
            for part in parts
            for k in (1, 2)
            if part == 2 or s == STEPS - 1 or k == part + 1
        ]

    def relay(s):
        for mine in (1, 2):
            @pl.when(group == mine)
            def _():
                far_copy(s, mine - 1, mine).wait_recv()
                far_copy(s, mine - 1, 3 - mine).start()

    def pack_far(s, part):
        @pl.when(group == 0)
        def _():
            for c in range(3):
                for d in range(4):
                    for b in range(4):
                        to = (d * 4 + b) * 8
                        xs[c, to : to + 8, :] = cur[c, (d * 5 + b) * 8 : (d * 5 + b) * 8 + 8, :]
                ends = cur[c, 192:200, :]
                for b in range(4):
                    moved = pltpu.roll(cur[c, 160 + b * 8 : 168 + b * 8, :], 121 + b, 1)
                    ends = jnp.where(ez == b, moved, ends) if b else jnp.where(
                        ez == b, moved, pltpu.roll(ends, 125, 1)
                    )
                xs[c, 128:136, :] = ends
                ends = pltpu.roll(cur[c, 32:40, :], 72, 1)
                for d in range(1, 4):
                    moved = pltpu.roll(cur[c, d * 40 + 32 : d * 40 + 40, :], 72 + 8 * d, 1)
                    ends = jnp.where(ey == d, moved, ends)
                xs[c, 136:144, :] = ends
                if part == 0:
                    for a in range(1, 5):
                        yi[pl.ds(72 * c + a - 1, NBR, stride=4), :] = xs[
                            c, pl.ds(a, NBR, stride=8), :
                        ]
                else:
                    yb[pl.ds(c, NBR, stride=3), :] = jnp.where(
                        low18, xs[c, pl.ds(0, NBR, stride=8), :], xs[c, pl.ds(4, NBR, stride=8), :]
                    )
            if part == 0:
                for i in range(2):
                    fint[s, i] = yi[i * 112 : i * 112 + 112, :].astype(BF16)
            else:
                fbnd[s] = yb[...].astype(BF16)
            for piece, k in direct(s, (0, 1) if part == 0 else (2,)):
                far_copy(s, piece, k).start()

    xs[...] = jnp.zeros((3, 8 * NBR, 128), F32)
    yi[216:224, :] = jnp.zeros((8, 128), F32)
    yb[48:64, :] = jnp.zeros((16, 128), F32)
    pack_far(0, 0)

    for i in range(3, 5):
        loads[i].wait()
    own_row[0:1, 0:64] = own_ref[0]
    own_row[0:1, 64:128] = own_ref[1]
    slot = lax.broadcasted_iota(jnp.int32, (256, 128), 0)
    elem = lax.broadcasted_iota(jnp.int32, (256, 128), 1)
    onehot = jnp.where(own_row[0:1, :] == lax.div(slot, 32), 1.0, 0.0)
    one = lax.broadcasted_iota(jnp.int32, (128, 128), 0)
    two = lax.broadcasted_iota(jnp.int32, (128, 128), 1)
    one_low, two_low = one < 64, two < 64
    earlier = jnp.where(one < two, jnp.where(two_low, 1.0, jnp.where(one_low, 0.0, 1.0)), 0.0)
    count = jnp.dot(onehot.astype(BF16), earlier.astype(BF16), preferred_element_type=F32)
    rank_hit = jnp.where(count == lax.rem(slot, 16).astype(F32), onehot, 0.0)
    mine = lax.rem(lax.div(slot, 16), 2) == lax.div(elem, 64)
    sel[...] = jnp.where(mine, rank_hit, 0.0).astype(BF16)
    urhs[1248:1280, :] = jnp.zeros((32, 384), BF16)
    zeros16 = jnp.zeros((16, 384), BF16)
    for i in range(9):
        srhs[i * 128 + 112 : i * 128 + 128, :] = zeros16
    kb[112:128, :] = jnp.zeros((16, 128), BF16)
    ks[112:128, :] = jnp.zeros((16, 128), BF16)

    halo.wait()
    for c in range(3):
        got = halo_in[c]
        cur[c, face4, :] = jnp.where(low25, cur[c, face4, :], pltpu.roll(got, 64, 1))
        pre[c, face4, :] = jnp.where(low25, pre[c, face4, :], got)
    inv[face4, :] = jnp.where(low25, inv[face4, :], pltpu.roll(halo_in[3], 64, 1))
    pack_far(0, 1)
    inv[...] = 1.0 / (inv[...] * wt_ref[...])
    finv[...] = jnp.where(low25, inv[face0, :], inv[face4, :])

    def gradient(s):
        for i in range(UROWS // 16):
            for c in range(3):
                u1, u2, u3 = split3(cur[c, i * 16 : i * 16 + 16, :])
                for k, part in enumerate((u1, u2, u3, u1, u2, u1)):
                    at = k * UROWS + i * 16
                    urhs[at : at + 16, c * 128 : c * 128 + 128] = part
        grad[s] = jnp.dot(gm_ref[...], urhs[...], preferred_element_type=F32)

    def stress(s):
        def rows(r, n):
            at = slice(r, r + n)
            g = [
                [
                    grad[s, j * 128 + r : j * 128 + r + n, c * 128 : c * 128 + 128]
                    for j in range(3)
                ]
                for c in range(3)
            ]
            exx, eyy, ezz = g[0][0], g[1][1], g[2][2]
            exy = 0.5 * (g[0][1] + g[1][0])
            exz = 0.5 * (g[0][2] + g[2][0])
            eyz = 0.5 * (g[1][2] + g[2][1])
            tr = exx + eyy + ezz
            third = tr * (1.0 / 3.0)
            m2 = 2.0 * mu_ref[at, :]
            sxy, sxz, syz = m2 * exy, m2 * exz, m2 * eyz
            dev = [m2 * (exx - third), m2 * (eyy - third), sxy, sxz, syz]
            total = [None] * 5
            for k in range(5):
                for l in range(3):
                    new = dec_ref[l : l + 1, :] * mem[l, k, at, :] + gains[l] * dev[k]
                    if s < STEPS - 1:
                        mem[l, k, at, :] = new
                    total[k] = new if total[k] is None else total[k] + new
            bulk = lam_ref[at, :] * tr
            sxx = bulk + m2 * exx - total[0]
            syy = bulk + m2 * eyy - total[1]
            szz = bulk + m2 * ezz + (total[0] + total[1])
            places = (
                (sxx, ((0, 0),)), (syy, ((1, 1),)), (szz, ((2, 2),)),
                (sxy - total[2], ((0, 1), (1, 0))), (sxz - total[3], ((0, 2), (2, 0))),
                (syz - total[4], ((1, 2), (2, 1))),
            )
            for val, where in places:
                p1 = val.astype(BF16)
                p2 = (val - p1.astype(F32)).astype(BF16)
                for k, part in enumerate((p1, p2, p1)):
                    for c, j in where:
                        to = k * 384 + j * 128 + r
                        srhs[to : to + n, c * 128 : c * 128 + 128] = part

        gains = [(1.0 - dec_ref[l : l + 1, :]) * RELAX[l] for l in range(3)]
        for i in range(7):
            rows(i * 16, 16)
        rows(112, 13)
        out = jnp.dot(fm_ref[...], srhs[...], preferred_element_type=F32)
        for c in range(3):
            force[c] = out[:, c * 128 : c * 128 + 128]

    def assemble(s):
        for c in range(3):
            for b in range(5):
                f0 = force[c, b * 8 : b * 8 + 8, :]
                f4 = force[c, 160 + b * 8 : 168 + b * 8, :]
                n0 = f0 + jnp.where(ez > 0, pltpu.roll(f4, 1, 1), 0.0)
                n4 = f4 + jnp.where(ez < 7, pltpu.roll(f0, 127, 1), 0.0)
                force[c, b * 8 : b * 8 + 8, :] = n0
                force[c, 160 + b * 8 : 168 + b * 8, :] = n4
            for d in range(5):
                f0 = force[c, d * 40 : d * 40 + 8, :]
                f4 = force[c, d * 40 + 32 : d * 40 + 40, :]
                n0 = f0 + jnp.where(ey > 0, pltpu.roll(f4, 8, 1), 0.0)
                n4 = f4 + jnp.where(ey < 7, pltpu.roll(f0, 120, 1), 0.0)
                force[c, d * 40 : d * 40 + 8, :] = n0
                force[c, d * 40 + 32 : d * 40 + 40, :] = n4
            own_face[c] = jnp.where(low25, force[c, face0, :], force[c, face4, :])
        f = [own_face[c] for c in range(3)]
        face_out[s, 0, 0] = jnp.where(low25, f[0], pltpu.roll(f[1], 64, 1))
        face_out[s, 0, 1] = f[2]
        face_out[s, 1, 0] = jnp.where(low25, pltpu.roll(f[0], 64, 1), f[1])
        face_out[s, 1, 1] = pltpu.roll(f[2], 64, 1)

    def face_copies(s):
        to_right = pltpu.make_async_remote_copy(
            src_ref=face_out.at[s, 1], dst_ref=face_left.at[s],
            send_sem=face_send.at[s, 0], recv_sem=face_recv.at[s, 0],
            device_id=right, device_id_type=MESH,
        )
        if s == STEPS - 1:
            return [to_right]
        to_left = pltpu.make_async_remote_copy(
            src_ref=face_out.at[s, 0], dst_ref=face_right.at[s],
            send_sem=face_send.at[s, 1], recv_sem=face_recv.at[s, 1],
            device_id=left, device_id_type=MESH,
        )
        return [to_right, to_left]

    def update_inside():
        for c in range(3):
            f0, f4 = force[c, face0, :], force[c, face4, :]
            force[c, face0, :] = f0 + jnp.where(low25, 0.0, pltpu.roll(f4, 64, 1))
            force[c, face4, :] = f4 + jnp.where(low25, pltpu.roll(f0, 64, 1), 0.0)
            base[c] = jnp.where(
                low25,
                2.0 * cur[c, face0, :] - pre[c, face0, :],
                2.0 * cur[c, face4, :] - pre[c, face4, :],
            )
        for i in range(UROWS // 16):
            at = slice(i * 16, i * 16 + 16)
            scale = inv[at, :]
            for c in range(3):
                u = cur[c, at, :]
                cur[c, at, :] = 2.0 * u - pre[c, at, :] + force[c, at, :] * scale
                pre[c, at, :] = u

    def update_ends(s):
        fl = [face_left[s, 0], pltpu.roll(face_left[s, 0], 64, 1), face_left[s, 1]]
        if s < STEPS - 1:
            fr = [
                pltpu.roll(face_right[s, 0], 64, 1), face_right[s, 0],
                pltpu.roll(face_right[s, 1], 64, 1),
            ]
        for c in range(3):
            got = jnp.where(low25, fl[c], fr[c]) if s < STEPS - 1 else fl[c]
            new = base[c] + (own_face[c] + got) * finv[...]
            cur[c, face0, :] = jnp.where(low25, new, cur[c, face0, :])
            if s < STEPS - 1:
                cur[c, face4, :] = jnp.where(low25, cur[c, face4, :], new)

    part_copies = []
    for s in range(STEPS):
        line = []
        for k in range(1, 8):
            to = lax.rem(sub + k, 8)
            line.append(
                pltpu.make_async_remote_copy(
                    src_ref=parts_out.at[s, to], dst_ref=parts_in.at[s, sub],
                    send_sem=part_send.at[s, k - 1], recv_sem=part_recv.at[s, k - 1],
                    device_id=(group, cuts, to), device_id_type=MESH,
                )
            )
        part_copies.append(line)

    def kernel_part(s):
        for mine in (1, 2):
            @pl.when(group == mine)
            def _():
                for part in range(3):
                    if s == STEPS - 1 or part != mine - 1:
                        far_copy(s, part, mine).wait_recv()

        for i in range(2):
            yi[i * 112 : i * 112 + 112, :] = fint[s, i].astype(F32)
        yb[...] = fbnd[s].astype(F32)
        for c in range(3):
            for a in range(1, 4):
                xs[c, pl.ds(a, NBR, stride=8), :] = yi[pl.ds(72 * c + a - 1, NBR, stride=4), :]
            mid = yi[pl.ds(72 * c + 3, NBR, stride=4), :]
            ends = yb[pl.ds(c, NBR, stride=3), :]
            xs[c, pl.ds(0, NBR, stride=8), :] = jnp.where(low18, ends, pltpu.roll(mid, 64, 1))
            xs[c, pl.ds(4, NBR, stride=8), :] = jnp.where(low18, mid, ends)
        for c in range(3):
            block = {}
            for d in range(4):
                for b in range(4):
                    at = (d * 4 + b) * 8
                    block[b, d] = xs[c, at : at + 8, :]
            zend, yend = xs[c, 128:136, :], xs[c, 136:144, :]
            for d in range(4):
                block[4, d] = jnp.where(
                    ey < 7, pltpu.roll(block[0, d], 120, 1), pltpu.roll(yend, 8 * (7 - d), 1)
                )
            for b in range(5):
                block[b, 4] = jnp.where(
                    ez < 7, pltpu.roll(block[b, 0], 127, 1), pltpu.roll(zend, 7 - b, 1)
                )
            line = [block[bd] for bd in BLOCKS] + [jnp.zeros((8, 128), F32)]
            for i in range(0, 26, 2):
                tile = jnp.concatenate(line[i : i + 2], axis=0).astype(BF16)
                for k in range(3):
                    at = k * UROWS + i * 8
                    frhs[at : at + 16, c * 128 : c * 128 + 128] = tile
        fgrad[...] = jnp.dot(gf_ref[...], frhs[...], preferred_element_type=F32)

        def rows(r, n):
            at = slice(r, r + n)

            def strain(get):
                g = [[get(c, j) for j in range(3)] for c in range(3)]
                diag = [g[0][0], g[1][1], g[2][2]]
                tr = diag[0] + diag[1] + diag[2]
                third = tr * (1.0 / 3.0)
                dev = [x - third for x in diag]
                shear = [g[0][1] + g[1][0], g[0][2] + g[2][0], g[1][2] + g[2][1]]
                return tr, dev, shear

            tr, dev, off = strain(
                lambda c, j: grad[s, j * 128 + r : j * 128 + r + n, c * 128 : c * 128 + 128]
            )
            trf, devf, offf = strain(
                lambda c, j: fgrad[j * 128 + r : j * 128 + r + n, c * 128 : c * 128 + 128]
            )
            m2 = 2.0 * mu_ref[at, :]
            kappa = lam_ref[at, :] + m2 * (1.0 / 3.0)
            kb[at, :] = (TIME_STEP * kappa * trf * tr).astype(BF16)
            prod = dev[0] * devf[0] + dev[1] * devf[1] + dev[2] * devf[2]
            cross = off[0] * offf[0] + off[1] * offf[1] + off[2] * offf[2]
            ks[at, :] = (TIME_STEP * m2 * (prod + 0.5 * cross)).astype(BF16)

        for i in range(7):
            rows(i * 16, 16)
        rows(112, 13)
        for i, ref in enumerate((kb, ks)):
            placed = lax.dot_general(
                sel[...], ref[...], (((1,), (1,)), ((), ())), preferred_element_type=F32
            ).astype(BF16)
            for t in range(8):
                parts_out[s, t, :, i * 128 : i * 128 + 128] = placed[t * 32 : t * 32 + 32, :]
        parts_in[s, sub] = parts_out[s, sub]
        for copy in part_copies[s]:
            copy.start()

    for i in range(5, 6):
        loads[i].wait()
    for s in range(STEPS):
        gradient(s)
        if s == 0:
            for load in loads[6:]:
                load.wait()
        stress(s)
        assemble(s)
        copies = face_copies(s)
        for copy in copies:
            copy.start()
        update_inside()
        if s < STEPS - 1:
            pack_far(s + 1, 0)
            relay(s)
            if s == 1:
                kernel_part(0)
        else:
            kernel_part(1)
            kernel_part(2)
        for copy in copies:
            copy.wait()
        update_ends(s)
        if s < STEPS - 1:
            pack_far(s + 1, 1)

    rest = jnp.zeros((104, 128), F32)
    for i in range(0, 25, 2):
        pair = BLOCKS[i : i + 2]
        blocks = []
        for c in range(3):
            both = []
            for b, d in pair:
                at = (d * 5 + b) * 8
                v = cur[c, at : at + 8, :]
                both.append(jnp.where(subl < 4, v, pltpu.roll(pltpu.roll(v, 64, 1), 4, 0)))
            second = both[-1]
            blocks.append(jnp.where(low, both[0], pltpu.roll(second, 64, 1)))
        turned = jnp.concatenate(blocks + [rest], axis=0).T
        for h, (b, d) in enumerate(pair):
            for y in range(8):
                tee[pl.ds(132 * y + 33 * b + d, 8, stride=4), :] = turned[
                    h * 64 + y * 8 : h * 64 + y * 8 + 8, :
                ]
    for i in range(9):
        block = tee[i * 128 : i * 128 + 128, :].T
        width = min(128, 1089 - i * 128)
        for c in range(3):
            disp_ref[0, c, :, i * 128 : i * 128 + width] = block[c * 8 : c * 8 + 8, 0:width]

    @pl.when(group == 0)
    def _():
        for s in range(STEPS):
            for part, k in direct(s, (0, 1, 2)):
                far_copy(s, part, k).wait_send()

    for mine in (1, 2):
        @pl.when(group == mine)
        def _():
            for s in range(STEPS - 1):
                far_copy(s, mine - 1, 3 - mine).wait_send()

    for s in range(STEPS):
        for copy in part_copies[s]:
            copy.wait()
    for i in range(2):
        cols = slice(i * 128, i * 128 + 128)
        for h in range(2):
            quarter = []
            for t in range(h * 4, h * 4 + 4):
                total = parts_in[0, t, :, cols].astype(F32)
                for s in range(1, STEPS):
                    total = total + parts_in[s, t, :, cols].astype(F32)
                quarter.append(total)
            turned = jnp.concatenate(quarter, axis=0).T
            ker_ref[i * 125 : i * 125 + 125, h * 128 : h * 128 + 128] = turned[0:125, :]


def per_device(consts, now, prev, mem, dens, lam, mu, dec, own):
    vmem = pl.BlockSpec(memory_space=pltpu.VMEM)
    hbm = pl.BlockSpec(memory_space=pltpu.HBM)
    dma = pltpu.SemaphoreType.DMA
    mem = jnp.transpose(mem, (1, 2, 3, 0, 4))
    own = jnp.transpose(own, (0, 2, 1))
    disp, kers = pl.pallas_call(
        kernel,
        out_shape=(
            jax.ShapeDtypeStruct((1, 3, 8, 1089), F32),
            jax.ShapeDtypeStruct((250, 256), F32),
        ),
        in_specs=[hbm] * 12,
        out_specs=(vmem, vmem),
        scratch_shapes=[
            pltpu.VMEM((384, GK), BF16),
            pltpu.VMEM((384, 3 * UROWS), BF16),
            pltpu.VMEM((UROWS, 1152), BF16),
            pltpu.VMEM((UROWS, 128), F32),
            pltpu.VMEM((1, 3, 8, 1089), F32),
            pltpu.VMEM((1, 3, 8, 1089), F32),
            pltpu.VMEM((3, 5, 125, 128), F32),
            pltpu.VMEM((8, 1089), F32),
            pltpu.VMEM((125, 128), F32),
            pltpu.VMEM((125, 128), F32),
            pltpu.VMEM((3, 128), F32),
            pltpu.VMEM((2, 1, 64), jnp.int32),
            pltpu.VMEM((8, 128), jnp.int32),
            dma((26,)),
            pltpu.VMEM((56, 128), F32),
            pltpu.VMEM((1152, 128), F32),
            pltpu.VMEM((3, UROWS, 128), F32),
            pltpu.VMEM((3, UROWS, 128), F32),
            pltpu.VMEM((UROWS, 128), F32),
            pltpu.VMEM((GK, 384), BF16),
            pltpu.VMEM((STEPS, 384, 384), F32),
            pltpu.VMEM((1152, 384), BF16),
            pltpu.VMEM((3, UROWS, 128), F32),
            pltpu.VMEM((3, 25, 128), F32),
            pltpu.VMEM((25, 128), F32),
            pltpu.VMEM((3, 8 * NBR, 128), F32),
            pltpu.VMEM((224, 128), F32),
            pltpu.VMEM((64, 128), F32),
            pltpu.VMEM((STEPS, 2, 112, 128), BF16),
            pltpu.VMEM((STEPS, 64, 128), BF16),
            pltpu.VMEM((3 * UROWS, 384), BF16),
            pltpu.VMEM((384, 384), F32),
            pltpu.VMEM((128, 128), BF16),
            pltpu.VMEM((128, 128), BF16),
            pltpu.VMEM((256, 128), BF16),
            pltpu.VMEM((4, 25, 128), F32),
            pltpu.VMEM((4, 25, 128), F32),
            pltpu.VMEM((3, 25, 128), F32),
            pltpu.VMEM((STEPS, 2, 2, 25, 128), F32),
            pltpu.VMEM((STEPS, 2, 25, 128), F32),
            pltpu.VMEM((STEPS, 2, 25, 128), F32),
            pltpu.VMEM((STEPS, 8, 32, 256), BF16),
            pltpu.VMEM((STEPS, 8, 32, 256), BF16),
            dma((2,)),
            dma((STEPS, 2)),
            dma((STEPS, 2)),
            dma((STEPS, 3, 2)),
            dma((STEPS, 3)),
            dma((STEPS, 7)),
            dma((STEPS, 7)),
        ],
        compiler_params=pltpu.CompilerParams(
            collective_id=0, has_side_effects=True
        ),
        name="wavefields",
    )(*consts, now, prev, mem, dens, lam, mu, dec, own)
    return disp, jnp.transpose(kers.reshape(250, 1, 256), (1, 2, 0))


def solution(mesh):
    consts = tuple(jnp.asarray(t) for t in tables())
    in_specs = (
        P("group", None, ("cuts", "sub"), None),
        P("group", None, ("cuts", "sub"), None),
        P("group", None, None, None, ("cuts", "sub")),
        P(("cuts", "sub"), None),
        P(None, ("cuts", "sub")),
        P(None, ("cuts", "sub")),
        P(None, ("cuts", "sub")),
        P(("cuts", "sub"), None, None),
    )
    out_specs = (P("group", None, ("cuts", "sub"), None), P("group", ("cuts", "sub"), None))
    return jax.shard_map(
        functools.partial(per_device, consts),
        mesh=mesh, in_specs=in_specs, out_specs=out_specs, check_vma=False,
    )
```

```python
import functools
import math

import jax
import jax.numpy as jnp
import numpy as np
from jax import lax
from jax.experimental import pallas as pl
from jax.experimental.pallas import tpu as pltpu
from jax.sharding import PartitionSpec as P

STEPS = 3
TIME_STEP = 0.03
STEP_SQUARE = 0.0009
RELAX = (0.12, 0.08, 0.05)
F32 = jnp.float32
BF16 = jnp.bfloat16
MESH = pl.DeviceIdType.MESH

BLOCKS = [(b, d) for d in range(5) for b in range(5)]
UROWS = 208
GK = 1280
NBR = 18


def gll():
    root = math.sqrt(3.0 / 7.0)
    x = [-1.0, -root, 0.0, root, 1.0]
    w = np.array([0.1, 49.0 / 90.0, 32.0 / 45.0, 49.0 / 90.0, 0.1])
    der = np.zeros((5, 5))
    for p in range(5):
        for a in range(5):
            acc = 0.0
            for m in range(5):
                if m != a:
                    fac = 1.0 / (x[a] - x[m])
                    for k in range(5):
                        if k != a and k != m:
                            fac = fac * (x[p] - x[k]) / (x[a] - x[k])
                    acc = acc + fac
            der[p, a] = acc
    return der.astype(np.float32).astype(np.float64), w.astype(np.float32).astype(np.float64)


def pieces(mat, count):
    out = []
    rest = mat.astype(np.float64)
    for _ in range(count):
        part = rest.astype(jnp.bfloat16)
        out.append(part)
        rest = rest - part.astype(np.float64)
    return out


def tables():
    der, w = gll()
    grad = np.zeros((384, UROWS))
    force = np.zeros((UROWS, 384))

    def row(a, b, d):
        return (d * 5 + b) * 8 + a

    for a in range(5):
        for b in range(5):
            for d in range(5):
                r = row(a, b, d)
                for p in range(5):
                    for j, q in enumerate(((p, b, d), (a, p, d), (a, b, p))):
                        n = j * 128 + q[0] * 25 + q[1] * 5 + q[2]
                        at = (a, b, d)[j]
                        grad[n, r] = der[p, at]
                        force[r, n] = -der[p, at] * w[q[0]] * w[q[1]] * w[q[2]]
    g = pieces(grad, 3)
    gm = np.zeros((384, GK), jnp.bfloat16)
    for i, k in enumerate((0, 0, 0, 1, 1, 2)):
        gm[:, i * UROWS : (i + 1) * UROWS] = g[k]
    gf = np.concatenate(g, axis=1)
    f = pieces(force, 2)
    fm = np.concatenate([f[k] for k in (0, 0, 1)], axis=1)
    ends = [row(4, b, d) for b, d in BLOCKS]
    gmg = np.zeros((384, 192), jnp.bfloat16)
    for i, k in enumerate((0, 0, 0, 1, 1, 2)):
        gmg[:, i * 32 : i * 32 + 25] = g[k][:, ends]
    fmg = np.zeros((32, 1152), jnp.bfloat16)
    fmg[0:25] = fm[ends]
    weight = np.ones((UROWS, 128))
    for a in range(5):
        for b in range(5):
            for d in range(5):
                for e in range(128):
                    ey, ez = (e // 8) % 8, e % 8
                    wx = w[0] + w[4] if a in (0, 4) else w[a]
                    wy = w[b] + (w[0] if (b == 4 and ey < 7) or (b == 0 and ey > 0) else 0.0)
                    wz = w[d] + (w[0] if (d == 4 and ez < 7) or (d == 0 and ez > 0) else 0.0)
                    weight[row(a, b, d), e] = wx * wy * wz
    return gm, gf, fm, (weight / STEP_SQUARE).astype(np.float32), gmg, fmg


def split3(x):
    x1 = x.astype(BF16)
    r1 = x - x1.astype(F32)
    x2 = r1.astype(BF16)
    x3 = (r1 - x2.astype(F32)).astype(BF16)
    return x1, x2, x3


def kernel(
    gm_hbm, gf_hbm, fm_hbm, wt_hbm, gmg_hbm, fmg_hbm,
    now_hbm, prev_hbm, mem_hbm, dens_hbm, lam_hbm, mu_hbm, dec_hbm, own_hbm,
    disp_hbm, ker_hbm,
    disp, kers, out_sem, gmg_ref, fmg_ref, ghost_sem, ghost_out, ghost_in, ghost_f,
    gm_ref, gf_ref, fm_ref, wt_ref, now_ref, prev_ref, mem, dens_ref, lam_ref, mu_ref,
    dec_ref, own_ref, own_row, load_sem,
    last, tee, cur, pre, inv, urhs, grad, srhs, force, base, finv, xs, yi, yb, fint, fbnd,
    frhs, fgrad, kb, ks, sel,
    halo_out, halo_in, own_face, face_out, face_left, face_right, parts_out, parts_in,
    halo_sem, face_send, face_recv, far_send, far_recv, part_send, part_recv,
):
    loads = [
        pltpu.make_async_copy(src, dst, load_sem.at[i])
        for i, (src, dst) in enumerate(
            (
                (now_hbm, now_ref), (prev_hbm, prev_ref), (dens_hbm, dens_ref),
                (wt_hbm, wt_ref), (own_hbm, own_ref), (gm_hbm, gm_ref),
                (dec_hbm, dec_ref), (lam_hbm, lam_ref), (mu_hbm, mu_ref),
                (fm_hbm, fm_ref), (gf_hbm, gf_ref), (gmg_hbm, gmg_ref), (fmg_hbm, fmg_ref),
            )
        )
    ]
    for l in range(3):
        for k in range(5):
            loads.append(
                pltpu.make_async_copy(
                    mem_hbm.at[l, k, :, 0, :], mem.at[l, k], load_sem.at[len(loads)]
                )
            )
    for load in loads:
        load.start()

    group = lax.axis_index("group")
    cuts = lax.axis_index("cuts")
    sub = lax.axis_index("sub")
    flat = cuts * 8 + sub
    ring = lax.axis_size("cuts") * 8
    nxt = lax.rem(flat + 1, ring)
    prv = lax.rem(flat + ring - 1, ring)
    right = (group, lax.div(nxt, 8), lax.rem(nxt, 8))
    left = (group, lax.div(prv, 8), lax.rem(prv, 8))

    barrier = pltpu.get_barrier_semaphore()
    for dev in (left, right):
        pl.semaphore_signal(barrier, inc=1, device_id=dev, device_id_type=MESH)
    for k in range(1, 3):
        pl.semaphore_signal(
            barrier, inc=1, device_id=(lax.rem(group + k, 3), cuts, sub), device_id_type=MESH
        )
    for k in range(1, 8):
        pl.semaphore_signal(
            barrier, inc=1, device_id=(group, cuts, lax.rem(sub + k, 8)), device_id_type=MESH
        )

    lane = lax.broadcasted_iota(jnp.int32, (8, 128), 1)
    subl = lax.broadcasted_iota(jnp.int32, (8, 128), 0)
    low = lane < 64
    ez = lax.rem(lane, 8)
    ey = lax.rem(lax.div(lane, 8), 8)
    low25 = lax.broadcasted_iota(jnp.int32, (25, 128), 1) < 64
    low18 = lax.broadcasted_iota(jnp.int32, (NBR, 128), 1) < 64
    face0, face4 = pl.ds(0, 25, stride=8), pl.ds(4, 25, stride=8)

    for i in range(3):
        loads[i].wait()
    last[...] = jnp.zeros((56, 128), F32)
    for c in range(3):
        last[c * 8 : c * 8 + 8, 0:65] = now_ref[0, c, :, 1024:1089]
        last[24 + c * 8 : 32 + c * 8, 0:65] = prev_ref[0, c, :, 1024:1089]
    last[48:56, 0:65] = dens_ref[:, 1024:1089]
    rest = jnp.zeros((72, 128), F32)
    for i in range(9):
        if i < 8:
            at = slice(i * 128, i * 128 + 128)
            stack = [now_ref[0, c, :, at] for c in range(3)]
            stack += [prev_ref[0, c, :, at] for c in range(3)] + [dens_ref[:, at], rest]
        else:
            stack = [last[...], rest]
        tee[i * 128 : i * 128 + 128, :] = jnp.concatenate(stack, axis=0).T
    for i in range(0, 25, 2):
        pair = BLOCKS[i : i + 2]
        rows = []
        for b, d in (pair + pair)[:2]:
            for y in range(8):
                rows.append(tee[pl.ds(132 * y + 33 * b + d, 8, stride=4), :])
        turned = jnp.concatenate(rows, axis=0).T
        for h, (b, d) in enumerate(pair):
            at = (d * 5 + b) * 8
            for q in range(7):
                v = turned[q * 8 : q * 8 + 8, :]
                swapped = pltpu.roll(v, 64, 1)
                if h == 0:
                    val = jnp.where(low, v, pltpu.roll(swapped, 4, 0))
                else:
                    val = jnp.where(low, swapped, pltpu.roll(v, 4, 0))
                if q < 3:
                    cur[q, at : at + 8, :] = val
                elif q < 6:
                    pre[q - 3, at : at + 8, :] = val
                else:
                    inv[at : at + 8, :] = val
    cur[:, 200:208, :] = jnp.zeros((3, 8, 128), F32)
    pre[:, 200:208, :] = jnp.zeros((3, 8, 128), F32)
    inv[200:208, :] = jnp.ones((8, 128), F32)
    for c in range(3):
        halo_out[c] = jnp.where(
            low25, cur[c, face0, :], pltpu.roll(pre[c, face0, :], 64, 1)
        )
    halo_out[3] = inv[face0, :]
    def far_copy(s, part, k):
        buf = fbnd.at[s] if part == 2 else fint.at[s, part]
        return pltpu.make_async_remote_copy(
            src_ref=buf, dst_ref=buf,
            send_sem=far_send.at[s, part, k - 1], recv_sem=far_recv.at[s, part],
            device_id=(k, cuts, sub), device_id_type=MESH,
        )

    def direct(s, parts):
        return [
            (part, k)
            for part in parts
            for k in (1, 2)
            if part == 2 or s == STEPS - 1 or k == part + 1
        ]

    def relay(s):
        for mine in (1, 2):
            @pl.when(group == mine)
            def _():
                far_copy(s, mine - 1, mine).wait_recv()
                far_copy(s, mine - 1, 3 - mine).start()

    def pack_far(s, part):
        @pl.when(group == 0)
        def _():
            for c in range(3):
                for d in range(4):
                    for b in range(4):
                        to = (d * 4 + b) * 8
                        xs[c, to : to + 8, :] = cur[c, (d * 5 + b) * 8 : (d * 5 + b) * 8 + 8, :]
                ends = cur[c, 192:200, :]
                for b in range(4):
                    moved = pltpu.roll(cur[c, 160 + b * 8 : 168 + b * 8, :], 121 + b, 1)
                    ends = jnp.where(ez == b, moved, ends) if b else jnp.where(
                        ez == b, moved, pltpu.roll(ends, 125, 1)
                    )
                xs[c, 128:136, :] = ends
                ends = pltpu.roll(cur[c, 32:40, :], 72, 1)
                for d in range(1, 4):
                    moved = pltpu.roll(cur[c, d * 40 + 32 : d * 40 + 40, :], 72 + 8 * d, 1)
                    ends = jnp.where(ey == d, moved, ends)
                xs[c, 136:144, :] = ends
                if part == 0:
                    for a in range(1, 5):
                        yi[pl.ds(72 * c + a - 1, NBR, stride=4), :] = xs[
                            c, pl.ds(a, NBR, stride=8), :
                        ]
                else:
                    yb[pl.ds(c, NBR, stride=3), :] = jnp.where(
                        low18, xs[c, pl.ds(0, NBR, stride=8), :], xs[c, pl.ds(4, NBR, stride=8), :]
                    )
            if part == 0:
                for i in range(2):
                    fint[s, i] = yi[i * 112 : i * 112 + 112, :].astype(BF16)
            else:
                fbnd[s] = yb[...].astype(BF16)
            for piece, k in direct(s, (0, 1) if part == 0 else (2,)):
                far_copy(s, piece, k).start()

    def gradient(s):
        for i in range(UROWS // 16):
            for c in range(3):
                u1, u2, u3 = split3(cur[c, i * 16 : i * 16 + 16, :])
                for k, part in enumerate((u1, u2, u3, u1, u2, u1)):
                    at = k * UROWS + i * 16
                    urhs[at : at + 16, c * 128 : c * 128 + 128] = part
        grad[s] = jnp.dot(gm_ref[...], urhs[...], preferred_element_type=F32)

    def stress_rows(get, lam, mu, relax, r, n):
        g = [[get(c, j) for j in range(3)] for c in range(3)]
        exx, eyy, ezz = g[0][0], g[1][1], g[2][2]
        exy = 0.5 * (g[0][1] + g[1][0])
        exz = 0.5 * (g[0][2] + g[2][0])
        eyz = 0.5 * (g[1][2] + g[2][1])
        tr = exx + eyy + ezz
        third = tr * (1.0 / 3.0)
        m2 = 2.0 * mu
        sxy, sxz, syz = m2 * exy, m2 * exz, m2 * eyz
        dev = [m2 * (exx - third), m2 * (eyy - third), sxy, sxz, syz]
        total = relax(dev)
        bulk = lam * tr
        sxx = bulk + m2 * exx - total[0]
        syy = bulk + m2 * eyy - total[1]
        szz = bulk + m2 * ezz + (total[0] + total[1])
        places = (
            (sxx, ((0, 0),)), (syy, ((1, 1),)), (szz, ((2, 2),)),
            (sxy - total[2], ((0, 1), (1, 0))), (sxz - total[3], ((0, 2), (2, 0))),
            (syz - total[4], ((1, 2), (2, 1))),
        )
        for val, where in places:
            p1 = val.astype(BF16)
            p2 = (val - p1.astype(F32)).astype(BF16)
            for k, part in enumerate((p1, p2, p1)):
                for c, j in where:
                    to = k * 384 + j * 128 + r
                    srhs[to : to + n, c * 128 : c * 128 + 128] = part

    chunks = [(i * 16, 16) for i in range(7)] + [(112, 13)]

    def stress(s, keep):
        gains = [(1.0 - dec_ref[l : l + 1, :]) * RELAX[l] for l in range(3)]
        for r, n in chunks:
            at = slice(r, r + n)

            def relax(dev):
                total = [None] * 5
                for k in range(5):
                    for l in range(3):
                        new = dec_ref[l : l + 1, :] * mem[l, k, at, :] + gains[l] * dev[k]
                        if keep:
                            mem[l, k, at, :] = new
                        total[k] = new if total[k] is None else total[k] + new
                return total

            stress_rows(
                lambda c, j: grad[s, j * 128 + r : j * 128 + r + n, c * 128 : c * 128 + 128],
                lam_ref[at, :], mu_ref[at, :], relax, r, n,
            )
        out = jnp.dot(fm_ref[...], srhs[...], preferred_element_type=F32)
        for c in range(3):
            force[c] = out[:, c * 128 : c * 128 + 128]

    def ghost_force():
        for c in range(3):
            u = jnp.where(low25, pre[c, face0, :], 0.0)
            u1, u2, u3 = split3(u)
            for k, part in enumerate((u1, u2, u3, u1, u2, u1)):
                urhs[k * 32 : k * 32 + 25, c * 128 : c * 128 + 128] = part
                urhs[k * 32 + 25 : k * 32 + 32, c * 128 : c * 128 + 128] = jnp.zeros(
                    (7, 128), BF16
                )
        fgrad[...] = jnp.dot(gmg_ref[...], urhs[0:192, :], preferred_element_type=F32)
        gain = ghost_in[125:126, :]
        for r, n in chunks:
            both = ghost_in[r : r + n, :]
            stress_rows(
                lambda c, j: fgrad[j * 128 + r : j * 128 + r + n, c * 128 : c * 128 + 128],
                both, pltpu.roll(both, 64, 1), lambda dev: [gain * x for x in dev], r, n,
            )
        out = jnp.dot(fmg_ref[...], srhs[...], preferred_element_type=F32)
        ez5, ey5 = ez[0:5], ey[0:5]
        for c in range(3):
            ghost_f[c] = out[:, c * 128 : c * 128 + 128]
            f0, f4 = ghost_f[c, 0:5, :], ghost_f[c, 20:25, :]
            ghost_f[c, 0:5, :] = f0 + jnp.where(ez5 > 0, pltpu.roll(f4, 1, 1), 0.0)
            ghost_f[c, 20:25, :] = f4 + jnp.where(ez5 < 7, pltpu.roll(f0, 127, 1), 0.0)
            b0, b4 = pl.ds(0, 5, stride=5), pl.ds(4, 5, stride=5)
            f0, f4 = ghost_f[c, b0, :], ghost_f[c, b4, :]
            ghost_f[c, b0, :] = f0 + jnp.where(ey5 > 0, pltpu.roll(f4, 8, 1), 0.0)
            ghost_f[c, b4, :] = f4 + jnp.where(ey5 < 7, pltpu.roll(f0, 120, 1), 0.0)

    def assemble(s):
        for c in range(3):
            for b in range(5):
                f0 = force[c, b * 8 : b * 8 + 8, :]
                f4 = force[c, 160 + b * 8 : 168 + b * 8, :]
                n0 = f0 + jnp.where(ez > 0, pltpu.roll(f4, 1, 1), 0.0)
                n4 = f4 + jnp.where(ez < 7, pltpu.roll(f0, 127, 1), 0.0)
                force[c, b * 8 : b * 8 + 8, :] = n0
                force[c, 160 + b * 8 : 168 + b * 8, :] = n4
            for d in range(5):
                f0 = force[c, d * 40 : d * 40 + 8, :]
                f4 = force[c, d * 40 + 32 : d * 40 + 40, :]
                n0 = f0 + jnp.where(ey > 0, pltpu.roll(f4, 8, 1), 0.0)
                n4 = f4 + jnp.where(ey < 7, pltpu.roll(f0, 120, 1), 0.0)
                force[c, d * 40 : d * 40 + 8, :] = n0
                force[c, d * 40 + 32 : d * 40 + 40, :] = n4
            own_face[c] = jnp.where(low25, force[c, face0, :], force[c, face4, :])

    def pack_faces(s):
        f = [own_face[c] for c in range(3)]
        face_out[s, 0, 0] = jnp.where(low25, f[0], pltpu.roll(f[1], 64, 1))
        face_out[s, 0, 1] = f[2]
        face_out[s, 1, 0] = jnp.where(low25, pltpu.roll(f[0], 64, 1), f[1])
        face_out[s, 1, 1] = pltpu.roll(f[2], 64, 1)

    def face_copies(s):
        to_right = pltpu.make_async_remote_copy(
            src_ref=face_out.at[s, 1], dst_ref=face_left.at[s],
            send_sem=face_send.at[s, 0], recv_sem=face_recv.at[s, 0],
            device_id=right, device_id_type=MESH,
        )
        if s == STEPS - 1:
            return [to_right]
        to_left = pltpu.make_async_remote_copy(
            src_ref=face_out.at[s, 0], dst_ref=face_right.at[s],
            send_sem=face_send.at[s, 1], recv_sem=face_recv.at[s, 1],
            device_id=left, device_id_type=MESH,
        )
        return [to_right, to_left]

    def update_inside():
        for c in range(3):
            f0, f4 = force[c, face0, :], force[c, face4, :]
            force[c, face0, :] = f0 + jnp.where(low25, 0.0, pltpu.roll(f4, 64, 1))
            force[c, face4, :] = f4 + jnp.where(low25, pltpu.roll(f0, 64, 1), 0.0)
            base[c] = jnp.where(
                low25,
                2.0 * cur[c, face0, :] - pre[c, face0, :],
                2.0 * cur[c, face4, :] - pre[c, face4, :],
            )
        for i in range(UROWS // 16):
            at = slice(i * 16, i * 16 + 16)
            scale = inv[at, :]
            for c in range(3):
                u = cur[c, at, :]
                cur[c, at, :] = 2.0 * u - pre[c, at, :] + force[c, at, :] * scale
                pre[c, at, :] = u

    def update_ends(s):
        fl = [face_left[s, 0], pltpu.roll(face_left[s, 0], 64, 1), face_left[s, 1]]
        if s == 0:
            fl = [fl[c] + ghost_f[c, 0:25, :] for c in range(3)]
        if s < STEPS - 1:
            fr = [
                pltpu.roll(face_right[s, 0], 64, 1), face_right[s, 0],
                pltpu.roll(face_right[s, 1], 64, 1),
            ]
        for c in range(3):
            got = jnp.where(low25, fl[c], fr[c]) if s < STEPS - 1 else fl[c]
            new = base[c] + (own_face[c] + got) * finv[...]
            cur[c, face0, :] = jnp.where(low25, new, cur[c, face0, :])
            if s < STEPS - 1:
                cur[c, face4, :] = jnp.where(low25, cur[c, face4, :], new)

    part_copies = []
    for s in range(STEPS):
        line = []
        for k in range(1, 8):
            to = lax.rem(sub + k, 8)
            line.append(
                pltpu.make_async_remote_copy(
                    src_ref=parts_out.at[s, to], dst_ref=parts_in.at[s, sub],
                    send_sem=part_send.at[s, k - 1], recv_sem=part_recv.at[s, k - 1],
                    device_id=(group, cuts, to), device_id_type=MESH,
                )
            )
        part_copies.append(line)

    def kernel_part(s):
        for mine in (1, 2):
            @pl.when(group == mine)
            def _():
                for part in range(3):
                    if s == STEPS - 1 or part != mine - 1:
                        far_copy(s, part, mine).wait_recv()

        for i in range(2):
            yi[i * 112 : i * 112 + 112, :] = fint[s, i].astype(F32)
        yb[...] = fbnd[s].astype(F32)
        for c in range(3):
            for a in range(1, 4):
                xs[c, pl.ds(a, NBR, stride=8), :] = yi[pl.ds(72 * c + a - 1, NBR, stride=4), :]
            mid = yi[pl.ds(72 * c + 3, NBR, stride=4), :]
            ends = yb[pl.ds(c, NBR, stride=3), :]
            xs[c, pl.ds(0, NBR, stride=8), :] = jnp.where(low18, ends, pltpu.roll(mid, 64, 1))
            xs[c, pl.ds(4, NBR, stride=8), :] = jnp.where(low18, mid, ends)
        for c in range(3):
            block = {}
            for d in range(4):
                for b in range(4):
                    at = (d * 4 + b) * 8
                    block[b, d] = xs[c, at : at + 8, :]
            zend, yend = xs[c, 128:136, :], xs[c, 136:144, :]
            for d in range(4):
                block[4, d] = jnp.where(
                    ey < 7, pltpu.roll(block[0, d], 120, 1), pltpu.roll(yend, 8 * (7 - d), 1)
                )
            for b in range(5):
                block[b, 4] = jnp.where(
                    ez < 7, pltpu.roll(block[b, 0], 127, 1), pltpu.roll(zend, 7 - b, 1)
                )
            line = [block[bd] for bd in BLOCKS] + [jnp.zeros((8, 128), F32)]
            for i in range(0, 26, 2):
                tile = jnp.concatenate(line[i : i + 2], axis=0).astype(BF16)
                for k in range(3):
                    at = k * UROWS + i * 8
                    frhs[at : at + 16, c * 128 : c * 128 + 128] = tile
        fgrad[...] = jnp.dot(gf_ref[...], frhs[...], preferred_element_type=F32)

        def rows(r, n):
            at = slice(r, r + n)

            def strain(get):
                g = [[get(c, j) for j in range(3)] for c in range(3)]
                diag = [g[0][0], g[1][1], g[2][2]]
                tr = diag[0] + diag[1] + diag[2]
                third = tr * (1.0 / 3.0)
                dev = [x - third for x in diag]
                shear = [g[0][1] + g[1][0], g[0][2] + g[2][0], g[1][2] + g[2][1]]
                return tr, dev, shear

            tr, dev, off = strain(
                lambda c, j: grad[s, j * 128 + r : j * 128 + r + n, c * 128 : c * 128 + 128]
            )
            trf, devf, offf = strain(
                lambda c, j: fgrad[j * 128 + r : j * 128 + r + n, c * 128 : c * 128 + 128]
            )
            m2 = 2.0 * mu_ref[at, :]
            kappa = lam_ref[at, :] + m2 * (1.0 / 3.0)
            kb[at, :] = (TIME_STEP * kappa * trf * tr).astype(BF16)
            prod = dev[0] * devf[0] + dev[1] * devf[1] + dev[2] * devf[2]
            cross = off[0] * offf[0] + off[1] * offf[1] + off[2] * offf[2]
            ks[at, :] = (TIME_STEP * m2 * (prod + 0.5 * cross)).astype(BF16)

        for i in range(7):
            rows(i * 16, 16)
        rows(112, 13)
        for i, ref in enumerate((kb, ks)):
            placed = lax.dot_general(
                sel[...], ref[...], (((1,), (1,)), ((), ())), preferred_element_type=F32
            ).astype(BF16)
            for t in range(8):
                parts_out[s, t, :, i * 128 : i * 128 + 128] = placed[t * 32 : t * 32 + 32, :]
        parts_in[s, sub] = parts_out[s, sub]
        for copy in part_copies[s]:
            copy.start()

    urhs[1248:1280, :] = jnp.zeros((32, 384), BF16)
    zeros16 = jnp.zeros((16, 384), BF16)
    for i in range(9):
        srhs[i * 128 + 112 : i * 128 + 128, :] = zeros16
    kb[112:128, :] = jnp.zeros((16, 128), BF16)
    ks[112:128, :] = jnp.zeros((16, 128), BF16)

    yi[216:224, :] = jnp.zeros((8, 128), F32)
    yb[48:64, :] = jnp.zeros((16, 128), F32)
    xs[...] = jnp.zeros((3, 8 * NBR, 128), F32)
    for c in range(3):
        cur[c, face4, :] = jnp.where(low25, cur[c, face4, :], 0.0)
    loads[5].wait()
    gradient(0)
    for load in loads[6:]:
        load.wait()
    gain = (1.0 - dec_ref[0:1, :]) * RELAX[0]
    for l in (1, 2):
        gain = gain + (1.0 - dec_ref[l : l + 1, :]) * RELAX[l]
    low_row = lax.broadcasted_iota(jnp.int32, (125, 128), 1) < 64
    ghost_out[0:125, :] = jnp.where(low_row, pltpu.roll(lam_ref[...], 64, 1), mu_ref[...])
    ghost_out[125:126, :] = pltpu.roll(jnp.broadcast_to(gain, (8, 128)), 64, 1)[0:1]
    stress(0, False)
    assemble(0)
    pack_faces(0)
    pl.semaphore_wait(barrier, 11)
    halo = pltpu.make_async_remote_copy(
        src_ref=halo_out, dst_ref=halo_in, send_sem=halo_sem.at[0], recv_sem=halo_sem.at[1],
        device_id=left, device_id_type=MESH,
    )
    halo.start()
    first_faces = face_copies(0)
    for copy in first_faces:
        copy.start()
    ghost = pltpu.make_async_remote_copy(
        src_ref=ghost_out, dst_ref=ghost_in, send_sem=ghost_sem.at[0], recv_sem=ghost_sem.at[1],
        device_id=right, device_id_type=MESH,
    )
    ghost.start()
    pack_far(0, 0)

    for i in range(3, 5):
        loads[i].wait()
    own_row[0:1, 0:64] = own_ref[0]
    own_row[0:1, 64:128] = own_ref[1]
    slot = lax.broadcasted_iota(jnp.int32, (256, 128), 0)
    elem = lax.broadcasted_iota(jnp.int32, (256, 128), 1)
    onehot = jnp.where(own_row[0:1, :] == lax.div(slot, 32), 1.0, 0.0)
    one = lax.broadcasted_iota(jnp.int32, (128, 128), 0)
    two = lax.broadcasted_iota(jnp.int32, (128, 128), 1)
    one_low, two_low = one < 64, two < 64
    earlier = jnp.where(one < two, jnp.where(two_low, 1.0, jnp.where(one_low, 0.0, 1.0)), 0.0)
    count = jnp.dot(onehot.astype(BF16), earlier.astype(BF16), preferred_element_type=F32)
    rank_hit = jnp.where(count == lax.rem(slot, 16).astype(F32), onehot, 0.0)
    mine = lax.rem(lax.div(slot, 16), 2) == lax.div(elem, 64)
    sel[...] = jnp.where(mine, rank_hit, 0.0).astype(BF16)
    halo.wait()
    for c in range(3):
        got = halo_in[c]
        cur[c, face4, :] = jnp.where(low25, cur[c, face4, :], pltpu.roll(got, 64, 1))
        pre[c, face4, :] = jnp.where(low25, pre[c, face4, :], got)
    inv[face4, :] = jnp.where(low25, inv[face4, :], pltpu.roll(halo_in[3], 64, 1))
    pack_far(0, 1)
    inv[...] = 1.0 / (inv[...] * wt_ref[...])
    finv[...] = jnp.where(low25, inv[face0, :], inv[face4, :])

    for s in range(STEPS):
        gradient(s)
        stress(s, s < STEPS - 1)
        assemble(s)
        if s == 0:
            copies = first_faces
        else:
            pack_faces(s)
            copies = face_copies(s)
            for copy in copies:
                copy.start()
        update_inside()
        if s < STEPS - 1:
            pack_far(s + 1, 0)
            if s == 0:
                ghost.wait()
                ghost_force()
            relay(s)
            if s == 1:
                kernel_part(0)
        else:
            kernel_part(1)
            kernel_part(2)
        for copy in copies:
            copy.wait()
        update_ends(s)
        if s < STEPS - 1:
            pack_far(s + 1, 1)

    rest = jnp.zeros((104, 128), F32)
    for i in range(0, 25, 2):
        pair = BLOCKS[i : i + 2]
        blocks = []
        for c in range(3):
            both = []
            for b, d in pair:
                at = (d * 5 + b) * 8
                v = cur[c, at : at + 8, :]
                both.append(jnp.where(subl < 4, v, pltpu.roll(pltpu.roll(v, 64, 1), 4, 0)))
            second = both[-1]
            blocks.append(jnp.where(low, both[0], pltpu.roll(second, 64, 1)))
        turned = jnp.concatenate(blocks + [rest], axis=0).T
        for h, (b, d) in enumerate(pair):
            for y in range(8):
                tee[pl.ds(132 * y + 33 * b + d, 8, stride=4), :] = turned[
                    h * 64 + y * 8 : h * 64 + y * 8 + 8, :
                ]
    for i in range(9):
        block = tee[i * 128 : i * 128 + 128, :].T
        width = min(128, 1089 - i * 128)
        for c in range(3):
            disp[0, c, :, i * 128 : i * 128 + width] = block[c * 8 : c * 8 + 8, 0:width]
    disp_out = pltpu.make_async_copy(disp, disp_hbm, out_sem.at[0])
    disp_out.start()

    @pl.when(group == 0)
    def _():
        for s in range(STEPS):
            for part, k in direct(s, (0, 1, 2)):
                far_copy(s, part, k).wait_send()

    for mine in (1, 2):
        @pl.when(group == mine)
        def _():
            for s in range(STEPS - 1):
                far_copy(s, mine - 1, 3 - mine).wait_send()

    for s in range(STEPS):
        for copy in part_copies[s]:
            copy.wait()
    for i in range(2):
        cols = slice(i * 128, i * 128 + 128)
        for h in range(2):
            quarter = []
            for t in range(h * 4, h * 4 + 4):
                total = parts_in[0, t, :, cols].astype(F32)
                for s in range(1, STEPS):
                    total = total + parts_in[s, t, :, cols].astype(F32)
                quarter.append(total)
            turned = jnp.concatenate(quarter, axis=0).T
            kers[h, i * 125 : i * 125 + 125, :] = turned[0:125, :]
    ker_outs = [
        pltpu.make_async_copy(
            kers.at[h], ker_hbm.at[:, 0, pl.ds(h * 128, 128)], out_sem.at[1 + h]
        )
        for h in range(2)
    ]
    for out in ker_outs:
        out.start()
    for out in ker_outs:
        out.wait()
    disp_out.wait()


def per_device(consts, now, prev, mem, dens, lam, mu, dec, own):
    hbm = pl.BlockSpec(memory_space=pl.ANY)
    dma = pltpu.SemaphoreType.DMA
    mem = jnp.transpose(mem, (1, 2, 3, 0, 4))
    own = jnp.transpose(own, (0, 2, 1))
    disp, kers = pl.pallas_call(
        kernel,
        out_shape=(
            jax.ShapeDtypeStruct((1, 3, 8, 1089), F32),
            jax.ShapeDtypeStruct((250, 1, 256), F32),
        ),
        in_specs=[hbm] * 14,
        out_specs=(hbm, hbm),
        scratch_shapes=[
            pltpu.VMEM((1, 3, 8, 1089), F32),
            pltpu.VMEM((2, 250, 128), F32),
            dma((3,)),
            pltpu.VMEM((384, 192), BF16),
            pltpu.VMEM((32, 1152), BF16),
            dma((2,)),
            pltpu.VMEM((126, 128), F32),
            pltpu.VMEM((126, 128), F32),
            pltpu.VMEM((3, 32, 128), F32),
            pltpu.VMEM((384, GK), BF16),
            pltpu.VMEM((384, 3 * UROWS), BF16),
            pltpu.VMEM((UROWS, 1152), BF16),
            pltpu.VMEM((UROWS, 128), F32),
            pltpu.VMEM((1, 3, 8, 1089), F32),
            pltpu.VMEM((1, 3, 8, 1089), F32),
            pltpu.VMEM((3, 5, 125, 128), F32),
            pltpu.VMEM((8, 1089), F32),
            pltpu.VMEM((125, 128), F32),
            pltpu.VMEM((125, 128), F32),
            pltpu.VMEM((3, 128), F32),
            pltpu.VMEM((2, 1, 64), jnp.int32),
            pltpu.VMEM((8, 128), jnp.int32),
            dma((28,)),
            pltpu.VMEM((56, 128), F32),
            pltpu.VMEM((1152, 128), F32),
            pltpu.VMEM((3, UROWS, 128), F32),
            pltpu.VMEM((3, UROWS, 128), F32),
            pltpu.VMEM((UROWS, 128), F32),
            pltpu.VMEM((GK, 384), BF16),
            pltpu.VMEM((STEPS, 384, 384), F32),
            pltpu.VMEM((1152, 384), BF16),
            pltpu.VMEM((3, UROWS, 128), F32),
            pltpu.VMEM((3, 25, 128), F32),
            pltpu.VMEM((25, 128), F32),
            pltpu.VMEM((3, 8 * NBR, 128), F32),
            pltpu.VMEM((224, 128), F32),
            pltpu.VMEM((64, 128), F32),
            pltpu.VMEM((STEPS, 2, 112, 128), BF16),
            pltpu.VMEM((STEPS, 64, 128), BF16),
            pltpu.VMEM((3 * UROWS, 384), BF16),
            pltpu.VMEM((384, 384), F32),
            pltpu.VMEM((128, 128), BF16),
            pltpu.VMEM((128, 128), BF16),
            pltpu.VMEM((256, 128), BF16),
            pltpu.VMEM((4, 25, 128), F32),
            pltpu.VMEM((4, 25, 128), F32),
            pltpu.VMEM((3, 25, 128), F32),
            pltpu.VMEM((STEPS, 2, 2, 25, 128), F32),
            pltpu.VMEM((STEPS, 2, 25, 128), F32),
            pltpu.VMEM((STEPS, 2, 25, 128), F32),
            pltpu.VMEM((STEPS, 8, 32, 256), BF16),
            pltpu.VMEM((STEPS, 8, 32, 256), BF16),
            dma((2,)),
            dma((STEPS, 2)),
            dma((STEPS, 2)),
            dma((STEPS, 3, 2)),
            dma((STEPS, 3)),
            dma((STEPS, 7)),
            dma((STEPS, 7)),
        ],
        compiler_params=pltpu.CompilerParams(
            collective_id=0, has_side_effects=True
        ),
        name="wavefields",
    )(*consts, now, prev, mem, dens, lam, mu, dec, own)
    return disp, jnp.transpose(kers, (1, 2, 0))


def solution(mesh):
    consts = tuple(jnp.asarray(t) for t in tables())
    in_specs = (
        P("group", None, ("cuts", "sub"), None),
        P("group", None, ("cuts", "sub"), None),
        P("group", None, None, None, ("cuts", "sub")),
        P(("cuts", "sub"), None),
        P(None, ("cuts", "sub")),
        P(None, ("cuts", "sub")),
        P(None, ("cuts", "sub")),
        P(("cuts", "sub"), None, None),
    )
    out_specs = (P("group", None, ("cuts", "sub"), None), P("group", ("cuts", "sub"), None))
    return jax.shard_map(
        functools.partial(per_device, consts),
        mesh=mesh, in_specs=in_specs, out_specs=out_specs, check_vma=False,
    )
```

```python
import functools
import math

import jax
import jax.numpy as jnp
import numpy as np
from jax import lax
from jax.experimental import pallas as pl
from jax.experimental.pallas import tpu as pltpu
from jax.sharding import PartitionSpec as P

STEPS = 3
TIME_STEP = 0.03
STEP_SQUARE = 0.0009
RELAX = (0.12, 0.08, 0.05)
F32 = jnp.float32
BF16 = jnp.bfloat16
MESH = pl.DeviceIdType.MESH

BLOCKS = [(b, d) for d in range(5) for b in range(5)]
UROWS = 208
GK = 1280
NBR = 18


def gll():
    root = math.sqrt(3.0 / 7.0)
    x = [-1.0, -root, 0.0, root, 1.0]
    w = np.array([0.1, 49.0 / 90.0, 32.0 / 45.0, 49.0 / 90.0, 0.1])
    der = np.zeros((5, 5))
    for p in range(5):
        for a in range(5):
            acc = 0.0
            for m in range(5):
                if m != a:
                    fac = 1.0 / (x[a] - x[m])
                    for k in range(5):
                        if k != a and k != m:
                            fac = fac * (x[p] - x[k]) / (x[a] - x[k])
                    acc = acc + fac
            der[p, a] = acc
    return der.astype(np.float32).astype(np.float64), w.astype(np.float32).astype(np.float64)


def pieces(mat, count):
    out = []
    rest = mat.astype(np.float64)
    for _ in range(count):
        part = rest.astype(jnp.bfloat16)
        out.append(part)
        rest = rest - part.astype(np.float64)
    return out


def tables():
    der, w = gll()
    grad = np.zeros((384, UROWS))
    force = np.zeros((UROWS, 384))

    def row(a, b, d):
        return (d * 5 + b) * 8 + a

    for a in range(5):
        for b in range(5):
            for d in range(5):
                r = row(a, b, d)
                for p in range(5):
                    for j, q in enumerate(((p, b, d), (a, p, d), (a, b, p))):
                        n = j * 128 + q[0] * 25 + q[1] * 5 + q[2]
                        at = (a, b, d)[j]
                        grad[n, r] = der[p, at]
                        force[r, n] = -der[p, at] * w[q[0]] * w[q[1]] * w[q[2]]
    g = pieces(grad, 3)
    gm = np.zeros((384, GK), jnp.bfloat16)
    for i, k in enumerate((0, 0, 0, 1, 1, 2)):
        gm[:, i * UROWS : (i + 1) * UROWS] = g[k]
    gf = np.concatenate(g, axis=1)
    f = pieces(force, 2)
    fm = np.concatenate([f[k] for k in (0, 0, 1)], axis=1)
    ends = [row(4, b, d) for b, d in BLOCKS]
    gmg = np.zeros((384, 192), jnp.bfloat16)
    for i, k in enumerate((0, 0, 0, 1, 1, 2)):
        gmg[:, i * 32 : i * 32 + 25] = g[k][:, ends]
    weight = np.ones((UROWS, 128))
    for a in range(5):
        for b in range(5):
            for d in range(5):
                for e in range(128):
                    ey, ez = (e // 8) % 8, e % 8
                    wx = w[0] + w[4] if a in (0, 4) else w[a]
                    wy = w[b] + (w[0] if (b == 4 and ey < 7) or (b == 0 and ey > 0) else 0.0)
                    wz = w[d] + (w[0] if (d == 4 and ez < 7) or (d == 0 and ez > 0) else 0.0)
                    weight[row(a, b, d), e] = wx * wy * wz
    return gm, gf, fm, (weight / STEP_SQUARE).astype(np.float32), gmg


def split3(x):
    x1 = x.astype(BF16)
    r1 = x - x1.astype(F32)
    x2 = r1.astype(BF16)
    x3 = (r1 - x2.astype(F32)).astype(BF16)
    return x1, x2, x3


def kernel(
    gm_hbm, gf_hbm, fm_hbm, wt_hbm, gmg_hbm,
    now_hbm, prev_hbm, mem_hbm, dens_hbm, lam_hbm, mu_hbm, dec_hbm, own_hbm,
    disp_ref, ker_ref,
    gmg_ref, ghost_sem, ghost_out, ghost_in, added,
    gm_ref, gf_ref, fm_ref, wt_ref, now_ref, prev_ref, mem, dens_ref, lam_ref, mu_ref,
    dec_ref, own_ref, own_row, load_sem,
    last, tee, cur, pre, inv, urhs, grad, srhs, force, base, finv, xs, yi, yb, fint, fbnd,
    frhs, fgrad, kb, ks, sel,
    halo_out, halo_in, own_face, face_out, face_left, face_right, parts_out, parts_in,
    halo_sem, face_send, face_recv, far_send, far_recv, part_send, part_recv,
):
    loads = [
        pltpu.make_async_copy(src, dst, load_sem.at[i])
        for i, (src, dst) in enumerate(
            (
                (now_hbm, now_ref), (prev_hbm, prev_ref), (dens_hbm, dens_ref),
                (wt_hbm, wt_ref), (own_hbm, own_ref), (gm_hbm, gm_ref),
                (dec_hbm, dec_ref), (lam_hbm, lam_ref), (mu_hbm, mu_ref),
                (fm_hbm, fm_ref), (gf_hbm, gf_ref), (gmg_hbm, gmg_ref),
            )
        )
    ]
    for l in range(3):
        for k in range(5):
            loads.append(
                pltpu.make_async_copy(
                    mem_hbm.at[l, k, :, 0, :], mem.at[l, k], load_sem.at[len(loads)]
                )
            )
    for load in loads:
        load.start()

    group = lax.axis_index("group")
    cuts = lax.axis_index("cuts")
    sub = lax.axis_index("sub")
    flat = cuts * 8 + sub
    ring = lax.axis_size("cuts") * 8
    nxt = lax.rem(flat + 1, ring)
    prv = lax.rem(flat + ring - 1, ring)
    right = (group, lax.div(nxt, 8), lax.rem(nxt, 8))
    left = (group, lax.div(prv, 8), lax.rem(prv, 8))

    barrier = pltpu.get_barrier_semaphore()
    for dev in (left, right):
        pl.semaphore_signal(barrier, inc=1, device_id=dev, device_id_type=MESH)
    for k in range(1, 3):
        pl.semaphore_signal(
            barrier, inc=1, device_id=(lax.rem(group + k, 3), cuts, sub), device_id_type=MESH
        )
    for k in range(1, 8):
        pl.semaphore_signal(
            barrier, inc=1, device_id=(group, cuts, lax.rem(sub + k, 8)), device_id_type=MESH
        )

    lane = lax.broadcasted_iota(jnp.int32, (8, 128), 1)
    subl = lax.broadcasted_iota(jnp.int32, (8, 128), 0)
    low = lane < 64
    ez = lax.rem(lane, 8)
    ey = lax.rem(lax.div(lane, 8), 8)
    low25 = lax.broadcasted_iota(jnp.int32, (25, 128), 1) < 64
    low18 = lax.broadcasted_iota(jnp.int32, (NBR, 128), 1) < 64
    face0, face4 = pl.ds(0, 25, stride=8), pl.ds(4, 25, stride=8)

    for i in range(3):
        loads[i].wait()
    last[...] = jnp.zeros((56, 128), F32)
    for c in range(3):
        last[c * 8 : c * 8 + 8, 0:65] = now_ref[0, c, :, 1024:1089]
        last[24 + c * 8 : 32 + c * 8, 0:65] = prev_ref[0, c, :, 1024:1089]
    last[48:56, 0:65] = dens_ref[:, 1024:1089]
    rest = jnp.zeros((72, 128), F32)
    for i in range(9):
        if i < 8:
            at = slice(i * 128, i * 128 + 128)
            stack = [now_ref[0, c, :, at] for c in range(3)]
            stack += [prev_ref[0, c, :, at] for c in range(3)] + [dens_ref[:, at], rest]
        else:
            stack = [last[...], rest]
        tee[i * 128 : i * 128 + 128, :] = jnp.concatenate(stack, axis=0).T
    for i in range(0, 25, 2):
        pair = BLOCKS[i : i + 2]
        rows = []
        for b, d in (pair + pair)[:2]:
            for y in range(8):
                rows.append(tee[pl.ds(132 * y + 33 * b + d, 8, stride=4), :])
        turned = jnp.concatenate(rows, axis=0).T
        for h, (b, d) in enumerate(pair):
            at = (d * 5 + b) * 8
            for q in range(7):
                v = turned[q * 8 : q * 8 + 8, :]
                swapped = pltpu.roll(v, 64, 1)
                if h == 0:
                    val = jnp.where(low, v, pltpu.roll(swapped, 4, 0))
                else:
                    val = jnp.where(low, swapped, pltpu.roll(v, 4, 0))
                if q < 3:
                    cur[q, at : at + 8, :] = val
                elif q < 6:
                    pre[q - 3, at : at + 8, :] = val
                else:
                    inv[at : at + 8, :] = val
    cur[:, 200:208, :] = jnp.zeros((3, 8, 128), F32)
    pre[:, 200:208, :] = jnp.zeros((3, 8, 128), F32)
    inv[200:208, :] = jnp.ones((8, 128), F32)
    for c in range(3):
        halo_out[c] = jnp.where(
            low25, cur[c, face0, :], pltpu.roll(pre[c, face0, :], 64, 1)
        )
    halo_out[3] = inv[face0, :]
    def far_copy(s, part, k):
        buf = fbnd.at[s] if part == 2 else fint.at[s, part]
        return pltpu.make_async_remote_copy(
            src_ref=buf, dst_ref=buf,
            send_sem=far_send.at[s, part, k - 1], recv_sem=far_recv.at[s, part],
            device_id=(k, cuts, sub), device_id_type=MESH,
        )

    def direct(s, parts):
        return [
            (part, k)
            for part in parts
            for k in (1, 2)
            if part == 2 or s == STEPS - 1 or k == part + 1
        ]

    def relay(s):
        for mine in (1, 2):
            @pl.when(group == mine)
            def _():
                far_copy(s, mine - 1, mine).wait_recv()
                far_copy(s, mine - 1, 3 - mine).start()

    def pack_far(s, part):
        @pl.when(group == 0)
        def _():
            for c in range(3):
                for d in range(4):
                    for b in range(4):
                        to = (d * 4 + b) * 8
                        xs[c, to : to + 8, :] = cur[c, (d * 5 + b) * 8 : (d * 5 + b) * 8 + 8, :]
                ends = cur[c, 192:200, :]
                for b in range(4):
                    moved = pltpu.roll(cur[c, 160 + b * 8 : 168 + b * 8, :], 121 + b, 1)
                    ends = jnp.where(ez == b, moved, ends) if b else jnp.where(
                        ez == b, moved, pltpu.roll(ends, 125, 1)
                    )
                xs[c, 128:136, :] = ends
                ends = pltpu.roll(cur[c, 32:40, :], 72, 1)
                for d in range(1, 4):
                    moved = pltpu.roll(cur[c, d * 40 + 32 : d * 40 + 40, :], 72 + 8 * d, 1)
                    ends = jnp.where(ey == d, moved, ends)
                xs[c, 136:144, :] = ends
                if part == 0:
                    for a in range(1, 5):
                        yi[pl.ds(72 * c + a - 1, NBR, stride=4), :] = xs[
                            c, pl.ds(a, NBR, stride=8), :
                        ]
                else:
                    yb[pl.ds(c, NBR, stride=3), :] = jnp.where(
                        low18, xs[c, pl.ds(0, NBR, stride=8), :], xs[c, pl.ds(4, NBR, stride=8), :]
                    )
            if part == 0:
                for i in range(2):
                    fint[s, i] = yi[i * 112 : i * 112 + 112, :].astype(BF16)
            else:
                fbnd[s] = yb[...].astype(BF16)
            for piece, k in direct(s, (0, 1) if part == 0 else (2,)):
                far_copy(s, piece, k).start()

    def gradient(s):
        for i in range(UROWS // 16):
            for c in range(3):
                u1, u2, u3 = split3(cur[c, i * 16 : i * 16 + 16, :])
                for k, part in enumerate((u1, u2, u3, u1, u2, u1)):
                    at = k * UROWS + i * 16
                    urhs[at : at + 16, c * 128 : c * 128 + 128] = part
        grad[s] = jnp.dot(gm_ref[...], urhs[...], preferred_element_type=F32)

    def stress_rows(get, lam, mu, relax, r, n):
        g = [[get(c, j) for j in range(3)] for c in range(3)]
        exx, eyy, ezz = g[0][0], g[1][1], g[2][2]
        exy = 0.5 * (g[0][1] + g[1][0])
        exz = 0.5 * (g[0][2] + g[2][0])
        eyz = 0.5 * (g[1][2] + g[2][1])
        tr = exx + eyy + ezz
        third = tr * (1.0 / 3.0)
        m2 = 2.0 * mu
        sxy, sxz, syz = m2 * exy, m2 * exz, m2 * eyz
        dev = [m2 * (exx - third), m2 * (eyy - third), sxy, sxz, syz]
        total = relax(dev)
        bulk = lam * tr
        sxx = bulk + m2 * exx - total[0]
        syy = bulk + m2 * eyy - total[1]
        szz = bulk + m2 * ezz + (total[0] + total[1])
        places = (
            (sxx, ((0, 0),)), (syy, ((1, 1),)), (szz, ((2, 2),)),
            (sxy - total[2], ((0, 1), (1, 0))), (sxz - total[3], ((0, 2), (2, 0))),
            (syz - total[4], ((1, 2), (2, 1))),
        )
        for val, where in places:
            p1 = val.astype(BF16)
            p2 = (val - p1.astype(F32)).astype(BF16)
            for k, part in enumerate((p1, p2, p1)):
                for c, j in where:
                    to = k * 384 + j * 128 + r
                    srhs[to : to + n, c * 128 : c * 128 + 128] = part

    chunks = [(i * 16, 16) for i in range(7)] + [(112, 13)]

    def stress(s, keep):
        gains = [(1.0 - dec_ref[l : l + 1, :]) * RELAX[l] for l in range(3)]
        for r, n in chunks:
            at = slice(r, r + n)

            def relax(dev):
                total = [None] * 5
                for k in range(5):
                    for l in range(3):
                        new = dec_ref[l : l + 1, :] * mem[l, k, at, :] + gains[l] * dev[k]
                        if keep:
                            mem[l, k, at, :] = new
                        total[k] = new if total[k] is None else total[k] + new
                return total

            stress_rows(
                lambda c, j: grad[s, j * 128 + r : j * 128 + r + n, c * 128 : c * 128 + 128],
                lam_ref[at, :], mu_ref[at, :], relax, r, n,
            )
        out = jnp.dot(fm_ref[...], srhs[...], preferred_element_type=F32)
        for c in range(3):
            force[c] = out[:, c * 128 : c * 128 + 128]

    def ends_force():
        for c in range(3):
            u1, u2, u3 = split3(jnp.where(low25, cur[c, face0, :], cur[c, face4, :]))
            for k, part in enumerate((u1, u2, u3, u1, u2, u1)):
                urhs[k * 32 : k * 32 + 25, c * 128 : c * 128 + 128] = part
                urhs[k * 32 + 25 : k * 32 + 32, c * 128 : c * 128 + 128] = jnp.zeros(
                    (7, 128), BF16
                )
        fgrad[...] = jnp.dot(gmg_ref[...], urhs[0:192, :], preferred_element_type=F32)
        row_low = low[0:1]
        high = jnp.where(row_low, 0.0, 1.0)
        gains = [high * (1.0 - dec_ref[l : l + 1, :]) * RELAX[l] for l in range(3)]
        gain = jnp.where(row_low, ghost_in[125:126, :], gains[0] + gains[1] + gains[2])
        for r, n in chunks:
            at = slice(r, r + n)
            both = ghost_in[at, :]
            is_low = lax.broadcasted_iota(jnp.int32, (n, 128), 1) < 64

            def relax(dev):
                for k in range(5):
                    for l in range(3):
                        mem[l, k, at, :] = mem[l, k, at, :] + gains[l] * dev[k]
                return [gain * x for x in dev]

            def get(c, j):
                rows = slice(j * 128 + r, j * 128 + r + n)
                cols = slice(c * 128, c * 128 + 128)
                val = fgrad[rows, cols]
                grad[0, rows, cols] = grad[0, rows, cols] + high * val
                return val

            stress_rows(
                get, jnp.where(is_low, both, lam_ref[at, :]),
                jnp.where(is_low, pltpu.roll(both, 64, 1), mu_ref[at, :]), relax, r, n,
            )
        out = jnp.dot(fm_ref[...], srhs[...], preferred_element_type=F32)
        for c in range(3):
            added[c] = out[:, c * 128 : c * 128 + 128]
        assemble(added)
        for c in range(3):
            force[c] = force[c] + high * added[c]
            own_face[c] = jnp.where(low25, own_face[c], force[c, face4, :])

    def assemble(force):
        for c in range(3):
            for b in range(5):
                f0 = force[c, b * 8 : b * 8 + 8, :]
                f4 = force[c, 160 + b * 8 : 168 + b * 8, :]
                n0 = f0 + jnp.where(ez > 0, pltpu.roll(f4, 1, 1), 0.0)
                n4 = f4 + jnp.where(ez < 7, pltpu.roll(f0, 127, 1), 0.0)
                force[c, b * 8 : b * 8 + 8, :] = n0
                force[c, 160 + b * 8 : 168 + b * 8, :] = n4
            for d in range(5):
                f0 = force[c, d * 40 : d * 40 + 8, :]
                f4 = force[c, d * 40 + 32 : d * 40 + 40, :]
                n0 = f0 + jnp.where(ey > 0, pltpu.roll(f4, 8, 1), 0.0)
                n4 = f4 + jnp.where(ey < 7, pltpu.roll(f0, 120, 1), 0.0)
                force[c, d * 40 : d * 40 + 8, :] = n0
                force[c, d * 40 + 32 : d * 40 + 40, :] = n4

    def pack_faces(s):
        for c in range(3):
            own_face[c] = jnp.where(low25, force[c, face0, :], force[c, face4, :])
        f = [own_face[c] for c in range(3)]
        face_out[s, 0, 0] = jnp.where(low25, f[0], pltpu.roll(f[1], 64, 1))
        face_out[s, 0, 1] = f[2]
        face_out[s, 1, 0] = jnp.where(low25, pltpu.roll(f[0], 64, 1), f[1])
        face_out[s, 1, 1] = pltpu.roll(f[2], 64, 1)

    def face_copies(s):
        to_right = pltpu.make_async_remote_copy(
            src_ref=face_out.at[s, 1], dst_ref=face_left.at[s],
            send_sem=face_send.at[s, 0], recv_sem=face_recv.at[s, 0],
            device_id=right, device_id_type=MESH,
        )
        if s == STEPS - 1:
            return [to_right]
        to_left = pltpu.make_async_remote_copy(
            src_ref=face_out.at[s, 0], dst_ref=face_right.at[s],
            send_sem=face_send.at[s, 1], recv_sem=face_recv.at[s, 1],
            device_id=left, device_id_type=MESH,
        )
        return [to_right, to_left]

    def update_inside():
        for c in range(3):
            f0, f4 = force[c, face0, :], force[c, face4, :]
            force[c, face0, :] = f0 + jnp.where(low25, 0.0, pltpu.roll(f4, 64, 1))
            force[c, face4, :] = f4 + jnp.where(low25, pltpu.roll(f0, 64, 1), 0.0)
            base[c] = jnp.where(
                low25,
                2.0 * cur[c, face0, :] - pre[c, face0, :],
                2.0 * cur[c, face4, :] - pre[c, face4, :],
            )
        for i in range(UROWS // 16):
            at = slice(i * 16, i * 16 + 16)
            scale = inv[at, :]
            for c in range(3):
                u = cur[c, at, :]
                cur[c, at, :] = 2.0 * u - pre[c, at, :] + force[c, at, :] * scale
                pre[c, at, :] = u

    def update_ends(s):
        fl = [face_left[s, 0], pltpu.roll(face_left[s, 0], 64, 1), face_left[s, 1]]
        if s == 0:
            fl = [fl[c] + added[c, face4, :] for c in range(3)]
        if s < STEPS - 1:
            fr = [
                pltpu.roll(face_right[s, 0], 64, 1), face_right[s, 0],
                pltpu.roll(face_right[s, 1], 64, 1),
            ]
        for c in range(3):
            got = jnp.where(low25, fl[c], fr[c]) if s < STEPS - 1 else fl[c]
            new = base[c] + (own_face[c] + got) * finv[...]
            cur[c, face0, :] = jnp.where(low25, new, cur[c, face0, :])
            if s < STEPS - 1:
                cur[c, face4, :] = jnp.where(low25, cur[c, face4, :], new)

    part_copies = []
    for s in range(STEPS):
        line = []
        for k in range(1, 8):
            to = lax.rem(sub + k, 8)
            line.append(
                pltpu.make_async_remote_copy(
                    src_ref=parts_out.at[s, to], dst_ref=parts_in.at[s, sub],
                    send_sem=part_send.at[s, k - 1], recv_sem=part_recv.at[s, k - 1],
                    device_id=(group, cuts, to), device_id_type=MESH,
                )
            )
        part_copies.append(line)

    def kernel_part(s):
        for mine in (1, 2):
            @pl.when(group == mine)
            def _():
                for part in range(3):
                    if s == STEPS - 1 or part != mine - 1:
                        far_copy(s, part, mine).wait_recv()

        for i in range(2):
            yi[i * 112 : i * 112 + 112, :] = fint[s, i].astype(F32)
        yb[...] = fbnd[s].astype(F32)
        for c in range(3):
            for a in range(1, 4):
                xs[c, pl.ds(a, NBR, stride=8), :] = yi[pl.ds(72 * c + a - 1, NBR, stride=4), :]
            mid = yi[pl.ds(72 * c + 3, NBR, stride=4), :]
            ends = yb[pl.ds(c, NBR, stride=3), :]
            xs[c, pl.ds(0, NBR, stride=8), :] = jnp.where(low18, ends, pltpu.roll(mid, 64, 1))
            xs[c, pl.ds(4, NBR, stride=8), :] = jnp.where(low18, mid, ends)
        for c in range(3):
            block = {}
            for d in range(4):
                for b in range(4):
                    at = (d * 4 + b) * 8
                    block[b, d] = xs[c, at : at + 8, :]
            zend, yend = xs[c, 128:136, :], xs[c, 136:144, :]
            for d in range(4):
                block[4, d] = jnp.where(
                    ey < 7, pltpu.roll(block[0, d], 120, 1), pltpu.roll(yend, 8 * (7 - d), 1)
                )
            for b in range(5):
                block[b, 4] = jnp.where(
                    ez < 7, pltpu.roll(block[b, 0], 127, 1), pltpu.roll(zend, 7 - b, 1)
                )
            line = [block[bd] for bd in BLOCKS] + [jnp.zeros((8, 128), F32)]
            for i in range(0, 26, 2):
                tile = jnp.concatenate(line[i : i + 2], axis=0).astype(BF16)
                for k in range(3):
                    at = k * UROWS + i * 8
                    frhs[at : at + 16, c * 128 : c * 128 + 128] = tile
        fgrad[...] = jnp.dot(gf_ref[...], frhs[...], preferred_element_type=F32)

        def rows(r, n):
            at = slice(r, r + n)

            def strain(get):
                g = [[get(c, j) for j in range(3)] for c in range(3)]
                diag = [g[0][0], g[1][1], g[2][2]]
                tr = diag[0] + diag[1] + diag[2]
                third = tr * (1.0 / 3.0)
                dev = [x - third for x in diag]
                shear = [g[0][1] + g[1][0], g[0][2] + g[2][0], g[1][2] + g[2][1]]
                return tr, dev, shear

            tr, dev, off = strain(
                lambda c, j: grad[s, j * 128 + r : j * 128 + r + n, c * 128 : c * 128 + 128]
            )
            trf, devf, offf = strain(
                lambda c, j: fgrad[j * 128 + r : j * 128 + r + n, c * 128 : c * 128 + 128]
            )
            m2 = 2.0 * mu_ref[at, :]
            kappa = lam_ref[at, :] + m2 * (1.0 / 3.0)
            kb[at, :] = (TIME_STEP * kappa * trf * tr).astype(BF16)
            prod = dev[0] * devf[0] + dev[1] * devf[1] + dev[2] * devf[2]
            cross = off[0] * offf[0] + off[1] * offf[1] + off[2] * offf[2]
            ks[at, :] = (TIME_STEP * m2 * (prod + 0.5 * cross)).astype(BF16)

        for i in range(7):
            rows(i * 16, 16)
        rows(112, 13)
        for i, ref in enumerate((kb, ks)):
            placed = lax.dot_general(
                sel[...], ref[...], (((1,), (1,)), ((), ())), preferred_element_type=F32
            ).astype(BF16)
            for t in range(8):
                parts_out[s, t, :, i * 128 : i * 128 + 128] = placed[t * 32 : t * 32 + 32, :]
        parts_in[s, sub] = parts_out[s, sub]
        for copy in part_copies[s]:
            copy.start()

    urhs[1248:1280, :] = jnp.zeros((32, 384), BF16)
    zeros16 = jnp.zeros((16, 384), BF16)
    for i in range(9):
        srhs[i * 128 + 112 : i * 128 + 128, :] = zeros16
    kb[112:128, :] = jnp.zeros((16, 128), BF16)
    ks[112:128, :] = jnp.zeros((16, 128), BF16)

    yi[216:224, :] = jnp.zeros((8, 128), F32)
    yb[48:64, :] = jnp.zeros((16, 128), F32)
    xs[...] = jnp.zeros((3, 8 * NBR, 128), F32)
    for c in range(3):
        cur[c, face4, :] = jnp.where(low25, cur[c, face4, :], 0.0)
    loads[5].wait()
    gradient(0)
    for load in loads[6:]:
        load.wait()
    gain = (1.0 - dec_ref[0:1, :]) * RELAX[0]
    for l in (1, 2):
        gain = gain + (1.0 - dec_ref[l : l + 1, :]) * RELAX[l]
    low_row = lax.broadcasted_iota(jnp.int32, (125, 128), 1) < 64
    ghost_out[0:125, :] = jnp.where(low_row, pltpu.roll(lam_ref[...], 64, 1), mu_ref[...])
    ghost_out[125:126, :] = pltpu.roll(jnp.broadcast_to(gain, (8, 128)), 64, 1)[0:1]
    stress(0, True)
    assemble(force)
    pack_faces(0)
    pl.semaphore_wait(barrier, 11)
    halo = pltpu.make_async_remote_copy(
        src_ref=halo_out, dst_ref=halo_in, send_sem=halo_sem.at[0], recv_sem=halo_sem.at[1],
        device_id=left, device_id_type=MESH,
    )
    halo.start()
    first_faces = face_copies(0)
    for copy in first_faces:
        copy.start()
    ghost = pltpu.make_async_remote_copy(
        src_ref=ghost_out, dst_ref=ghost_in, send_sem=ghost_sem.at[0], recv_sem=ghost_sem.at[1],
        device_id=right, device_id_type=MESH,
    )
    ghost.start()
    pack_far(0, 0)

    for i in range(3, 5):
        loads[i].wait()
    own_row[0:1, 0:64] = own_ref[0]
    own_row[0:1, 64:128] = own_ref[1]
    slot = lax.broadcasted_iota(jnp.int32, (256, 128), 0)
    elem = lax.broadcasted_iota(jnp.int32, (256, 128), 1)
    onehot = jnp.where(own_row[0:1, :] == lax.div(slot, 32), 1.0, 0.0)
    one = lax.broadcasted_iota(jnp.int32, (128, 128), 0)
    two = lax.broadcasted_iota(jnp.int32, (128, 128), 1)
    one_low, two_low = one < 64, two < 64
    earlier = jnp.where(one < two, jnp.where(two_low, 1.0, jnp.where(one_low, 0.0, 1.0)), 0.0)
    count = jnp.dot(onehot.astype(BF16), earlier.astype(BF16), preferred_element_type=F32)
    rank_hit = jnp.where(count == lax.rem(slot, 16).astype(F32), onehot, 0.0)
    mine = lax.rem(lax.div(slot, 16), 2) == lax.div(elem, 64)
    sel[...] = jnp.where(mine, rank_hit, 0.0).astype(BF16)
    halo.wait()
    for c in range(3):
        got = halo_in[c]
        cur[c, face4, :] = jnp.where(low25, cur[c, face4, :], pltpu.roll(got, 64, 1))
        pre[c, face4, :] = jnp.where(low25, pre[c, face4, :], got)
    inv[face4, :] = jnp.where(low25, inv[face4, :], pltpu.roll(halo_in[3], 64, 1))
    pack_far(0, 1)
    inv[...] = 1.0 / (inv[...] * wt_ref[...])
    finv[...] = jnp.where(low25, inv[face0, :], inv[face4, :])

    for s in range(STEPS):
        if s == 0:
            copies = first_faces
            ghost.wait()
            ends_force()
        else:
            gradient(s)
            stress(s, s < STEPS - 1)
            assemble(force)
            pack_faces(s)
            copies = face_copies(s)
            for copy in copies:
                copy.start()
        update_inside()
        if s < STEPS - 1:
            pack_far(s + 1, 0)
            relay(s)
            if s == 1:
                kernel_part(0)
        else:
            kernel_part(1)
            kernel_part(2)
        for copy in copies:
            copy.wait()
        update_ends(s)
        if s < STEPS - 1:
            pack_far(s + 1, 1)

    rest = jnp.zeros((104, 128), F32)
    for i in range(0, 25, 2):
        pair = BLOCKS[i : i + 2]
        blocks = []
        for c in range(3):
            both = []
            for b, d in pair:
                at = (d * 5 + b) * 8
                v = cur[c, at : at + 8, :]
                both.append(jnp.where(subl < 4, v, pltpu.roll(pltpu.roll(v, 64, 1), 4, 0)))
            second = both[-1]
            blocks.append(jnp.where(low, both[0], pltpu.roll(second, 64, 1)))
        turned = jnp.concatenate(blocks + [rest], axis=0).T
        for h, (b, d) in enumerate(pair):
            for y in range(8):
                tee[pl.ds(132 * y + 33 * b + d, 8, stride=4), :] = turned[
                    h * 64 + y * 8 : h * 64 + y * 8 + 8, :
                ]
    for i in range(9):
        block = tee[i * 128 : i * 128 + 128, :].T
        width = min(128, 1089 - i * 128)
        for c in range(3):
            disp_ref[0, c, :, i * 128 : i * 128 + width] = block[c * 8 : c * 8 + 8, 0:width]

    @pl.when(group == 0)
    def _():
        for s in range(STEPS):
            for part, k in direct(s, (0, 1, 2)):
                far_copy(s, part, k).wait_send()

    for mine in (1, 2):
        @pl.when(group == mine)
        def _():
            for s in range(STEPS - 1):
                far_copy(s, mine - 1, 3 - mine).wait_send()

    for s in range(STEPS):
        for copy in part_copies[s]:
            copy.wait()
    for i in range(2):
        cols = slice(i * 128, i * 128 + 128)
        for h in range(2):
            quarter = []
            for t in range(h * 4, h * 4 + 4):
                total = parts_in[0, t, :, cols].astype(F32)
                for s in range(1, STEPS):
                    total = total + parts_in[s, t, :, cols].astype(F32)
                quarter.append(total)
            turned = jnp.concatenate(quarter, axis=0).T
            ker_ref[i * 125 : i * 125 + 125, h * 128 : h * 128 + 128] = turned[0:125, :]


def per_device(consts, now, prev, mem, dens, lam, mu, dec, own):
    hbm = pl.BlockSpec(memory_space=pl.ANY)
    dma = pltpu.SemaphoreType.DMA
    mem = jnp.transpose(mem, (1, 2, 3, 0, 4))
    own = jnp.transpose(own, (0, 2, 1))
    disp, kers = pl.pallas_call(
        kernel,
        out_shape=(
            pltpu.VMEM((1, 3, 8, 1089), F32),
            pltpu.VMEM((250, 256), F32),
        ),
        in_specs=[hbm] * 13,
        out_specs=(pl.BlockSpec(memory_space=pltpu.VMEM),) * 2,
        scratch_shapes=[
            pltpu.VMEM((384, 192), BF16),
            dma((2,)),
            pltpu.VMEM((126, 128), F32),
            pltpu.VMEM((126, 128), F32),
            pltpu.VMEM((3, UROWS, 128), F32),
            pltpu.VMEM((384, GK), BF16),
            pltpu.VMEM((384, 3 * UROWS), BF16),
            pltpu.VMEM((UROWS, 1152), BF16),
            pltpu.VMEM((UROWS, 128), F32),
            pltpu.VMEM((1, 3, 8, 1089), F32),
            pltpu.VMEM((1, 3, 8, 1089), F32),
            pltpu.VMEM((3, 5, 125, 128), F32),
            pltpu.VMEM((8, 1089), F32),
            pltpu.VMEM((125, 128), F32),
            pltpu.VMEM((125, 128), F32),
            pltpu.VMEM((3, 128), F32),
            pltpu.VMEM((2, 1, 64), jnp.int32),
            pltpu.VMEM((8, 128), jnp.int32),
            dma((27,)),
            pltpu.VMEM((56, 128), F32),
            pltpu.VMEM((1152, 128), F32),
            pltpu.VMEM((3, UROWS, 128), F32),
            pltpu.VMEM((3, UROWS, 128), F32),
            pltpu.VMEM((UROWS, 128), F32),
            pltpu.VMEM((GK, 384), BF16),
            pltpu.VMEM((STEPS, 384, 384), F32),
            pltpu.VMEM((1152, 384), BF16),
            pltpu.VMEM((3, UROWS, 128), F32),
            pltpu.VMEM((3, 25, 128), F32),
            pltpu.VMEM((25, 128), F32),
            pltpu.VMEM((3, 8 * NBR, 128), F32),
            pltpu.VMEM((224, 128), F32),
            pltpu.VMEM((64, 128), F32),
            pltpu.VMEM((STEPS, 2, 112, 128), BF16),
            pltpu.VMEM((STEPS, 64, 128), BF16),
            pltpu.VMEM((3 * UROWS, 384), BF16),
            pltpu.VMEM((384, 384), F32),
            pltpu.VMEM((128, 128), BF16),
            pltpu.VMEM((128, 128), BF16),
            pltpu.VMEM((256, 128), BF16),
            pltpu.VMEM((4, 25, 128), F32),
            pltpu.VMEM((4, 25, 128), F32),
            pltpu.VMEM((3, 25, 128), F32),
            pltpu.VMEM((STEPS, 2, 2, 25, 128), F32),
            pltpu.VMEM((STEPS, 2, 25, 128), F32),
            pltpu.VMEM((STEPS, 2, 25, 128), F32),
            pltpu.VMEM((STEPS, 8, 32, 256), BF16),
            pltpu.VMEM((STEPS, 8, 32, 256), BF16),
            dma((2,)),
            dma((STEPS, 2)),
            dma((STEPS, 2)),
            dma((STEPS, 3, 2)),
            dma((STEPS, 3)),
            dma((STEPS, 7)),
            dma((STEPS, 7)),
        ],
        compiler_params=pltpu.CompilerParams(
            collective_id=0, has_side_effects=True
        ),
        name="wavefields",
    )(*consts, now, prev, mem, dens, lam, mu, dec, own)
    return disp, jnp.transpose(kers.reshape(250, 1, 256), (1, 2, 0))


def solution(mesh):
    consts = tuple(jnp.asarray(t) for t in tables())
    in_specs = (
        P("group", None, ("cuts", "sub"), None),
        P("group", None, ("cuts", "sub"), None),
        P("group", None, None, None, ("cuts", "sub")),
        P(("cuts", "sub"), None),
        P(None, ("cuts", "sub")),
        P(None, ("cuts", "sub")),
        P(None, ("cuts", "sub")),
        P(("cuts", "sub"), None, None),
    )
    out_specs = (P("group", None, ("cuts", "sub"), None), P("group", ("cuts", "sub"), None))
    return jax.shard_map(
        functools.partial(per_device, consts),
        mesh=mesh, in_specs=in_specs, out_specs=out_specs, check_vma=False,
    )
```

```python
import functools
import math

import jax
import jax.numpy as jnp
import numpy as np
from jax import lax
from jax.experimental import pallas as pl
from jax.experimental.pallas import tpu as pltpu
from jax.sharding import PartitionSpec as P

STEPS = 3
TIME_STEP = 0.03
STEP_SQUARE = 0.0009
RELAX = (0.12, 0.08, 0.05)
F32 = jnp.float32
BF16 = jnp.bfloat16
MESH = pl.DeviceIdType.MESH

BLOCKS = [(b, d) for d in range(5) for b in range(5)]
UROWS = 208
GK = 1280
NBR = 18


def gll():
    root = math.sqrt(3.0 / 7.0)
    x = [-1.0, -root, 0.0, root, 1.0]
    w = np.array([0.1, 49.0 / 90.0, 32.0 / 45.0, 49.0 / 90.0, 0.1])
    der = np.zeros((5, 5))
    for p in range(5):
        for a in range(5):
            acc = 0.0
            for m in range(5):
                if m != a:
                    fac = 1.0 / (x[a] - x[m])
                    for k in range(5):
                        if k != a and k != m:
                            fac = fac * (x[p] - x[k]) / (x[a] - x[k])
                    acc = acc + fac
            der[p, a] = acc
    return der.astype(np.float32).astype(np.float64), w.astype(np.float32).astype(np.float64)


def pieces(mat, count):
    out = []
    rest = mat.astype(np.float64)
    for _ in range(count):
        part = rest.astype(jnp.bfloat16)
        out.append(part)
        rest = rest - part.astype(np.float64)
    return out


def tables():
    der, w = gll()
    grad = np.zeros((384, UROWS))
    force = np.zeros((UROWS, 384))

    def row(a, b, d):
        return (d * 5 + b) * 8 + a

    for a in range(5):
        for b in range(5):
            for d in range(5):
                r = row(a, b, d)
                for p in range(5):
                    for j, q in enumerate(((p, b, d), (a, p, d), (a, b, p))):
                        n = j * 128 + q[0] * 25 + q[1] * 5 + q[2]
                        at = (a, b, d)[j]
                        grad[n, r] = der[p, at]
                        force[r, n] = -der[p, at] * w[q[0]] * w[q[1]] * w[q[2]]
    g = pieces(grad, 3)
    gm = np.zeros((384, GK), jnp.bfloat16)
    for i, k in enumerate((0, 0, 0, 1, 1, 2)):
        gm[:, i * UROWS : (i + 1) * UROWS] = g[k]
    gf = np.concatenate(g, axis=1)
    f = pieces(force, 2)
    fm = np.concatenate([f[k] for k in (0, 0, 1)], axis=1)
    ends = [row(4, b, d) for b, d in BLOCKS]
    gmg = np.zeros((384, 192), jnp.bfloat16)
    for i, k in enumerate((0, 0, 0, 1, 1, 2)):
        gmg[:, i * 32 : i * 32 + 25] = g[k][:, ends]
    weight = np.ones((UROWS, 128))
    for a in range(5):
        for b in range(5):
            for d in range(5):
                for e in range(128):
                    ey, ez = (e // 8) % 8, e % 8
                    wx = w[0] + w[4] if a in (0, 4) else w[a]
                    wy = w[b] + (w[0] if (b == 4 and ey < 7) or (b == 0 and ey > 0) else 0.0)
                    wz = w[d] + (w[0] if (d == 4 and ez < 7) or (d == 0 and ez > 0) else 0.0)
                    weight[row(a, b, d), e] = wx * wy * wz
    return gm, gf, fm, (weight / STEP_SQUARE).astype(np.float32), gmg


def split3(x):
    x1 = x.astype(BF16)
    r1 = x - x1.astype(F32)
    x2 = r1.astype(BF16)
    x3 = (r1 - x2.astype(F32)).astype(BF16)
    return x1, x2, x3


def kernel(
    gm_hbm, gf_hbm, fm_hbm, wt_hbm, gmg_hbm,
    now_hbm, prev_hbm, mem_hbm, dens_hbm, lam_hbm, mu_hbm, dec_hbm, own_hbm,
    disp_ref, ker_ref,
    gmg_ref, ghost_sem, ghost_out, ghost_in, added,
    gm_ref, gf_ref, fm_ref, wt_ref, now_ref, prev_ref, mem, dens_ref, lam_ref, mu_ref,
    dec_ref, own_ref, own_row, load_sem,
    last, tee, cur, pre, inv, urhs, grad, srhs, force, base, finv, xs, yi, yb, fint, fbnd,
    frhs, fgrad, kb, ks, sel,
    halo_out, halo_in, own_face, face_out, face_left, face_right, parts_out, parts_in,
    halo_sem, face_send, face_recv, far_send, far_recv, part_send, part_recv,
):
    group = lax.axis_index("group")
    cuts = lax.axis_index("cuts")
    sub = lax.axis_index("sub")
    flat = cuts * 8 + sub
    ring = lax.axis_size("cuts") * 8
    nxt = lax.rem(flat + 1, ring)
    prv = lax.rem(flat + ring - 1, ring)
    right = (group, lax.div(nxt, 8), lax.rem(nxt, 8))
    left = (group, lax.div(prv, 8), lax.rem(prv, 8))

    barrier = pltpu.get_barrier_semaphore()
    for dev in (left, right):
        pl.semaphore_signal(barrier, inc=1, device_id=dev, device_id_type=MESH)
    for k in range(1, 3):
        pl.semaphore_signal(
            barrier, inc=1, device_id=(lax.rem(group + k, 3), cuts, sub), device_id_type=MESH
        )
    for k in range(1, 8):
        pl.semaphore_signal(
            barrier, inc=1, device_id=(group, cuts, lax.rem(sub + k, 8)), device_id_type=MESH
        )

    loads = [
        pltpu.make_async_copy(src, dst, load_sem.at[i])
        for i, (src, dst) in enumerate(
            (
                (now_hbm, now_ref), (prev_hbm, prev_ref), (dens_hbm, dens_ref),
                (wt_hbm, wt_ref), (own_hbm, own_ref), (gm_hbm, gm_ref),
                (dec_hbm, dec_ref), (lam_hbm, lam_ref), (mu_hbm, mu_ref),
                (fm_hbm, fm_ref), (gf_hbm, gf_ref), (gmg_hbm, gmg_ref),
            )
        )
    ]
    for l in range(3):
        for k in range(5):
            loads.append(
                pltpu.make_async_copy(
                    mem_hbm.at[l, k, :, 0, :], mem.at[l, k], load_sem.at[len(loads)]
                )
            )
    for load in loads:
        load.start()

    lane = lax.broadcasted_iota(jnp.int32, (8, 128), 1)
    subl = lax.broadcasted_iota(jnp.int32, (8, 128), 0)
    low = lane < 64
    ez = lax.rem(lane, 8)
    ey = lax.rem(lax.div(lane, 8), 8)
    low25 = lax.broadcasted_iota(jnp.int32, (25, 128), 1) < 64
    low18 = lax.broadcasted_iota(jnp.int32, (NBR, 128), 1) < 64
    face0, face4 = pl.ds(0, 25, stride=8), pl.ds(4, 25, stride=8)

    for i in range(3):
        loads[i].wait()
    last[...] = jnp.zeros((56, 128), F32)
    for c in range(3):
        last[c * 8 : c * 8 + 8, 0:65] = now_ref[0, c, :, 1024:1089]
        last[24 + c * 8 : 32 + c * 8, 0:65] = prev_ref[0, c, :, 1024:1089]
    last[48:56, 0:65] = dens_ref[:, 1024:1089]
    rest = jnp.zeros((72, 128), F32)
    for i in range(9):
        if i < 8:
            at = slice(i * 128, i * 128 + 128)
            stack = [now_ref[0, c, :, at] for c in range(3)]
            stack += [prev_ref[0, c, :, at] for c in range(3)] + [dens_ref[:, at], rest]
        else:
            stack = [last[...], rest]
        tee[i * 128 : i * 128 + 128, :] = jnp.concatenate(stack, axis=0).T
    for i in range(0, 25, 2):
        pair = BLOCKS[i : i + 2]
        rows = []
        for b, d in (pair + pair)[:2]:
            for y in range(8):
                rows.append(tee[pl.ds(132 * y + 33 * b + d, 8, stride=4), :])
        turned = jnp.concatenate(rows, axis=0).T
        for h, (b, d) in enumerate(pair):
            at = (d * 5 + b) * 8
            for q in range(7):
                v = turned[q * 8 : q * 8 + 8, :]
                swapped = pltpu.roll(v, 64, 1)
                if h == 0:
                    val = jnp.where(low, v, pltpu.roll(swapped, 4, 0))
                else:
                    val = jnp.where(low, swapped, pltpu.roll(v, 4, 0))
                if q < 3:
                    cur[q, at : at + 8, :] = val
                elif q < 6:
                    pre[q - 3, at : at + 8, :] = val
                else:
                    inv[at : at + 8, :] = val
    cur[:, 200:208, :] = jnp.zeros((3, 8, 128), F32)
    pre[:, 200:208, :] = jnp.zeros((3, 8, 128), F32)
    inv[200:208, :] = jnp.ones((8, 128), F32)
    for c in range(3):
        halo_out[c] = jnp.where(
            low25, cur[c, face0, :], pltpu.roll(pre[c, face0, :], 64, 1)
        )
    halo_out[3] = inv[face0, :]
    def far_copy(s, part, k):
        buf = fbnd.at[s] if part == 2 else fint.at[s, part]
        return pltpu.make_async_remote_copy(
            src_ref=buf, dst_ref=buf,
            send_sem=far_send.at[s, part, k - 1], recv_sem=far_recv.at[s, part],
            device_id=(k, cuts, sub), device_id_type=MESH,
        )

    def direct(s, parts):
        return [
            (part, k)
            for part in parts
            for k in (1, 2)
            if part == 2 or s == STEPS - 1 or k == part + 1
        ]

    def relay(s):
        for mine in (1, 2):
            @pl.when(group == mine)
            def _():
                far_copy(s, mine - 1, mine).wait_recv()
                far_copy(s, mine - 1, 3 - mine).start()

    def pack_far(s, part):
        @pl.when(group == 0)
        def _():
            for c in range(3):
                for d in range(4):
                    for b in range(4):
                        to = (d * 4 + b) * 8
                        xs[c, to : to + 8, :] = cur[c, (d * 5 + b) * 8 : (d * 5 + b) * 8 + 8, :]
                ends = cur[c, 192:200, :]
                for b in range(4):
                    moved = pltpu.roll(cur[c, 160 + b * 8 : 168 + b * 8, :], 121 + b, 1)
                    ends = jnp.where(ez == b, moved, ends) if b else jnp.where(
                        ez == b, moved, pltpu.roll(ends, 125, 1)
                    )
                xs[c, 128:136, :] = ends
                ends = pltpu.roll(cur[c, 32:40, :], 72, 1)
                for d in range(1, 4):
                    moved = pltpu.roll(cur[c, d * 40 + 32 : d * 40 + 40, :], 72 + 8 * d, 1)
                    ends = jnp.where(ey == d, moved, ends)
                xs[c, 136:144, :] = ends
                if part == 0:
                    for a in range(1, 5):
                        yi[pl.ds(72 * c + a - 1, NBR, stride=4), :] = xs[
                            c, pl.ds(a, NBR, stride=8), :
                        ]
                else:
                    yb[pl.ds(c, NBR, stride=3), :] = jnp.where(
                        low18, xs[c, pl.ds(0, NBR, stride=8), :], xs[c, pl.ds(4, NBR, stride=8), :]
                    )
            if part == 0:
                for i in range(2):
                    fint[s, i] = yi[i * 112 : i * 112 + 112, :].astype(BF16)
            else:
                fbnd[s] = yb[...].astype(BF16)
            for piece, k in direct(s, (0, 1) if part == 0 else (2,)):
                far_copy(s, piece, k).start()

    def gradient(s):
        for i in range(UROWS // 16):
            for c in range(3):
                u1, u2, u3 = split3(cur[c, i * 16 : i * 16 + 16, :])
                for k, part in enumerate((u1, u2, u3, u1, u2, u1)):
                    at = k * UROWS + i * 16
                    urhs[at : at + 16, c * 128 : c * 128 + 128] = part
        grad[s] = jnp.dot(gm_ref[...], urhs[...], preferred_element_type=F32)

    def stress_rows(get, lam, mu, relax, r, n):
        g = [[get(c, j) for j in range(3)] for c in range(3)]
        exx, eyy, ezz = g[0][0], g[1][1], g[2][2]
        exy = 0.5 * (g[0][1] + g[1][0])
        exz = 0.5 * (g[0][2] + g[2][0])
        eyz = 0.5 * (g[1][2] + g[2][1])
        tr = exx + eyy + ezz
        third = tr * (1.0 / 3.0)
        m2 = 2.0 * mu
        sxy, sxz, syz = m2 * exy, m2 * exz, m2 * eyz
        dev = [m2 * (exx - third), m2 * (eyy - third), sxy, sxz, syz]
        total = relax(dev)
        bulk = lam * tr
        sxx = bulk + m2 * exx - total[0]
        syy = bulk + m2 * eyy - total[1]
        szz = bulk + m2 * ezz + (total[0] + total[1])
        places = (
            (sxx, ((0, 0),)), (syy, ((1, 1),)), (szz, ((2, 2),)),
            (sxy - total[2], ((0, 1), (1, 0))), (sxz - total[3], ((0, 2), (2, 0))),
            (syz - total[4], ((1, 2), (2, 1))),
        )
        for val, where in places:
            p1 = val.astype(BF16)
            p2 = (val - p1.astype(F32)).astype(BF16)
            for k, part in enumerate((p1, p2, p1)):
                for c, j in where:
                    to = k * 384 + j * 128 + r
                    srhs[to : to + n, c * 128 : c * 128 + 128] = part

    chunks = [(i * 16, 16) for i in range(7)] + [(112, 13)]

    def stress(s, keep):
        gains = [(1.0 - dec_ref[l : l + 1, :]) * RELAX[l] for l in range(3)]
        for r, n in chunks:
            at = slice(r, r + n)

            def relax(dev):
                total = [None] * 5
                for k in range(5):
                    for l in range(3):
                        new = dec_ref[l : l + 1, :] * mem[l, k, at, :] + gains[l] * dev[k]
                        if keep:
                            mem[l, k, at, :] = new
                        total[k] = new if total[k] is None else total[k] + new
                return total

            stress_rows(
                lambda c, j: grad[s, j * 128 + r : j * 128 + r + n, c * 128 : c * 128 + 128],
                lam_ref[at, :], mu_ref[at, :], relax, r, n,
            )
        out = jnp.dot(fm_ref[...], srhs[...], preferred_element_type=F32)
        for c in range(3):
            force[c] = out[:, c * 128 : c * 128 + 128]

    def ends_force():
        for c in range(3):
            u1, u2, u3 = split3(jnp.where(low25, cur[c, face0, :], cur[c, face4, :]))
            for k, part in enumerate((u1, u2, u3, u1, u2, u1)):
                urhs[k * 32 : k * 32 + 25, c * 128 : c * 128 + 128] = part
                urhs[k * 32 + 25 : k * 32 + 32, c * 128 : c * 128 + 128] = jnp.zeros(
                    (7, 128), BF16
                )
        fgrad[...] = jnp.dot(gmg_ref[...], urhs[0:192, :], preferred_element_type=F32)
        row_low = low[0:1]
        high = jnp.where(row_low, 0.0, 1.0)
        gains = [high * (1.0 - dec_ref[l : l + 1, :]) * RELAX[l] for l in range(3)]
        gain = jnp.where(row_low, ghost_in[125:126, :], gains[0] + gains[1] + gains[2])
        for r, n in chunks:
            at = slice(r, r + n)
            both = ghost_in[at, :]
            is_low = lax.broadcasted_iota(jnp.int32, (n, 128), 1) < 64

            def relax(dev):
                for k in range(5):
                    for l in range(3):
                        mem[l, k, at, :] = mem[l, k, at, :] + gains[l] * dev[k]
                return [gain * x for x in dev]

            def get(c, j):
                rows = slice(j * 128 + r, j * 128 + r + n)
                cols = slice(c * 128, c * 128 + 128)
                val = fgrad[rows, cols]
                grad[0, rows, cols] = grad[0, rows, cols] + high * val
                return val

            stress_rows(
                get, jnp.where(is_low, both, lam_ref[at, :]),
                jnp.where(is_low, pltpu.roll(both, 64, 1), mu_ref[at, :]), relax, r, n,
            )
        out = jnp.dot(fm_ref[...], srhs[...], preferred_element_type=F32)
        for c in range(3):
            added[c] = out[:, c * 128 : c * 128 + 128]
        assemble(added)
        for c in range(3):
            force[c] = force[c] + high * added[c]
            own_face[c] = jnp.where(low25, own_face[c], force[c, face4, :])

    def assemble(force):
        for c in range(3):
            for b in range(5):
                f0 = force[c, b * 8 : b * 8 + 8, :]
                f4 = force[c, 160 + b * 8 : 168 + b * 8, :]
                n0 = f0 + jnp.where(ez > 0, pltpu.roll(f4, 1, 1), 0.0)
                n4 = f4 + jnp.where(ez < 7, pltpu.roll(f0, 127, 1), 0.0)
                force[c, b * 8 : b * 8 + 8, :] = n0
                force[c, 160 + b * 8 : 168 + b * 8, :] = n4
            for d in range(5):
                f0 = force[c, d * 40 : d * 40 + 8, :]
                f4 = force[c, d * 40 + 32 : d * 40 + 40, :]
                n0 = f0 + jnp.where(ey > 0, pltpu.roll(f4, 8, 1), 0.0)
                n4 = f4 + jnp.where(ey < 7, pltpu.roll(f0, 120, 1), 0.0)
                force[c, d * 40 : d * 40 + 8, :] = n0
                force[c, d * 40 + 32 : d * 40 + 40, :] = n4

    def pack_faces(s):
        for c in range(3):
            own_face[c] = jnp.where(low25, force[c, face0, :], force[c, face4, :])
        f = [own_face[c] for c in range(3)]
        face_out[s, 0, 0] = jnp.where(low25, f[0], pltpu.roll(f[1], 64, 1))
        face_out[s, 0, 1] = f[2]
        face_out[s, 1, 0] = jnp.where(low25, pltpu.roll(f[0], 64, 1), f[1])
        face_out[s, 1, 1] = pltpu.roll(f[2], 64, 1)

    def face_copies(s):
        to_right = pltpu.make_async_remote_copy(
            src_ref=face_out.at[s, 1], dst_ref=face_left.at[s],
            send_sem=face_send.at[s, 0], recv_sem=face_recv.at[s, 0],
            device_id=right, device_id_type=MESH,
        )
        if s == STEPS - 1:
            return [to_right]
        to_left = pltpu.make_async_remote_copy(
            src_ref=face_out.at[s, 0], dst_ref=face_right.at[s],
            send_sem=face_send.at[s, 1], recv_sem=face_recv.at[s, 1],
            device_id=left, device_id_type=MESH,
        )
        return [to_right, to_left]

    def update_inside():
        for c in range(3):
            f0, f4 = force[c, face0, :], force[c, face4, :]
            force[c, face0, :] = f0 + jnp.where(low25, 0.0, pltpu.roll(f4, 64, 1))
            force[c, face4, :] = f4 + jnp.where(low25, pltpu.roll(f0, 64, 1), 0.0)
            base[c] = jnp.where(
                low25,
                2.0 * cur[c, face0, :] - pre[c, face0, :],
                2.0 * cur[c, face4, :] - pre[c, face4, :],
            )
        for i in range(UROWS // 16):
            at = slice(i * 16, i * 16 + 16)
            scale = inv[at, :]
            for c in range(3):
                u = cur[c, at, :]
                cur[c, at, :] = 2.0 * u - pre[c, at, :] + force[c, at, :] * scale
                pre[c, at, :] = u

    def update_ends(s):
        fl = [face_left[s, 0], pltpu.roll(face_left[s, 0], 64, 1), face_left[s, 1]]
        if s == 0:
            fl = [fl[c] + added[c, face4, :] for c in range(3)]
        if s < STEPS - 1:
            fr = [
                pltpu.roll(face_right[s, 0], 64, 1), face_right[s, 0],
                pltpu.roll(face_right[s, 1], 64, 1),
            ]
        for c in range(3):
            got = jnp.where(low25, fl[c], fr[c]) if s < STEPS - 1 else fl[c]
            new = base[c] + (own_face[c] + got) * finv[...]
            cur[c, face0, :] = jnp.where(low25, new, cur[c, face0, :])
            if s < STEPS - 1:
                cur[c, face4, :] = jnp.where(low25, cur[c, face4, :], new)

    part_copies = []
    for s in range(STEPS):
        line = []
        for k in range(1, 8):
            to = lax.rem(sub + k, 8)
            line.append(
                pltpu.make_async_remote_copy(
                    src_ref=parts_out.at[s, to], dst_ref=parts_in.at[s, sub],
                    send_sem=part_send.at[s, k - 1], recv_sem=part_recv.at[s, k - 1],
                    device_id=(group, cuts, to), device_id_type=MESH,
                )
            )
        part_copies.append(line)

    def kernel_part(s):
        for mine in (1, 2):
            @pl.when(group == mine)
            def _():
                for part in range(3):
                    if s == STEPS - 1 or part != mine - 1:
                        far_copy(s, part, mine).wait_recv()

        for i in range(2):
            yi[i * 112 : i * 112 + 112, :] = fint[s, i].astype(F32)
        yb[...] = fbnd[s].astype(F32)
        for c in range(3):
            for a in range(1, 4):
                xs[c, pl.ds(a, NBR, stride=8), :] = yi[pl.ds(72 * c + a - 1, NBR, stride=4), :]
            mid = yi[pl.ds(72 * c + 3, NBR, stride=4), :]
            ends = yb[pl.ds(c, NBR, stride=3), :]
            xs[c, pl.ds(0, NBR, stride=8), :] = jnp.where(low18, ends, pltpu.roll(mid, 64, 1))
            xs[c, pl.ds(4, NBR, stride=8), :] = jnp.where(low18, mid, ends)
        for c in range(3):
            block = {}
            for d in range(4):
                for b in range(4):
                    at = (d * 4 + b) * 8
                    block[b, d] = xs[c, at : at + 8, :]
            zend, yend = xs[c, 128:136, :], xs[c, 136:144, :]
            for d in range(4):
                block[4, d] = jnp.where(
                    ey < 7, pltpu.roll(block[0, d], 120, 1), pltpu.roll(yend, 8 * (7 - d), 1)
                )
            for b in range(5):
                block[b, 4] = jnp.where(
                    ez < 7, pltpu.roll(block[b, 0], 127, 1), pltpu.roll(zend, 7 - b, 1)
                )
            line = [block[bd] for bd in BLOCKS] + [jnp.zeros((8, 128), F32)]
            for i in range(0, 26, 2):
                tile = jnp.concatenate(line[i : i + 2], axis=0).astype(BF16)
                for k in range(3):
                    at = k * UROWS + i * 8
                    frhs[at : at + 16, c * 128 : c * 128 + 128] = tile
        fgrad[...] = jnp.dot(gf_ref[...], frhs[...], preferred_element_type=F32)

        def rows(r, n):
            at = slice(r, r + n)

            def strain(get):
                g = [[get(c, j) for j in range(3)] for c in range(3)]
                diag = [g[0][0], g[1][1], g[2][2]]
                tr = diag[0] + diag[1] + diag[2]
                third = tr * (1.0 / 3.0)
                dev = [x - third for x in diag]
                shear = [g[0][1] + g[1][0], g[0][2] + g[2][0], g[1][2] + g[2][1]]
                return tr, dev, shear

            tr, dev, off = strain(
                lambda c, j: grad[s, j * 128 + r : j * 128 + r + n, c * 128 : c * 128 + 128]
            )
            trf, devf, offf = strain(
                lambda c, j: fgrad[j * 128 + r : j * 128 + r + n, c * 128 : c * 128 + 128]
            )
            m2 = 2.0 * mu_ref[at, :]
            kappa = lam_ref[at, :] + m2 * (1.0 / 3.0)
            kb[at, :] = (TIME_STEP * kappa * trf * tr).astype(BF16)
            prod = dev[0] * devf[0] + dev[1] * devf[1] + dev[2] * devf[2]
            cross = off[0] * offf[0] + off[1] * offf[1] + off[2] * offf[2]
            ks[at, :] = (TIME_STEP * m2 * (prod + 0.5 * cross)).astype(BF16)

        for i in range(7):
            rows(i * 16, 16)
        rows(112, 13)
        for i, ref in enumerate((kb, ks)):
            placed = lax.dot_general(
                sel[...], ref[...], (((1,), (1,)), ((), ())), preferred_element_type=F32
            ).astype(BF16)
            for t in range(8):
                parts_out[s, t, :, i * 128 : i * 128 + 128] = placed[t * 32 : t * 32 + 32, :]
        parts_in[s, sub] = parts_out[s, sub]
        for copy in part_copies[s]:
            copy.start()

    urhs[1248:1280, :] = jnp.zeros((32, 384), BF16)
    zeros16 = jnp.zeros((16, 384), BF16)
    for i in range(9):
        srhs[i * 128 + 112 : i * 128 + 128, :] = zeros16
    kb[112:128, :] = jnp.zeros((16, 128), BF16)
    ks[112:128, :] = jnp.zeros((16, 128), BF16)

    yi[216:224, :] = jnp.zeros((8, 128), F32)
    yb[48:64, :] = jnp.zeros((16, 128), F32)
    xs[...] = jnp.zeros((3, 8 * NBR, 128), F32)
    for c in range(3):
        cur[c, face4, :] = jnp.where(low25, cur[c, face4, :], 0.0)
    loads[5].wait()
    gradient(0)
    for load in loads[6:]:
        load.wait()
    gain = (1.0 - dec_ref[0:1, :]) * RELAX[0]
    for l in (1, 2):
        gain = gain + (1.0 - dec_ref[l : l + 1, :]) * RELAX[l]
    low_row = lax.broadcasted_iota(jnp.int32, (125, 128), 1) < 64
    ghost_out[0:125, :] = jnp.where(low_row, pltpu.roll(lam_ref[...], 64, 1), mu_ref[...])
    ghost_out[125:126, :] = pltpu.roll(jnp.broadcast_to(gain, (8, 128)), 64, 1)[0:1]
    stress(0, True)
    assemble(force)
    pack_faces(0)
    pl.semaphore_wait(barrier, 11)
    halo = pltpu.make_async_remote_copy(
        src_ref=halo_out, dst_ref=halo_in, send_sem=halo_sem.at[0], recv_sem=halo_sem.at[1],
        device_id=left, device_id_type=MESH,
    )
    halo.start()
    first_faces = face_copies(0)
    for copy in first_faces:
        copy.start()
    ghost = pltpu.make_async_remote_copy(
        src_ref=ghost_out, dst_ref=ghost_in, send_sem=ghost_sem.at[0], recv_sem=ghost_sem.at[1],
        device_id=right, device_id_type=MESH,
    )
    ghost.start()
    pack_far(0, 0)

    for i in range(3, 5):
        loads[i].wait()
    own_row[0:1, 0:64] = own_ref[0]
    own_row[0:1, 64:128] = own_ref[1]
    slot = lax.broadcasted_iota(jnp.int32, (256, 128), 0)
    elem = lax.broadcasted_iota(jnp.int32, (256, 128), 1)
    onehot = jnp.where(own_row[0:1, :] == lax.div(slot, 32), 1.0, 0.0)
    one = lax.broadcasted_iota(jnp.int32, (128, 128), 0)
    two = lax.broadcasted_iota(jnp.int32, (128, 128), 1)
    one_low, two_low = one < 64, two < 64
    earlier = jnp.where(one < two, jnp.where(two_low, 1.0, jnp.where(one_low, 0.0, 1.0)), 0.0)
    count = jnp.dot(onehot.astype(BF16), earlier.astype(BF16), preferred_element_type=F32)
    rank_hit = jnp.where(count == lax.rem(slot, 16).astype(F32), onehot, 0.0)
    mine = lax.rem(lax.div(slot, 16), 2) == lax.div(elem, 64)
    sel[...] = jnp.where(mine, rank_hit, 0.0).astype(BF16)
    halo.wait()
    for c in range(3):
        got = halo_in[c]
        cur[c, face4, :] = jnp.where(low25, cur[c, face4, :], pltpu.roll(got, 64, 1))
        pre[c, face4, :] = jnp.where(low25, pre[c, face4, :], got)
    inv[face4, :] = jnp.where(low25, inv[face4, :], pltpu.roll(halo_in[3], 64, 1))
    pack_far(0, 1)
    inv[...] = 1.0 / (inv[...] * wt_ref[...])
    finv[...] = jnp.where(low25, inv[face0, :], inv[face4, :])

    for s in range(STEPS):
        if s == 0:
            copies = first_faces
            ghost.wait()
            ends_force()
        else:
            gradient(s)
            stress(s, s < STEPS - 1)
            assemble(force)
            pack_faces(s)
            copies = face_copies(s)
            for copy in copies:
                copy.start()
        update_inside()
        if s < STEPS - 1:
            pack_far(s + 1, 0)
            relay(s)
            if s == 1:
                kernel_part(0)
        else:
            kernel_part(1)
            kernel_part(2)
        for copy in copies:
            copy.wait()
        update_ends(s)
        if s < STEPS - 1:
            pack_far(s + 1, 1)

    rest = jnp.zeros((104, 128), F32)
    for i in range(0, 25, 2):
        pair = BLOCKS[i : i + 2]
        blocks = []
        for c in range(3):
            both = []
            for b, d in pair:
                at = (d * 5 + b) * 8
                v = cur[c, at : at + 8, :]
                both.append(jnp.where(subl < 4, v, pltpu.roll(pltpu.roll(v, 64, 1), 4, 0)))
            second = both[-1]
            blocks.append(jnp.where(low, both[0], pltpu.roll(second, 64, 1)))
        turned = jnp.concatenate(blocks + [rest], axis=0).T
        for h, (b, d) in enumerate(pair):
            for y in range(8):
                tee[pl.ds(132 * y + 33 * b + d, 8, stride=4), :] = turned[
                    h * 64 + y * 8 : h * 64 + y * 8 + 8, :
                ]
    for i in range(9):
        block = tee[i * 128 : i * 128 + 128, :].T
        width = min(128, 1089 - i * 128)
        for c in range(3):
            disp_ref[0, c, :, i * 128 : i * 128 + width] = block[c * 8 : c * 8 + 8, 0:width]

    @pl.when(group == 0)
    def _():
        for s in range(STEPS):
            for part, k in direct(s, (0, 1, 2)):
                far_copy(s, part, k).wait_send()

    for mine in (1, 2):
        @pl.when(group == mine)
        def _():
            for s in range(STEPS - 1):
                far_copy(s, mine - 1, 3 - mine).wait_send()

    for s in range(STEPS):
        for copy in part_copies[s]:
            copy.wait()
    for i in range(2):
        cols = slice(i * 128, i * 128 + 128)
        for h in range(2):
            quarter = []
            for t in range(h * 4, h * 4 + 4):
                total = parts_in[0, t, :, cols].astype(F32)
                for s in range(1, STEPS):
                    total = total + parts_in[s, t, :, cols].astype(F32)
                quarter.append(total)
            turned = jnp.concatenate(quarter, axis=0).T
            ker_ref[h, i * 125 : i * 125 + 125, :] = turned[0:125, :]


def finish(disp_ref, ker_ref, disp_hbm, ker_hbm, sem):
    copies = [pltpu.make_async_copy(disp_ref, disp_hbm, sem.at[0])]
    for h in range(2):
        copies.append(
            pltpu.make_async_copy(
                ker_ref.at[h], ker_hbm.at[:, 0, pl.ds(h * 128, 128)], sem.at[1 + h]
            )
        )
    for copy in copies:
        copy.start()
    for copy in copies:
        copy.wait()


def per_device(consts, now, prev, mem, dens, lam, mu, dec, own):
    hbm = pl.BlockSpec(memory_space=pl.ANY)
    dma = pltpu.SemaphoreType.DMA
    mem = jnp.transpose(mem, (1, 2, 3, 0, 4))
    own = jnp.transpose(own, (0, 2, 1))
    disp, kers = pl.pallas_call(
        kernel,
        out_shape=(
            pltpu.VMEM((1, 3, 8, 1089), F32),
            pltpu.VMEM((2, 250, 128), F32),
        ),
        in_specs=[hbm] * 13,
        out_specs=(pl.BlockSpec(memory_space=pltpu.VMEM),) * 2,
        scratch_shapes=[
            pltpu.VMEM((384, 192), BF16),
            dma((2,)),
            pltpu.VMEM((126, 128), F32),
            pltpu.VMEM((126, 128), F32),
            pltpu.VMEM((3, UROWS, 128), F32),
            pltpu.VMEM((384, GK), BF16),
            pltpu.VMEM((384, 3 * UROWS), BF16),
            pltpu.VMEM((UROWS, 1152), BF16),
            pltpu.VMEM((UROWS, 128), F32),
            pltpu.VMEM((1, 3, 8, 1089), F32),
            pltpu.VMEM((1, 3, 8, 1089), F32),
            pltpu.VMEM((3, 5, 125, 128), F32),
            pltpu.VMEM((8, 1089), F32),
            pltpu.VMEM((125, 128), F32),
            pltpu.VMEM((125, 128), F32),
            pltpu.VMEM((3, 128), F32),
            pltpu.VMEM((2, 1, 64), jnp.int32),
            pltpu.VMEM((8, 128), jnp.int32),
            dma((27,)),
            pltpu.VMEM((56, 128), F32),
            pltpu.VMEM((1152, 128), F32),
            pltpu.VMEM((3, UROWS, 128), F32),
            pltpu.VMEM((3, UROWS, 128), F32),
            pltpu.VMEM((UROWS, 128), F32),
            pltpu.VMEM((GK, 384), BF16),
            pltpu.VMEM((STEPS, 384, 384), F32),
            pltpu.VMEM((1152, 384), BF16),
            pltpu.VMEM((3, UROWS, 128), F32),
            pltpu.VMEM((3, 25, 128), F32),
            pltpu.VMEM((25, 128), F32),
            pltpu.VMEM((3, 8 * NBR, 128), F32),
            pltpu.VMEM((224, 128), F32),
            pltpu.VMEM((64, 128), F32),
            pltpu.VMEM((STEPS, 2, 112, 128), BF16),
            pltpu.VMEM((STEPS, 64, 128), BF16),
            pltpu.VMEM((3 * UROWS, 384), BF16),
            pltpu.VMEM((384, 384), F32),
            pltpu.VMEM((128, 128), BF16),
            pltpu.VMEM((128, 128), BF16),
            pltpu.VMEM((256, 128), BF16),
            pltpu.VMEM((4, 25, 128), F32),
            pltpu.VMEM((4, 25, 128), F32),
            pltpu.VMEM((3, 25, 128), F32),
            pltpu.VMEM((STEPS, 2, 2, 25, 128), F32),
            pltpu.VMEM((STEPS, 2, 25, 128), F32),
            pltpu.VMEM((STEPS, 2, 25, 128), F32),
            pltpu.VMEM((STEPS, 8, 32, 256), BF16),
            pltpu.VMEM((STEPS, 8, 32, 256), BF16),
            dma((2,)),
            dma((STEPS, 2)),
            dma((STEPS, 2)),
            dma((STEPS, 3, 2)),
            dma((STEPS, 3)),
            dma((STEPS, 7)),
            dma((STEPS, 7)),
        ],
        compiler_params=pltpu.CompilerParams(
            collective_id=0, has_side_effects=True
        ),
        name="wavefields",
    )(*consts, now, prev, mem, dens, lam, mu, dec, own)
    disp, kers = pl.pallas_call(
        finish,
        out_shape=(
            jax.ShapeDtypeStruct((1, 3, 8, 1089), F32),
            jax.ShapeDtypeStruct((250, 1, 256), F32),
        ),
        in_specs=[pl.BlockSpec(memory_space=pltpu.VMEM)] * 2,
        out_specs=(hbm, hbm),
        scratch_shapes=[dma((3,))],
        compiler_params=pltpu.CompilerParams(vmem_limit_bytes=8 * 1024 * 1024),
        name="results",
    )(disp, kers)
    return disp, jnp.transpose(kers, (1, 2, 0))


def solution(mesh):
    consts = tuple(jnp.asarray(t) for t in tables())
    in_specs = (
        P("group", None, ("cuts", "sub"), None),
        P("group", None, ("cuts", "sub"), None),
        P("group", None, None, None, ("cuts", "sub")),
        P(("cuts", "sub"), None),
        P(None, ("cuts", "sub")),
        P(None, ("cuts", "sub")),
        P(None, ("cuts", "sub")),
        P(("cuts", "sub"), None, None),
    )
    out_specs = (P("group", None, ("cuts", "sub"), None), P("group", ("cuts", "sub"), None))
    return jax.shard_map(
        functools.partial(per_device, consts),
        mesh=mesh, in_specs=in_specs, out_specs=out_specs, check_vma=False,
    )
```

```python
import functools
import math

import jax
import jax.numpy as jnp
import numpy as np
from jax import lax
from jax.experimental import pallas as pl
from jax.experimental.pallas import tpu as pltpu
from jax.sharding import PartitionSpec as P

STEPS = 3
TIME_STEP = 0.03
STEP_SQUARE = 0.0009
RELAX = (0.12, 0.08, 0.05)
F32 = jnp.float32
BF16 = jnp.bfloat16
MESH = pl.DeviceIdType.MESH

BLOCKS = [(b, d) for d in range(5) for b in range(5)]
UROWS = 208
GK = 1280
NBR = 18


def gll():
    root = math.sqrt(3.0 / 7.0)
    x = [-1.0, -root, 0.0, root, 1.0]
    w = np.array([0.1, 49.0 / 90.0, 32.0 / 45.0, 49.0 / 90.0, 0.1])
    der = np.zeros((5, 5))
    for p in range(5):
        for a in range(5):
            acc = 0.0
            for m in range(5):
                if m != a:
                    fac = 1.0 / (x[a] - x[m])
                    for k in range(5):
                        if k != a and k != m:
                            fac = fac * (x[p] - x[k]) / (x[a] - x[k])
                    acc = acc + fac
            der[p, a] = acc
    return der.astype(np.float32).astype(np.float64), w.astype(np.float32).astype(np.float64)


def pieces(mat, count):
    out = []
    rest = mat.astype(np.float64)
    for _ in range(count):
        part = rest.astype(jnp.bfloat16)
        out.append(part)
        rest = rest - part.astype(np.float64)
    return out


def tables():
    der, w = gll()
    grad = np.zeros((384, UROWS))
    force = np.zeros((UROWS, 384))

    def row(a, b, d):
        return (d * 5 + b) * 8 + a

    for a in range(5):
        for b in range(5):
            for d in range(5):
                r = row(a, b, d)
                for p in range(5):
                    for j, q in enumerate(((p, b, d), (a, p, d), (a, b, p))):
                        n = j * 128 + q[0] * 25 + q[1] * 5 + q[2]
                        at = (a, b, d)[j]
                        grad[n, r] = der[p, at]
                        force[r, n] = -der[p, at] * w[q[0]] * w[q[1]] * w[q[2]]
    g = pieces(grad, 3)
    gm = np.zeros((384, GK), jnp.bfloat16)
    for i, k in enumerate((0, 0, 0, 1, 1, 2)):
        gm[:, i * UROWS : (i + 1) * UROWS] = g[k]
    gf = np.concatenate(g, axis=1)
    f = pieces(force, 2)
    fm = np.concatenate([f[k] for k in (0, 0, 1)], axis=1)
    ends = [row(4, b, d) for b, d in BLOCKS]
    gmg = np.zeros((384, 192), jnp.bfloat16)
    for i, k in enumerate((0, 0, 0, 1, 1, 2)):
        gmg[:, i * 32 : i * 32 + 25] = g[k][:, ends]
    weight = np.ones((UROWS, 128))
    for a in range(5):
        for b in range(5):
            for d in range(5):
                for e in range(128):
                    ey, ez = (e // 8) % 8, e % 8
                    wx = w[0] + w[4] if a in (0, 4) else w[a]
                    wy = w[b] + (w[0] if (b == 4 and ey < 7) or (b == 0 and ey > 0) else 0.0)
                    wz = w[d] + (w[0] if (d == 4 and ez < 7) or (d == 0 and ez > 0) else 0.0)
                    weight[row(a, b, d), e] = wx * wy * wz
    return gm, gf, fm, (weight / STEP_SQUARE).astype(np.float32), gmg


def split3(x):
    x1 = x.astype(BF16)
    r1 = x - x1.astype(F32)
    x2 = r1.astype(BF16)
    x3 = (r1 - x2.astype(F32)).astype(BF16)
    return x1, x2, x3


def kernel(
    gm_hbm, gf_hbm, fm_hbm, wt_hbm, gmg_hbm,
    now_hbm, prev_hbm, mem_hbm, dens_hbm, lam_hbm, mu_hbm, dec_hbm, own_hbm,
    disp_ref, ker_ref,
    gmg_ref, ghost_sem, ghost_out, ghost_in, early, added,
    gm_ref, gf_ref, fm_ref, wt_ref, now_ref, prev_ref, mem, dens_ref, lam_ref, mu_ref,
    dec_ref, own_ref, own_row, load_sem,
    last, tee, cur, pre, inv, urhs, grad, srhs, force, base, finv, xs, yi, yb, fint, fbnd,
    frhs, fgrad, kb, ks, sel,
    halo_out, halo_in, own_face, face_out, face_left, face_right, parts_out, parts_in,
    halo_sem, face_send, face_recv, far_send, far_recv, part_send, part_recv,
):
    group = lax.axis_index("group")
    cuts = lax.axis_index("cuts")
    sub = lax.axis_index("sub")
    flat = cuts * 8 + sub
    ring = lax.axis_size("cuts") * 8
    nxt = lax.rem(flat + 1, ring)
    prv = lax.rem(flat + ring - 1, ring)
    right = (group, lax.div(nxt, 8), lax.rem(nxt, 8))
    left = (group, lax.div(prv, 8), lax.rem(prv, 8))

    barrier = pltpu.get_barrier_semaphore()
    for dev in (left, right):
        pl.semaphore_signal(barrier, inc=1, device_id=dev, device_id_type=MESH)
    for k in range(1, 3):
        pl.semaphore_signal(
            barrier, inc=1, device_id=(lax.rem(group + k, 3), cuts, sub), device_id_type=MESH
        )
    for k in range(1, 8):
        pl.semaphore_signal(
            barrier, inc=1, device_id=(group, cuts, lax.rem(sub + k, 8)), device_id_type=MESH
        )

    loads = [
        pltpu.make_async_copy(src, dst, load_sem.at[i])
        for i, (src, dst) in enumerate(
            (
                (now_hbm, now_ref), (prev_hbm, prev_ref), (dens_hbm, dens_ref),
                (wt_hbm, wt_ref), (own_hbm, own_ref), (gm_hbm, gm_ref),
                (dec_hbm, dec_ref), (lam_hbm, lam_ref), (mu_hbm, mu_ref),
                (fm_hbm, fm_ref), (gf_hbm, gf_ref), (gmg_hbm, gmg_ref),
            )
        )
    ]
    for l in range(3):
        for k in range(5):
            loads.append(
                pltpu.make_async_copy(
                    mem_hbm.at[l, k, :, 0, :], mem.at[l, k], load_sem.at[len(loads)]
                )
            )
    for load in loads:
        load.start()

    lane = lax.broadcasted_iota(jnp.int32, (8, 128), 1)
    subl = lax.broadcasted_iota(jnp.int32, (8, 128), 0)
    low = lane < 64
    ez = lax.rem(lane, 8)
    ey = lax.rem(lax.div(lane, 8), 8)
    low25 = lax.broadcasted_iota(jnp.int32, (25, 128), 1) < 64
    low18 = lax.broadcasted_iota(jnp.int32, (NBR, 128), 1) < 64
    face0, face4 = pl.ds(0, 25, stride=8), pl.ds(4, 25, stride=8)

    for i in range(3):
        loads[i].wait()
    last[...] = jnp.zeros((56, 128), F32)
    for c in range(3):
        last[c * 8 : c * 8 + 8, 0:65] = now_ref[0, c, :, 1024:1089]
        last[24 + c * 8 : 32 + c * 8, 0:65] = prev_ref[0, c, :, 1024:1089]
    last[48:56, 0:65] = dens_ref[:, 1024:1089]
    rest = jnp.zeros((72, 128), F32)
    for i in range(9):
        if i < 8:
            at = slice(i * 128, i * 128 + 128)
            stack = [now_ref[0, c, :, at] for c in range(3)]
            stack += [prev_ref[0, c, :, at] for c in range(3)] + [dens_ref[:, at], rest]
        else:
            stack = [last[...], rest]
        tee[i * 128 : i * 128 + 128, :] = jnp.concatenate(stack, axis=0).T
    for i in range(0, 25, 2):
        pair = BLOCKS[i : i + 2]
        rows = []
        for b, d in (pair + pair)[:2]:
            for y in range(8):
                rows.append(tee[pl.ds(132 * y + 33 * b + d, 8, stride=4), :])
        turned = jnp.concatenate(rows, axis=0).T
        for h, (b, d) in enumerate(pair):
            at = (d * 5 + b) * 8
            for q in range(7):
                v = turned[q * 8 : q * 8 + 8, :]
                swapped = pltpu.roll(v, 64, 1)
                if h == 0:
                    val = jnp.where(low, v, pltpu.roll(swapped, 4, 0))
                else:
                    val = jnp.where(low, swapped, pltpu.roll(v, 4, 0))
                if q < 3:
                    cur[q, at : at + 8, :] = val
                elif q < 6:
                    pre[q - 3, at : at + 8, :] = val
                else:
                    inv[at : at + 8, :] = val
    cur[:, 200:208, :] = jnp.zeros((3, 8, 128), F32)
    pre[:, 200:208, :] = jnp.zeros((3, 8, 128), F32)
    inv[200:208, :] = jnp.ones((8, 128), F32)
    for c in range(3):
        halo_out[c] = jnp.where(
            low25, cur[c, face0, :], pltpu.roll(pre[c, face0, :], 64, 1)
        )
    halo_out[3] = inv[face0, :]
    def far_copy(s, part, k):
        buf = fbnd.at[s] if part == 2 else fint.at[s, part]
        return pltpu.make_async_remote_copy(
            src_ref=buf, dst_ref=buf,
            send_sem=far_send.at[s, part, k - 1], recv_sem=far_recv.at[s, part],
            device_id=(k, cuts, sub), device_id_type=MESH,
        )

    def direct(s, parts):
        return [
            (part, k)
            for part in parts
            for k in (1, 2)
            if part == 2 or s == STEPS - 1 or k == part + 1
        ]

    def relay(s):
        for mine in (1, 2):
            @pl.when(group == mine)
            def _():
                far_copy(s, mine - 1, mine).wait_recv()
                far_copy(s, mine - 1, 3 - mine).start()

    def pack_far(s, part):
        @pl.when(group == 0)
        def _():
            for c in range(3):
                for d in range(4):
                    for b in range(4):
                        to = (d * 4 + b) * 8
                        xs[c, to : to + 8, :] = cur[c, (d * 5 + b) * 8 : (d * 5 + b) * 8 + 8, :]
                ends = cur[c, 192:200, :]
                for b in range(4):
                    moved = pltpu.roll(cur[c, 160 + b * 8 : 168 + b * 8, :], 121 + b, 1)
                    ends = jnp.where(ez == b, moved, ends) if b else jnp.where(
                        ez == b, moved, pltpu.roll(ends, 125, 1)
                    )
                xs[c, 128:136, :] = ends
                ends = pltpu.roll(cur[c, 32:40, :], 72, 1)
                for d in range(1, 4):
                    moved = pltpu.roll(cur[c, d * 40 + 32 : d * 40 + 40, :], 72 + 8 * d, 1)
                    ends = jnp.where(ey == d, moved, ends)
                xs[c, 136:144, :] = ends
                if part == 0:
                    for a in range(1, 5):
                        yi[pl.ds(72 * c + a - 1, NBR, stride=4), :] = xs[
                            c, pl.ds(a, NBR, stride=8), :
                        ]
                else:
                    yb[pl.ds(c, NBR, stride=3), :] = jnp.where(
                        low18, xs[c, pl.ds(0, NBR, stride=8), :], xs[c, pl.ds(4, NBR, stride=8), :]
                    )
            if part == 0:
                for i in range(2):
                    fint[s, i] = yi[i * 112 : i * 112 + 112, :].astype(BF16)
            else:
                fbnd[s] = yb[0:64, :].astype(BF16)
            for piece, k in direct(s, (0, 1) if part == 0 else (2,)):
                far_copy(s, piece, k).start()

    def gradient(s):
        for i in range(UROWS // 16):
            for c in range(3):
                u1, u2, u3 = split3(cur[c, i * 16 : i * 16 + 16, :])
                for k, part in enumerate((u1, u2, u3, u1, u2, u1)):
                    at = k * UROWS + i * 16
                    urhs[at : at + 16, c * 128 : c * 128 + 128] = part
        grad[s] = jnp.dot(gm_ref[...], urhs[...], preferred_element_type=F32)

    def stress_rows(get, lam, mu, relax, r, n):
        g = [[get(c, j) for j in range(3)] for c in range(3)]
        exx, eyy, ezz = g[0][0], g[1][1], g[2][2]
        exy = 0.5 * (g[0][1] + g[1][0])
        exz = 0.5 * (g[0][2] + g[2][0])
        eyz = 0.5 * (g[1][2] + g[2][1])
        tr = exx + eyy + ezz
        third = tr * (1.0 / 3.0)
        m2 = 2.0 * mu
        sxy, sxz, syz = m2 * exy, m2 * exz, m2 * eyz
        dev = [m2 * (exx - third), m2 * (eyy - third), sxy, sxz, syz]
        total = relax(dev)
        bulk = lam * tr
        sxx = bulk + m2 * exx - total[0]
        syy = bulk + m2 * eyy - total[1]
        szz = bulk + m2 * ezz + (total[0] + total[1])
        places = (
            (sxx, ((0, 0),)), (syy, ((1, 1),)), (szz, ((2, 2),)),
            (sxy - total[2], ((0, 1), (1, 0))), (sxz - total[3], ((0, 2), (2, 0))),
            (syz - total[4], ((1, 2), (2, 1))),
        )
        for val, where in places:
            p1 = val.astype(BF16)
            p2 = (val - p1.astype(F32)).astype(BF16)
            for k, part in enumerate((p1, p2, p1)):
                for c, j in where:
                    to = k * 384 + j * 128 + r
                    srhs[to : to + n, c * 128 : c * 128 + 128] = part

    chunks = [(i * 16, 16) for i in range(7)] + [(112, 13)]

    def stress(s, keep):
        gains = [(1.0 - dec_ref[l : l + 1, :]) * RELAX[l] for l in range(3)]
        for r, n in chunks:
            at = slice(r, r + n)

            def relax(dev):
                total = [None] * 5
                for k in range(5):
                    for l in range(3):
                        new = dec_ref[l : l + 1, :] * mem[l, k, at, :] + gains[l] * dev[k]
                        if keep:
                            mem[l, k, at, :] = new
                        total[k] = new if total[k] is None else total[k] + new
                return total

            stress_rows(
                lambda c, j: grad[s, j * 128 + r : j * 128 + r + n, c * 128 : c * 128 + 128],
                lam_ref[at, :], mu_ref[at, :], relax, r, n,
            )
        out = jnp.dot(fm_ref[...], srhs[...], preferred_element_type=F32)
        for c in range(3):
            force[c, 0:UROWS, :] = out[:, c * 128 : c * 128 + 128]

    def ends_force():
        for c in range(3):
            u1, u2, u3 = split3(jnp.where(low25, cur[c, face0, :], cur[c, face4, :]))
            for k, part in enumerate((u1, u2, u3, u1, u2, u1)):
                urhs[k * 32 : k * 32 + 25, c * 128 : c * 128 + 128] = part
                urhs[k * 32 + 25 : k * 32 + 32, c * 128 : c * 128 + 128] = jnp.zeros(
                    (7, 128), BF16
                )
        fgrad[...] = jnp.dot(gmg_ref[...], urhs[0:192, :], preferred_element_type=F32)
        row_low = low[0:1]
        high = jnp.where(row_low, 0.0, 1.0)
        gains = [high * (1.0 - dec_ref[l : l + 1, :]) * RELAX[l] for l in range(3)]
        gain = jnp.where(row_low, ghost_in[125:126, :], gains[0] + gains[1] + gains[2])
        for r, n in chunks:
            at = slice(r, r + n)
            both = ghost_in[at, :]
            is_low = lax.broadcasted_iota(jnp.int32, (n, 128), 1) < 64

            def relax(dev):
                for k in range(5):
                    for l in range(3):
                        mem[l, k, at, :] = mem[l, k, at, :] + gains[l] * dev[k]
                return [gain * x for x in dev]

            def get(c, j):
                rows = slice(j * 128 + r, j * 128 + r + n)
                cols = slice(c * 128, c * 128 + 128)
                val = fgrad[rows, cols]
                grad[0, rows, cols] = grad[0, rows, cols] + high * val
                return val

            stress_rows(
                get, jnp.where(is_low, both, lam_ref[at, :]),
                jnp.where(is_low, pltpu.roll(both, 64, 1), mu_ref[at, :]), relax, r, n,
            )
        out = jnp.dot(fm_ref[...], srhs[...], preferred_element_type=F32)
        for c in range(3):
            added[c, 0:UROWS, :] = out[:, c * 128 : c * 128 + 128]
        assemble(added)
        for c in range(3):
            force[c, 0:UROWS, :] = force[c, 0:UROWS, :] + high * added[c, 0:UROWS, :]
            own_face[c] = jnp.where(low25, own_face[c], force[c, face4, :])

    def assemble(force):
        for c in range(3):
            for b in range(5):
                f0 = force[c, b * 8 : b * 8 + 8, :]
                f4 = force[c, 160 + b * 8 : 168 + b * 8, :]
                n0 = f0 + jnp.where(ez > 0, pltpu.roll(f4, 1, 1), 0.0)
                n4 = f4 + jnp.where(ez < 7, pltpu.roll(f0, 127, 1), 0.0)
                force[c, b * 8 : b * 8 + 8, :] = n0
                force[c, 160 + b * 8 : 168 + b * 8, :] = n4
            for d in range(5):
                f0 = force[c, d * 40 : d * 40 + 8, :]
                f4 = force[c, d * 40 + 32 : d * 40 + 40, :]
                n0 = f0 + jnp.where(ey > 0, pltpu.roll(f4, 8, 1), 0.0)
                n4 = f4 + jnp.where(ey < 7, pltpu.roll(f0, 120, 1), 0.0)
                force[c, d * 40 : d * 40 + 8, :] = n0
                force[c, d * 40 + 32 : d * 40 + 40, :] = n4

    def pack_faces(s):
        for c in range(3):
            own_face[c] = jnp.where(low25, force[c, face0, :], force[c, face4, :])
        f = [own_face[c] for c in range(3)]
        face_out[s, 0, 0] = jnp.where(low25, f[0], pltpu.roll(f[1], 64, 1))
        face_out[s, 0, 1] = f[2]
        face_out[s, 1, 0] = jnp.where(low25, pltpu.roll(f[0], 64, 1), f[1])
        face_out[s, 1, 1] = pltpu.roll(f[2], 64, 1)

    def face_copies(s):
        to_right = pltpu.make_async_remote_copy(
            src_ref=face_out.at[s, 1], dst_ref=face_left.at[s],
            send_sem=face_send.at[s, 0], recv_sem=face_recv.at[s, 0],
            device_id=right, device_id_type=MESH,
        )
        if s == STEPS - 1:
            return [to_right]
        to_left = pltpu.make_async_remote_copy(
            src_ref=face_out.at[s, 0], dst_ref=face_right.at[s],
            send_sem=face_send.at[s, 1], recv_sem=face_recv.at[s, 1],
            device_id=left, device_id_type=MESH,
        )
        return [to_right, to_left]

    def update_inside():
        for c in range(3):
            f0, f4 = force[c, face0, :], force[c, face4, :]
            force[c, face0, :] = f0 + jnp.where(low25, 0.0, pltpu.roll(f4, 64, 1))
            force[c, face4, :] = f4 + jnp.where(low25, pltpu.roll(f0, 64, 1), 0.0)
            base[c] = jnp.where(
                low25,
                2.0 * cur[c, face0, :] - pre[c, face0, :],
                2.0 * cur[c, face4, :] - pre[c, face4, :],
            )
        for i in range(UROWS // 16):
            at = slice(i * 16, i * 16 + 16)
            scale = inv[at, :]
            for c in range(3):
                u = cur[c, at, :]
                cur[c, at, :] = 2.0 * u - pre[c, at, :] + force[c, at, :] * scale
                pre[c, at, :] = u

    def update_ends(s):
        fl = [face_left[s, 0], pltpu.roll(face_left[s, 0], 64, 1), face_left[s, 1]]
        if s == 0:
            fl = [fl[c] + added[c, face4, :] for c in range(3)]
        if s < STEPS - 1:
            fr = [
                pltpu.roll(face_right[s, 0], 64, 1), face_right[s, 0],
                pltpu.roll(face_right[s, 1], 64, 1),
            ]
        for c in range(3):
            got = jnp.where(low25, fl[c], fr[c]) if s < STEPS - 1 else fl[c]
            new = base[c] + (own_face[c] + got) * finv[...]
            cur[c, face0, :] = jnp.where(low25, new, cur[c, face0, :])
            if s < STEPS - 1:
                cur[c, face4, :] = jnp.where(low25, cur[c, face4, :], new)

    part_copies = []
    for s in range(STEPS):
        line = []
        for k in range(1, 8):
            to = lax.rem(sub + k, 8)
            line.append(
                pltpu.make_async_remote_copy(
                    src_ref=parts_out.at[s, to], dst_ref=parts_in.at[s, sub],
                    send_sem=part_send.at[s, k - 1], recv_sem=part_recv.at[s, k - 1],
                    device_id=(group, cuts, to), device_id_type=MESH,
                )
            )
        part_copies.append(line)

    def kernel_part(s):
        for mine in (1, 2):
            @pl.when(group == mine)
            def _():
                for part in range(3):
                    if s == STEPS - 1 or part != mine - 1:
                        far_copy(s, part, mine).wait_recv()

        for i in range(2):
            yi[i * 112 : i * 112 + 112, :] = fint[s, i].astype(F32)
        yb[0:64, :] = fbnd[s].astype(F32)
        for c in range(3):
            for a in range(1, 4):
                xs[c, pl.ds(a, NBR, stride=8), :] = yi[pl.ds(72 * c + a - 1, NBR, stride=4), :]
            mid = yi[pl.ds(72 * c + 3, NBR, stride=4), :]
            ends = yb[pl.ds(c, NBR, stride=3), :]
            xs[c, pl.ds(0, NBR, stride=8), :] = jnp.where(low18, ends, pltpu.roll(mid, 64, 1))
            xs[c, pl.ds(4, NBR, stride=8), :] = jnp.where(low18, mid, ends)
        for c in range(3):
            block = {}
            for d in range(4):
                for b in range(4):
                    at = (d * 4 + b) * 8
                    block[b, d] = xs[c, at : at + 8, :]
            zend, yend = xs[c, 128:136, :], xs[c, 136:144, :]
            for d in range(4):
                block[4, d] = jnp.where(
                    ey < 7, pltpu.roll(block[0, d], 120, 1), pltpu.roll(yend, 8 * (7 - d), 1)
                )
            for b in range(5):
                block[b, 4] = jnp.where(
                    ez < 7, pltpu.roll(block[b, 0], 127, 1), pltpu.roll(zend, 7 - b, 1)
                )
            line = [block[bd] for bd in BLOCKS] + [jnp.zeros((8, 128), F32)]
            for i in range(0, 26, 2):
                tile = jnp.concatenate(line[i : i + 2], axis=0).astype(BF16)
                for k in range(3):
                    at = k * UROWS + i * 8
                    frhs[at : at + 16, c * 128 : c * 128 + 128] = tile
        fgrad[...] = jnp.dot(gf_ref[...], frhs[...], preferred_element_type=F32)

        def rows(r, n):
            at = slice(r, r + n)

            def strain(get):
                g = [[get(c, j) for j in range(3)] for c in range(3)]
                diag = [g[0][0], g[1][1], g[2][2]]
                tr = diag[0] + diag[1] + diag[2]
                third = tr * (1.0 / 3.0)
                dev = [x - third for x in diag]
                shear = [g[0][1] + g[1][0], g[0][2] + g[2][0], g[1][2] + g[2][1]]
                return tr, dev, shear

            tr, dev, off = strain(
                lambda c, j: grad[s, j * 128 + r : j * 128 + r + n, c * 128 : c * 128 + 128]
            )
            trf, devf, offf = strain(
                lambda c, j: fgrad[j * 128 + r : j * 128 + r + n, c * 128 : c * 128 + 128]
            )
            m2 = 2.0 * mu_ref[at, :]
            kappa = lam_ref[at, :] + m2 * (1.0 / 3.0)
            kb[at, :] = (TIME_STEP * kappa * trf * tr).astype(BF16)
            prod = dev[0] * devf[0] + dev[1] * devf[1] + dev[2] * devf[2]
            cross = off[0] * offf[0] + off[1] * offf[1] + off[2] * offf[2]
            ks[at, :] = (TIME_STEP * m2 * (prod + 0.5 * cross)).astype(BF16)

        for i in range(7):
            rows(i * 16, 16)
        rows(112, 13)
        for i, ref in enumerate((kb, ks)):
            placed = lax.dot_general(
                sel[...], ref[...], (((1,), (1,)), ((), ())), preferred_element_type=F32
            ).astype(BF16)
            for t in range(8):
                parts_out[s, t, :, i * 128 : i * 128 + 128] = placed[t * 32 : t * 32 + 32, :]
        parts_in[s, sub] = parts_out[s, sub]
        for copy in part_copies[s]:
            copy.start()

    urhs[1248:1280, :] = jnp.zeros((32, 384), BF16)
    zeros16 = jnp.zeros((16, 384), BF16)
    for i in range(9):
        srhs[i * 128 + 112 : i * 128 + 128, :] = zeros16
    kb[112:128, :] = jnp.zeros((16, 128), BF16)
    ks[112:128, :] = jnp.zeros((16, 128), BF16)

    yi[216:224, :] = jnp.zeros((8, 128), F32)
    yb[48:64, :] = jnp.zeros((16, 128), F32)
    xs[...] = jnp.zeros((3, 200, 128), F32)
    for c in range(3):
        cur[c, face4, :] = jnp.where(low25, cur[c, face4, :], 0.0)
    loads[5].wait()
    gradient(0)
    for load in loads[6:]:
        load.wait()
    gain = (1.0 - dec_ref[0:1, :]) * RELAX[0]
    for l in (1, 2):
        gain = gain + (1.0 - dec_ref[l : l + 1, :]) * RELAX[l]
    low_row = lax.broadcasted_iota(jnp.int32, (125, 128), 1) < 64
    ghost_out[0:125, :] = jnp.where(low_row, pltpu.roll(lam_ref[...], 64, 1), mu_ref[...])
    ghost_out[125:126, :] = pltpu.roll(jnp.broadcast_to(gain, (8, 128)), 64, 1)[0:1]
    stress(0, True)
    assemble(force)
    pack_faces(0)
    pl.semaphore_wait(barrier, 11)
    halo = pltpu.make_async_remote_copy(
        src_ref=halo_out, dst_ref=halo_in, send_sem=halo_sem.at[0], recv_sem=halo_sem.at[1],
        device_id=left, device_id_type=MESH,
    )
    halo.start()
    first_faces = face_copies(0)
    for copy in first_faces:
        copy.start()
    ghost = pltpu.make_async_remote_copy(
        src_ref=ghost_out, dst_ref=ghost_in, send_sem=ghost_sem.at[0], recv_sem=ghost_sem.at[1],
        device_id=right, device_id_type=MESH,
    )
    ghost.start()
    pack_far(0, 0)

    for i in range(3, 5):
        loads[i].wait()
    own_row[0:1, 0:64] = own_ref[0]
    own_row[0:1, 64:128] = own_ref[1]
    slot = lax.broadcasted_iota(jnp.int32, (256, 128), 0)
    elem = lax.broadcasted_iota(jnp.int32, (256, 128), 1)
    onehot = jnp.where(own_row[0:1, :] == lax.div(slot, 32), 1.0, 0.0)
    one = lax.broadcasted_iota(jnp.int32, (128, 128), 0)
    two = lax.broadcasted_iota(jnp.int32, (128, 128), 1)
    one_low, two_low = one < 64, two < 64
    earlier = jnp.where(one < two, jnp.where(two_low, 1.0, jnp.where(one_low, 0.0, 1.0)), 0.0)
    count = jnp.dot(onehot.astype(BF16), earlier.astype(BF16), preferred_element_type=F32)
    rank_hit = jnp.where(count == lax.rem(slot, 16).astype(F32), onehot, 0.0)
    mine = lax.rem(lax.div(slot, 16), 2) == lax.div(elem, 64)
    sel[...] = jnp.where(mine, rank_hit, 0.0).astype(BF16)
    halo.wait()
    for c in range(3):
        got = halo_in[c]
        cur[c, face4, :] = jnp.where(low25, cur[c, face4, :], pltpu.roll(got, 64, 1))
        pre[c, face4, :] = jnp.where(low25, pre[c, face4, :], got)
    inv[face4, :] = jnp.where(low25, inv[face4, :], pltpu.roll(halo_in[3], 64, 1))
    pack_far(0, 1)
    inv[0:UROWS, :] = 1.0 / (inv[0:UROWS, :] * wt_ref[...])
    finv[...] = jnp.where(low25, inv[face0, :], inv[face4, :])

    for s in range(STEPS):
        if s == 0:
            copies = first_faces
            ghost.wait()
            ends_force()
        else:
            gradient(s)
            stress(s, s < STEPS - 1)
            assemble(force)
            pack_faces(s)
            copies = face_copies(s)
            for copy in copies:
                copy.start()
        update_inside()
        if s < STEPS - 1:
            pack_far(s + 1, 0)
            relay(s)
            if s == 1:
                kernel_part(0)
        else:
            kernel_part(1)
            kernel_part(2)
        for copy in copies:
            copy.wait()
        update_ends(s)
        if s < STEPS - 1:
            pack_far(s + 1, 1)

    rest = jnp.zeros((104, 128), F32)
    for i in range(0, 25, 2):
        pair = BLOCKS[i : i + 2]
        blocks = []
        for c in range(3):
            both = []
            for b, d in pair:
                at = (d * 5 + b) * 8
                v = cur[c, at : at + 8, :]
                both.append(jnp.where(subl < 4, v, pltpu.roll(pltpu.roll(v, 64, 1), 4, 0)))
            second = both[-1]
            blocks.append(jnp.where(low, both[0], pltpu.roll(second, 64, 1)))
        turned = jnp.concatenate(blocks + [rest], axis=0).T
        for h, (b, d) in enumerate(pair):
            for y in range(8):
                tee[pl.ds(132 * y + 33 * b + d, 8, stride=4), :] = turned[
                    h * 64 + y * 8 : h * 64 + y * 8 + 8, :
                ]
    for i in range(9):
        block = tee[i * 128 : i * 128 + 128, :].T
        width = min(128, 1089 - i * 128)
        for c in range(3):
            disp_ref[0, c, :, i * 128 : i * 128 + width] = block[c * 8 : c * 8 + 8, 0:width]

    @pl.when(group == 0)
    def _():
        for s in range(STEPS):
            for part, k in direct(s, (0, 1, 2)):
                far_copy(s, part, k).wait_send()

    for mine in (1, 2):
        @pl.when(group == mine)
        def _():
            for s in range(STEPS - 1):
                far_copy(s, mine - 1, 3 - mine).wait_send()

    for s in range(STEPS - 1):
        for copy in part_copies[s]:
            copy.wait()
    for t in range(8):
        early[t] = parts_in[0, t].astype(F32) + parts_in[1, t].astype(F32)
    for copy in part_copies[STEPS - 1]:
        copy.wait()
    for i in range(2):
        cols = slice(i * 128, i * 128 + 128)
        for h in range(2):
            quarter = [
                early[t, :, cols] + parts_in[STEPS - 1, t, :, cols].astype(F32)
                for t in range(h * 4, h * 4 + 4)
            ]
            turned = jnp.concatenate(quarter, axis=0).T
            ker_ref[h, i * 125 : i * 125 + 125, :] = turned[0:125, :]


def finish(disp_ref, ker_ref, disp_hbm, ker_hbm, sem):
    copies = [pltpu.make_async_copy(disp_ref, disp_hbm, sem.at[0])]
    for h in range(2):
        copies.append(
            pltpu.make_async_copy(
                ker_ref.at[h], ker_hbm.at[:, 0, pl.ds(h * 128, 128)], sem.at[1 + h]
            )
        )
    for copy in copies:
        copy.start()
    for copy in copies:
        copy.wait()


def per_device(consts, now, prev, mem, dens, lam, mu, dec, own):
    hbm = pl.BlockSpec(memory_space=pl.ANY)
    dma = pltpu.SemaphoreType.DMA
    mem = jnp.transpose(mem, (1, 2, 3, 0, 4))
    own = jnp.transpose(own, (0, 2, 1))
    disp, kers = pl.pallas_call(
        kernel,
        out_shape=(
            pltpu.VMEM((1, 3, 8, 1089), F32),
            pltpu.VMEM((2, 250, 128), F32),
        ),
        in_specs=[hbm] * 13,
        out_specs=(pl.BlockSpec(memory_space=pltpu.VMEM),) * 2,
        scratch_shapes=[
            pltpu.VMEM((384, 192), BF16),
            dma((2,)),
            pltpu.VMEM((126, 128), F32),
            pltpu.VMEM((126, 128), F32),
            pltpu.VMEM((8, 32, 256), F32),
            pltpu.VMEM((3, 256, 128), F32),
            pltpu.VMEM((384, GK), BF16),
            pltpu.VMEM((384, 3 * UROWS), BF16),
            pltpu.VMEM((UROWS, 1152), BF16),
            pltpu.VMEM((UROWS, 128), F32),
            pltpu.VMEM((1, 3, 8, 1089), F32),
            pltpu.VMEM((1, 3, 8, 1089), F32),
            pltpu.VMEM((3, 5, 125, 128), F32),
            pltpu.VMEM((8, 1089), F32),
            pltpu.VMEM((125, 128), F32),
            pltpu.VMEM((125, 128), F32),
            pltpu.VMEM((3, 128), F32),
            pltpu.VMEM((2, 1, 64), jnp.int32),
            pltpu.VMEM((8, 128), jnp.int32),
            dma((27,)),
            pltpu.VMEM((56, 128), F32),
            pltpu.VMEM((1152, 128), F32),
            pltpu.VMEM((3, 256, 128), F32),
            pltpu.VMEM((3, 256, 128), F32),
            pltpu.VMEM((256, 128), F32),
            pltpu.VMEM((GK, 384), BF16),
            pltpu.VMEM((STEPS, 384, 384), F32),
            pltpu.VMEM((1152, 384), BF16),
            pltpu.VMEM((3, 256, 128), F32),
            pltpu.VMEM((3, 25, 128), F32),
            pltpu.VMEM((25, 128), F32),
            pltpu.VMEM((3, 200, 128), F32),
            pltpu.VMEM((248, 128), F32),
            pltpu.VMEM((80, 128), F32),
            pltpu.VMEM((STEPS, 2, 112, 128), BF16),
            pltpu.VMEM((STEPS, 64, 128), BF16),
            pltpu.VMEM((3 * UROWS, 384), BF16),
            pltpu.VMEM((384, 384), F32),
            pltpu.VMEM((128, 128), BF16),
            pltpu.VMEM((128, 128), BF16),
            pltpu.VMEM((256, 128), BF16),
            pltpu.VMEM((4, 25, 128), F32),
            pltpu.VMEM((4, 25, 128), F32),
            pltpu.VMEM((3, 25, 128), F32),
            pltpu.VMEM((STEPS, 2, 2, 25, 128), F32),
            pltpu.VMEM((STEPS, 2, 25, 128), F32),
            pltpu.VMEM((STEPS, 2, 25, 128), F32),
            pltpu.VMEM((STEPS, 8, 32, 256), BF16),
            pltpu.VMEM((STEPS, 8, 32, 256), BF16),
            dma((2,)),
            dma((STEPS, 2)),
            dma((STEPS, 2)),
            dma((STEPS, 3, 2)),
            dma((STEPS, 3)),
            dma((STEPS, 7)),
            dma((STEPS, 7)),
        ],
        compiler_params=pltpu.CompilerParams(
            collective_id=0, has_side_effects=True
        ),
        name="wavefields",
    )(*consts, now, prev, mem, dens, lam, mu, dec, own)
    disp, kers = pl.pallas_call(
        finish,
        out_shape=(
            jax.ShapeDtypeStruct((1, 3, 8, 1089), F32),
            jax.ShapeDtypeStruct((250, 1, 256), F32),
        ),
        in_specs=[pl.BlockSpec(memory_space=pltpu.VMEM)] * 2,
        out_specs=(hbm, hbm),
        scratch_shapes=[dma((3,))],
        compiler_params=pltpu.CompilerParams(vmem_limit_bytes=8 * 1024 * 1024),
        name="results",
    )(disp, kers)
    return disp, jnp.transpose(kers, (1, 2, 0))


def solution(mesh):
    consts = tuple(jnp.asarray(t) for t in tables())
    in_specs = (
        P("group", None, ("cuts", "sub"), None),
        P("group", None, ("cuts", "sub"), None),
        P("group", None, None, None, ("cuts", "sub")),
        P(("cuts", "sub"), None),
        P(None, ("cuts", "sub")),
        P(None, ("cuts", "sub")),
        P(None, ("cuts", "sub")),
        P(("cuts", "sub"), None, None),
    )
    out_specs = (P("group", None, ("cuts", "sub"), None), P("group", ("cuts", "sub"), None))
    return jax.shard_map(
        functools.partial(per_device, consts),
        mesh=mesh, in_specs=in_specs, out_specs=out_specs, check_vma=False,
    )
```
